32 devices in a mesh: groups: 2 (over y), seq: 4 (over z), fsdp: 2 (over x), head: 2 (over core).
Axes of the slice: x: 2, y: 2, z: 4, core: 2. Of those that a mesh axis runs over, the one named last changes fastest.
Arguments:
- frames: bfloat16 [6144, 3072], P(('groups', 'seq')), parts along dimension 0, may hold values from -330 to 330
- modulation: float32 [4, 3072], P('groups'), parts along dimension 0, may hold values from -2.5 to 2.5
- w_qkv: bfloat16 [3072, 3, 2048], P('seq', None, ('fsdp', 'head')), may hold values from -0.109375 to 0.109375
- b_qkv: float32 [3, 2048], P(None, ('fsdp', 'head')), may hold values from -2.5 to 2.5
- qk_gain: float32 [2, 128], replicated, may hold values from 0.7 to 2.4
- block_lists: int32 [16, 27], P(('groups', 'seq')), parts along dimension 0, may hold values from -1 to 7, as said below
Outputs:
- attention: bfloat16 [6144, 2048], P(('groups', 'seq'), ('fsdp', 'head')), parts along dimension 0
The draws below stay inside these ranges and needn't reach their ends.
There are 2 independent parts, one for each index of `groups`. The reference program is written for one: setup_inputs(seed, part) draws one part's arguments, and reference() takes and returns one part's arrays. A program takes and returns all parts, laid end to end along the dimension named above; an argument that names none is the same for every part. Nothing has to cross between parts.
Inputs may be any that keep to these rules, and one draw needn't show every extreme that they name: `block_lists`: tile g lies at width g // 2, time (g % 2) // 1 and height g % 1 of a 2 x 1 x 4 grid of tiles. Entry (a + 1) * 9 + (b + 1) * 3 + (c + 1) of row g, for a, b, c in -1, 0, 1, is the tile at time + a, height + b and width + c of tile g, or -1 where that tile is outside the grid or left out of the list. Entry 13 is always g.
All inputs are finite; a program needn't handle non-finite values.
Results may differ from the reference program's by a relative error of at most 0.0058.
Values may be sent and summed in bfloat16 or wider, within the bound.
No kernel may reach another device: no remote copies, remote signals or barrier semaphores. Data moves between devices by JAX's collectives and lax.ppermute only.
A program may use at most 128 MiB of HBM per device.

```python
import math
import jax
import jax.numpy as jnp
from jax import lax

D = 3072
HEADS = 16
HD = 128
TILE = 384
TIME_TILES = 2
WIN = 27
BH = 1
TILE_DEV = 2
WIDTH_TILES = 4
TILES = 8
TOKENS = 3072


def draw_frames(key, part):
    first, second, third = jax.random.split(key, 3)
    column_scale = jnp.exp(jax.random.uniform(second, (D,), jnp.float32, 0.0, math.log(10.0)))
    base = jax.random.truncated_normal(first, -6.0, 6.0, (TOKENS, D), jnp.float32)
    row_scale = jnp.exp(jax.random.uniform(third, (TOKENS, 1), jnp.float32, 0.0, math.log(4.0)))
    return (base * column_scale * row_scale).astype(jnp.bfloat16)


def draw_block_lists(key, part):
    tile_ids = jnp.arange(TILES, dtype=jnp.int32)[:, None]
    entry = jnp.arange(WIN, dtype=jnp.int32)[None, :]
    step_time = entry // 9 - 1
    step_height = entry // 3 % 3 - 1
    step_width = entry % 3 - 1
    column = tile_ids // TILE_DEV
    moment = tile_ids % TILE_DEV // BH
    height = tile_ids % BH
    new_time = moment + step_time
    new_height = height + step_height
    new_column = column + step_width
    inside = (new_time >= 0) & (new_time < TIME_TILES) & (new_height >= 0) & (new_height < BH)
    inside = inside & (new_column >= 0) & (new_column < WIDTH_TILES)
    keep = (jax.random.randint(key, (TILES, WIN), 0, 4) > 0) | (entry == 13)
    target = new_column * TILE_DEV + new_time * BH + new_height
    return jnp.where(inside & keep, target, -1).astype(jnp.int32)


def shard_levels(own_key, dims, cuts, smallest, high):
    level, own = 1.0, jax.random.fold_in(own_key, 6)
    for axis_at, parts in cuts:
        draws = jnp.exp(jax.random.uniform(jax.random.fold_in(own, axis_at), (parts,), jnp.float32, smallest / len(cuts), high / len(cuts)))
        level = level * jnp.repeat(draws, dims[axis_at] // parts).reshape([-1 if axis == axis_at else 1 for axis in range(len(dims))])
    return level


def gaussian(stream_key, extent, deviation, reach, cuts=(), kind=jnp.bfloat16):
    gain = shard_levels(stream_key, extent, cuts, -0.22, 0.18) if cuts else 1.0
    values = jax.random.normal(stream_key, extent, jnp.float32) * deviation * gain
    return jnp.minimum(jnp.maximum(values, -reach), reach).astype(kind)


def setup_inputs(seed: int = 0, part: int = 0) -> dict:
    arg_keys = jax.random.split(jax.random.key(seed), 7)
    part_splits = jax.random.split(jax.random.fold_in(arg_keys[6], part), 7)
    frames = draw_frames(jax.random.fold_in(jax.random.fold_in(arg_keys[6], part), 71), part)
    modulation = gaussian(part_splits[1], (2, D), 0.5, 2.5, (), jnp.float32)
    w_qkv = gaussian(arg_keys[2], (D, 3, HEADS * HD), D ** -0.5, 0.109375, ((0, 4), (2, 4)))
    b_qkv = gaussian(arg_keys[3], (3, HEADS * HD), 0.5, 2.5, ((1, 4),), jnp.float32)
    qk_gain = jnp.clip(jax.random.uniform(arg_keys[4], (2, HD), jnp.float32, 0.7, 2.4), 0.7, 2.4)
    block_lists = draw_block_lists(jax.random.fold_in(jax.random.fold_in(arg_keys[6], part), 71), part)
    return dict(frames=frames, modulation=modulation, w_qkv=w_qkv, b_qkv=b_qkv, qk_gain=qk_gain, block_lists=block_lists)


def rms_scale(tensor, gain_row):
    return tensor * lax.rsqrt(lax.optimization_barrier(jnp.mean(tensor * tensor, axis=-1, keepdims=True)) + 1e-06) * gain_row

def reference(frames, modulation, w_qkv, b_qkv, qk_gain, block_lists):
    inputs = frames.astype(jnp.float32)
    average = lax.optimization_barrier(jnp.mean(inputs, axis=-1, keepdims=True))
    centred = inputs - average
    variance = lax.optimization_barrier(jnp.mean(centred * centred, axis=-1, keepdims=True))
    normed = centred * lax.rsqrt(variance + 1e-06) * (1.0 + modulation[0]) + modulation[1]
    normed = normed.astype(jnp.bfloat16)
    width_cols = HEADS * HD
    projected = jnp.dot(normed, w_qkv.reshape(D, 3 * width_cols), preferred_element_type=jnp.float32)
    projected = projected.reshape(TOKENS, 3, width_cols) + b_qkv
    projected = projected.reshape(TOKENS, 3, HEADS, HD)
    queries = rms_scale(projected[:, 0], qk_gain[0]).astype(jnp.bfloat16)
    key_rows = rms_scale(projected[:, 1], qk_gain[1]).astype(jnp.bfloat16)
    values = projected[:, 2].astype(jnp.bfloat16)
    factor = 1.0 / HD ** 0.5
    query_tiles = queries.reshape(TILES, TILE, HEADS, HD)
    key_tiles = key_rows.reshape(TILES, TILE, HEADS, HD)
    value_tiles = values.reshape(TILES, TILE, HEADS, HD)
    tile_numbers = jnp.arange(TILES, dtype=jnp.int32)

    def one_tile(tile_parts):
        query_block, tile_number, tile_list = tile_parts
        column = tile_number // TILE_DEV
        raw = ((column - 1) * TILE_DEV + jnp.arange(3 * TILE_DEV, dtype=jnp.int32)).astype(jnp.int32)
        clipped = jnp.clip(raw, 0, TILES - 1).astype(jnp.int32)
        listed = jnp.any((tile_list[:, None] == raw[None, :]) & (tile_list[:, None] >= 0), axis=0)
        near_keys = key_tiles[clipped].reshape(3 * TILE_DEV * TILE, HEADS, HD).astype(jnp.float32)
        near_values = value_tiles[clipped].reshape(3 * TILE_DEV * TILE, HEADS, HD).astype(jnp.float32)
        seen = jnp.repeat(listed, TILE)
        scores = jnp.einsum('qhd,khd->hqk', query_block.astype(jnp.float32), near_keys) * factor
        weights = jnp.where(seen[None, None, :], jnp.exp(scores), 0.0)
        totals = lax.optimization_barrier(jnp.sum(weights, axis=-1))
        rounded = lax.optimization_barrier(weights.astype(jnp.bfloat16)).astype(jnp.float32)
        mixture = jnp.einsum('hqk,khd->qhd', rounded, near_values)
        return (mixture / jnp.transpose(totals)[:, :, None]).astype(jnp.bfloat16)
    result = lax.map(one_tile, (query_tiles, tile_numbers, block_lists))
    return result.reshape(TOKENS, HEADS * HD)
```

```python
import math

import jax
import jax.numpy as jnp
from jax import lax
from jax.experimental import pallas as pl
from jax.experimental.pallas import tpu as pltpu
from jax.sharding import PartitionSpec as P

EPS = 1e-06
HIDDEN = -1e30


def with_halo(shard, sides, width):
    for axis, dim in sides:
        devices, length = (lax.axis_size(axis), shard.shape[dim])
        up = [(i, (i + 1) % devices) for i in range(devices - 1)]
        down = [(j, i) for i, j in up]
        last = lax.slice_in_dim(shard, length - width, length, axis=dim)
        first = lax.slice_in_dim(shard, 0, width, axis=dim)
        before = lax.ppermute(last, axis, up)
        after = lax.ppermute(first, axis, down)
        shard = jnp.concatenate([before, shard, after], axis=dim)
    return shard


def normed_heads(tensor, gain_row, head_dim):
    shaped = tensor.reshape(tensor.shape[0], tensor.shape[1] // head_dim, head_dim)
    scaled = (
        shaped * lax.rsqrt(jnp.mean(shaped * shaped, axis=-1, keepdims=True) + EPS) * gain_row
    )
    return scaled.astype(jnp.bfloat16)


def visible_tiles(block_lists):
    position = lax.axis_index("seq")
    tile_dev = block_lists.shape[0]
    candidates = (position - 1) * tile_dev + jnp.arange(3 * tile_dev, dtype=jnp.int32)
    matches = (block_lists[:, :, None] == candidates[None, None, :]) & (
        block_lists[:, :, None] >= 0
    )
    return jnp.any(matches, axis=1)


def general(frames, modulation, w_qkv, b_qkv, qk_gain, block_lists):
    inputs = frames.astype(jnp.float32)
    average = jnp.mean(inputs, axis=-1, keepdims=True)
    centred = inputs - average
    variance = jnp.mean(centred * centred, axis=-1, keepdims=True)
    normed = centred * lax.rsqrt(variance + EPS) * (1.0 + modulation[0]) + modulation[1]
    normed = normed.astype(jnp.bfloat16)
    tokens = normed.shape[0]
    width_cols = w_qkv.shape[2]
    head_dim = qk_gain.shape[1]
    heads = width_cols // head_dim
    projected = jnp.einsum(
        "td,djc->tjc",
        normed,
        lax.all_gather(w_qkv, "seq", axis=0, tiled=True),
        preferred_element_type=jnp.float32,
    )
    projected = projected + b_qkv
    queries = normed_heads(projected[:, 0], qk_gain[0], head_dim)
    key_rows = normed_heads(projected[:, 1], qk_gain[1], head_dim)
    values = projected[:, 2].astype(jnp.bfloat16).reshape(tokens, heads, head_dim)
    stacked = jnp.stack([key_rows, values], axis=0)
    neighbourhood = with_halo(stacked, (("seq", 1),), tokens)
    tile_len = tokens // block_lists.shape[0]
    allowed_keys = jnp.repeat(
        jnp.repeat(visible_tiles(block_lists), tile_len, axis=0), tile_len, axis=1
    )
    factor = 1.0 / math.sqrt(head_dim)
    scores = (
        jnp.einsum("qhd,khd->hqk", queries, neighbourhood[0], preferred_element_type=jnp.float32)
        * factor
    )
    weights = jnp.where(allowed_keys[None, :, :], jnp.exp(scores), 0.0)
    totals = jnp.sum(weights, axis=-1)
    mixture = jnp.einsum(
        "hqk,khd->qhd",
        weights.astype(jnp.bfloat16),
        neighbourhood[1],
        preferred_element_type=jnp.float32,
    )
    result = (mixture / jnp.transpose(totals)[:, :, None]).astype(jnp.bfloat16)
    return result.reshape(tokens, width_cols)


def norm_kernel(x_ref, mod_ref, o_ref):
    x = x_ref[...].astype(jnp.float32)
    centred = x - jnp.mean(x, axis=-1, keepdims=True)
    variance = jnp.mean(centred * centred, axis=-1, keepdims=True)
    scaled = centred * lax.rsqrt(variance + EPS) * (1.0 + mod_ref[0:1, :]) + mod_ref[1:2, :]
    o_ref[...] = scaled.astype(jnp.bfloat16)


def normalize(frames, modulation):
    tokens, width = frames.shape
    rows = 128
    return pl.pallas_call(
        norm_kernel,
        grid=(tokens // rows,),
        in_specs=[
            pl.BlockSpec((rows, width), lambda i: (i, 0)),
            pl.BlockSpec((2, width), lambda i: (0, 0)),
        ],
        out_specs=pl.BlockSpec((rows, width), lambda i: (i, 0)),
        out_shape=jax.ShapeDtypeStruct((tokens, width), jnp.bfloat16),
        cost_estimate=pl.CostEstimate(
            flops=10 * tokens * width, bytes_accessed=4 * tokens * width, transcendentals=0
        ),
        name="normalize",
    )(frames, modulation)


def project(place, x, w, pieces, bias, gain, first, count, last_seq):
    tokens, width = x.shape
    rows, half = w.shape[1], w.shape[2] // 2
    head_dim = gain.shape[1]
    step = 256

    def kernel(place_ref, x_ref, own_ref, down_ref, up_ref, two_ref, far_ref, b_ref, g_ref, o_ref, acc_ref):
        z = place_ref[0]
        j = pl.program_id(0) + first

        def add(ref, source, fresh):
            at = pl.multiple_of(source * rows, 128)
            for r in range(tokens // step):
                part = jnp.dot(
                    x_ref[pl.ds(r * step, step), pl.ds(at, rows)],
                    ref[0],
                    preferred_element_type=jnp.float32,
                )
                if fresh:
                    acc_ref[pl.ds(r * step, step), :] = part
                else:
                    acc_ref[pl.ds(r * step, step), :] += part

        add(own_ref, z, True)
        add(two_ref, (z + 2) % (last_seq + 1), False)
        pl.when(z < last_seq)(lambda: add(down_ref, z + 1, False))
        pl.when(z > 0)(lambda: add(up_ref, z - 1, False))
        pl.when((z == 0) | (z == last_seq))(lambda: add(far_ref, last_seq - z, False))

        full = acc_ref[...] + b_ref[pl.ds(j, 1), :]

        @pl.when(j == 2)
        def _():
            o_ref[0] = full.astype(jnp.bfloat16)

        @pl.when(j < 2)
        def _():
            for h in range(half // head_dim):
                part = full[:, h * head_dim : (h + 1) * head_dim]
                mean = jnp.mean(part * part, axis=-1, keepdims=True)
                scaled = part * lax.rsqrt(mean + EPS) * g_ref[pl.ds(j, 1), :]
                o_ref[0, :, h * head_dim : (h + 1) * head_dim] = scaled.astype(jnp.bfloat16)

    piece = pl.BlockSpec((1, rows, half), lambda j, s: (j, 0, 0))
    return pl.pallas_call(
        kernel,
        grid_spec=pltpu.PrefetchScalarGridSpec(
            num_scalar_prefetch=1,
            grid=(count,),
            in_specs=[
                pl.BlockSpec((tokens, width), lambda j, s: (0, 0)),
                pl.BlockSpec((1, rows, half), lambda j, s: (j + first, 0, s[1])),
                piece,
                piece,
                piece,
                piece,
                pl.BlockSpec((3, half), lambda j, s: (0, s[1])),
                pl.BlockSpec((2, head_dim), lambda j, s: (0, 0)),
            ],
            out_specs=pl.BlockSpec((1, tokens, half), lambda j, s: (j, 0, 0)),
            scratch_shapes=[pltpu.VMEM((tokens, half), jnp.float32)],
        ),
        out_shape=jax.ShapeDtypeStruct((count, tokens, half), jnp.bfloat16),
        compiler_params=pltpu.CompilerParams(vmem_limit_bytes=40 << 20),
        cost_estimate=pl.CostEstimate(
            flops=2 * tokens * width * half * count,
            bytes_accessed=2 * (tokens * width + count * half * (width + tokens)),
            transcendentals=0,
        ),
        name="project",
    )(place, x, w, *pieces, bias, gain)


def attend(place, limits, q, own, before, after, carried, width_cols, head_dim):
    tokens, half = q.shape[1], q.shape[2]
    tiles = limits.shape[0]
    tile = tokens // tiles
    heads = half // head_dim
    scale = math.log2(math.e) / math.sqrt(head_dim)

    def kernel(place_ref, limit_ref, q_ref, own_ref, before_ref, after_ref, *rest):
        o_ref = rest[-1]
        i = pl.program_id(1)
        query = q_ref[0]
        total = jnp.zeros((tile, 128), jnp.float32)
        mixed = jnp.zeros((tile, head_dim), jnp.float32)
        for side, ref in enumerate((own_ref, before_ref, after_ref)):
            column = (1, 0, 2)[side]
            for t in range(tiles):
                keys = ref[0, t * tile : (t + 1) * tile, :]
                values = ref[1, t * tile : (t + 1) * tile, :]
                scores = lax.dot_general(
                    query, keys, (((1,), (1,)), ((), ())), preferred_element_type=jnp.float32
                )
                weights = jnp.exp2(scores * scale + limit_ref[i, column * tiles + t])
                for c in range(tile // 128):
                    total = total + weights[:, c * 128 : (c + 1) * 128]
                mixed = mixed + jnp.dot(
                    weights.astype(jnp.bfloat16), values, preferred_element_type=jnp.float32
                )
        o_ref[...] = (mixed / jnp.sum(total, axis=-1, keepdims=True)).astype(jnp.bfloat16)

    rows = pl.BlockSpec((2, tokens, head_dim), lambda h, i, s: (0, 0, h))
    carried = () if carried is None else (carried,)
    return pl.pallas_call(
        kernel,
        grid_spec=pltpu.PrefetchScalarGridSpec(
            num_scalar_prefetch=1,
            grid=(heads, tiles),
            in_specs=[
                pl.BlockSpec(memory_space=pltpu.SMEM),
                pl.BlockSpec((1, tile, head_dim), lambda h, i, s: (0, i, h)),
                rows,
                rows,
                rows,
            ]
            + [pl.BlockSpec(memory_space=pl.ANY)] * len(carried),
            out_specs=pl.BlockSpec((tile, head_dim), lambda h, i, s: (i, s[1] * heads + h)),
        ),
        out_shape=jax.ShapeDtypeStruct((tokens, width_cols), jnp.bfloat16),
        input_output_aliases={6: 0} if carried else {},
        compiler_params=pltpu.CompilerParams(vmem_limit_bytes=40 << 20),
        cost_estimate=pl.CostEstimate(
            flops=4 * tokens * 3 * tokens * half,
            bytes_accessed=2 * tokens * half * 8,
            transcendentals=3 * tokens * tokens * heads,
        ),
        name="attend",
    )(place, limits, q, own, before, after, *carried)


def swap(value):
    return lax.ppermute(value, "groups", [(0, 1), (1, 0)])


def per_device(frames, modulation, w_qkv, b_qkv, qk_gain, block_lists):
    columns = lax.axis_size("seq")
    head_dim = qk_gain.shape[1]
    width_cols = w_qkv.shape[2]
    heads = width_cols // head_dim
    tokens = frames.shape[0]
    if columns != 4 or lax.axis_size("groups") != 2 or heads % 2:
        return general(frames, modulation, w_qkv, b_qkv, qk_gain, block_lists)

    seq = lax.axis_index("seq").astype(jnp.int32)
    mine = lax.axis_index("groups").astype(jnp.int32)
    last = columns - 1
    half = width_cols // 2
    rows = w_qkv.shape[0]
    down = [(i + 1, i) for i in range(last)]
    up = [(i, i + 1) for i in range(last)]
    ends = [(1, 0), (last - 1, last)]
    across = [(i, (i + 2) % columns) for i in range(columns)]

    w = jnp.transpose(w_qkv, (1, 0, 2))
    order = ((1, 2), (0, 1))
    sent = [
        lax.dynamic_slice(w, (first, 0, mine * half), (count, rows, half)) for first, count in order
    ]
    mine_pieces, twin_pieces = [], []
    for part in sent:
        two = lax.ppermute(part, "seq", across)
        below = lax.ppermute(part, "seq", down)
        above = lax.ppermute(part, "seq", up)
        far = lax.ppermute(two, "seq", ends)
        group = (below, above, two, far)
        mine_pieces.append(group)
        twin_pieces.append(tuple(swap(p) for p in group))

    x = normalize(frames, modulation)
    limits = jnp.where(visible_tiles(block_lists), 0.0, HIDDEN).astype(jnp.float32)
    out = None
    kv, q, places = [], [], []
    for which, pieces in ((mine, mine_pieces), (1 - mine, twin_pieces)):
        place = jnp.stack([seq, which])
        places.append(place)
        kv.append(project(place, x, w, pieces[0], b_qkv, qk_gain, 1, 2, last))
        q.append(project(place, x, w, pieces[1], b_qkv, qk_gain, 0, 1, last))
    halos = [(lax.ppermute(a, "seq", up), lax.ppermute(a, "seq", down)) for a in kv]
    for place, q_half, own, (before, after) in zip(places, q, kv, halos):
        out = attend(place, limits, q_half, own, before, after, out, width_cols, head_dim)
    return out


def solution(mesh):
    placed = (
        P(("groups", "seq"), None),
        P("groups", None),
        P("seq", None, ("fsdp", "head")),
        P(None, ("fsdp", "head")),
        P(),
        P(("groups", "seq"), None),
    )
    return jax.shard_map(
        per_device,
        mesh=mesh,
        in_specs=placed,
        out_specs=P(("groups", "seq"), ("fsdp", "head")),
        check_vma=False,
    )
```

```python
import math

import jax
import jax.numpy as jnp
from jax import lax
from jax.experimental import pallas as pl
from jax.experimental.pallas import tpu as pltpu
from jax.sharding import PartitionSpec as P

EPS = 1e-06
HIDDEN = -1e30
COST = pl.CostEstimate(flops=1 << 20, bytes_accessed=1 << 10, transcendentals=0)
LONG = pl.CostEstimate(flops=1 << 37, bytes_accessed=1 << 10, transcendentals=0)


def with_halo(shard, sides, width):
    for axis, dim in sides:
        devices, length = (lax.axis_size(axis), shard.shape[dim])
        up = [(i, (i + 1) % devices) for i in range(devices - 1)]
        down = [(j, i) for i, j in up]
        last = lax.slice_in_dim(shard, length - width, length, axis=dim)
        first = lax.slice_in_dim(shard, 0, width, axis=dim)
        before = lax.ppermute(last, axis, up)
        after = lax.ppermute(first, axis, down)
        shard = jnp.concatenate([before, shard, after], axis=dim)
    return shard


def normed_heads(tensor, gain_row, head_dim):
    shaped = tensor.reshape(tensor.shape[0], tensor.shape[1] // head_dim, head_dim)
    scaled = (
        shaped * lax.rsqrt(jnp.mean(shaped * shaped, axis=-1, keepdims=True) + EPS) * gain_row
    )
    return scaled.astype(jnp.bfloat16)


def visible_tiles(block_lists):
    position = lax.axis_index("seq")
    tile_dev = block_lists.shape[0]
    candidates = (position - 1) * tile_dev + jnp.arange(3 * tile_dev, dtype=jnp.int32)
    matches = (block_lists[:, :, None] == candidates[None, None, :]) & (
        block_lists[:, :, None] >= 0
    )
    return jnp.any(matches, axis=1)


def general(frames, modulation, w_qkv, b_qkv, qk_gain, block_lists):
    inputs = frames.astype(jnp.float32)
    average = jnp.mean(inputs, axis=-1, keepdims=True)
    centred = inputs - average
    variance = jnp.mean(centred * centred, axis=-1, keepdims=True)
    normed = centred * lax.rsqrt(variance + EPS) * (1.0 + modulation[0]) + modulation[1]
    normed = normed.astype(jnp.bfloat16)
    tokens = normed.shape[0]
    width_cols = w_qkv.shape[2]
    head_dim = qk_gain.shape[1]
    heads = width_cols // head_dim
    projected = jnp.einsum(
        "td,djc->tjc",
        normed,
        lax.all_gather(w_qkv, "seq", axis=0, tiled=True),
        preferred_element_type=jnp.float32,
    )
    projected = projected + b_qkv
    queries = normed_heads(projected[:, 0], qk_gain[0], head_dim)
    key_rows = normed_heads(projected[:, 1], qk_gain[1], head_dim)
    values = projected[:, 2].astype(jnp.bfloat16).reshape(tokens, heads, head_dim)
    stacked = jnp.stack([key_rows, values], axis=0)
    neighbourhood = with_halo(stacked, (("seq", 1),), tokens)
    tile_len = tokens // block_lists.shape[0]
    allowed_keys = jnp.repeat(
        jnp.repeat(visible_tiles(block_lists), tile_len, axis=0), tile_len, axis=1
    )
    factor = 1.0 / math.sqrt(head_dim)
    scores = (
        jnp.einsum("qhd,khd->hqk", queries, neighbourhood[0], preferred_element_type=jnp.float32)
        * factor
    )
    weights = jnp.where(allowed_keys[None, :, :], jnp.exp(scores), 0.0)
    totals = jnp.sum(weights, axis=-1)
    mixture = jnp.einsum(
        "hqk,khd->qhd",
        weights.astype(jnp.bfloat16),
        neighbourhood[1],
        preferred_element_type=jnp.float32,
    )
    result = (mixture / jnp.transpose(totals)[:, :, None]).astype(jnp.bfloat16)
    return result.reshape(tokens, width_cols)


class Line:
    def __init__(self):
        self.held = []

    def reached(self, *values):
        boxes = [[v] for v in values]
        self.held += boxes
        return boxes

    def after(self, *values):
        out = lax.optimization_barrier((*values, *(box[0] for box in self.held)))
        for box, value in zip(self.held, out[len(values) :]):
            box[0] = value
        return out[: len(values)]

    def drop(self, *boxes):
        self.held = [box for box in self.held if all(box is not b for b in boxes)]
        return [box[0] for box in boxes]


def norm_kernel(x_ref, mod_ref, o_ref):
    x = x_ref[...].astype(jnp.float32)
    centred = x - jnp.mean(x, axis=-1, keepdims=True)
    variance = jnp.mean(centred * centred, axis=-1, keepdims=True)
    scaled = centred * lax.rsqrt(variance + EPS) * (1.0 + mod_ref[0:1, :]) + mod_ref[1:2, :]
    o_ref[...] = scaled.astype(jnp.bfloat16)


def normalize(frames, modulation, rows, cost=COST):
    tokens, width = frames.shape
    return pl.pallas_call(
        norm_kernel,
        grid=(tokens // rows,),
        in_specs=[
            pl.BlockSpec((rows, width), lambda i: (i, 0)),
            pl.BlockSpec((2, width), lambda i: (0, 0)),
        ],
        out_specs=pl.BlockSpec((rows, width), lambda i: (i, 0)),
        out_shape=jax.ShapeDtypeStruct((tokens, width), jnp.bfloat16),
        cost_estimate=cost,
        name="normalize",
    )(frames, modulation)


def project(place, own_x, quarters, weights, bias, gain, norms, cost=COST):
    sources = [own_x] * (own_x is not None) + list(quarters)
    tokens = own_x.shape[0] if own_x is not None else 4 * quarters[0].shape[0]
    rows, cols = weights[0].shape
    head_dim = gain.shape[1]
    outs = (own_x is not None) + bool(quarters)
    step = 256

    def kernel(place_ref, *refs):
        x_refs, weight_refs = refs[: len(sources)], refs[len(sources) : len(sources) + 4]
        b_ref, g_ref = refs[len(sources) + 4 : len(sources) + 6]
        out_refs = refs[len(sources) + 6 :]
        z, q = place_ref[0], place_ref[1]

        def piece(ref, at, size, out_ref, to_row):
            total = b_ref[...]
            for s in range(4):
                cut = pl.multiple_of((z ^ s) * rows, 128)
                total = total + jnp.dot(
                    ref[pl.ds(at, size), pl.ds(cut, rows)],
                    weight_refs[s][...],
                    preferred_element_type=jnp.float32,
                )
            for i, row in enumerate(norms):
                part = total[:, i * head_dim : (i + 1) * head_dim]
                if row is not None:
                    mean = jnp.mean(part * part, axis=-1, keepdims=True)
                    part = part * lax.rsqrt(mean + EPS) * g_ref[row : row + 1, :]
                out_ref[pl.ds(to_row, size), i * head_dim : (i + 1) * head_dim] = part.astype(
                    jnp.bfloat16
                )

        if own_x is not None:
            for r in range(tokens // step):
                piece(x_refs[0], r * step, step, out_refs[0], r * step)
        for i, ref in enumerate(x_refs[len(sources) - len(quarters) :]):
            size = ref.shape[0]
            piece(ref, 0, size, out_refs[-1], pl.multiple_of((q ^ i) * size, 64))

    vmem = pl.BlockSpec(memory_space=pltpu.VMEM)
    out = jax.ShapeDtypeStruct((tokens, cols), jnp.bfloat16)
    return pl.pallas_call(
        kernel,
        in_specs=[pl.BlockSpec(memory_space=pltpu.SMEM)] + [vmem] * (len(sources) + 6),
        out_specs=[vmem] * outs,
        out_shape=[out] * outs,
        compiler_params=pltpu.CompilerParams(vmem_limit_bytes=40 << 20),
        cost_estimate=cost,
        name="project",
    )(place, *sources, *weights, bias, gain)


def tile_step(query, rows_ref, at, tile, head_dim, limit, total, mixed):
    scale = math.log2(math.e) / math.sqrt(head_dim)
    keys = rows_ref[at : at + tile, :head_dim]
    values = rows_ref[at : at + tile, head_dim:]
    scores = lax.dot_general(
        query, keys, (((1,), (1,)), ((), ())), preferred_element_type=jnp.float32
    )
    weights = jnp.exp2(scores * scale + limit)
    for c in range(tile // 128):
        total = total + weights[:, c * 128 : (c + 1) * 128]
    mixed = mixed + jnp.dot(
        weights.astype(jnp.bfloat16), values, preferred_element_type=jnp.float32
    )
    return total, mixed


def attend_pair(place, limits, queries, rows):
    tokens, head_dim = queries[0].shape
    tiles = limits.shape[1]
    tile = tokens // tiles

    def kernel(place_ref, limit_ref, q0_ref, q1_ref, rows0_ref, rows1_ref, done_ref, mixed_ref, total_ref):
        is_mid = (place_ref[0] == 1) | (place_ref[0] == 2)
        for column, q_ref in enumerate((q0_ref, q1_ref)):
            for i in range(tiles):
                here = slice(i * tile, (i + 1) * tile)
                query = q_ref[here, :]
                total = jnp.zeros((tile, 128), jnp.float32)
                mixed = jnp.zeros((tile, head_dim), jnp.float32)
                for side, ref in enumerate((rows0_ref, rows1_ref)):
                    for t in range(tiles):
                        limit = limit_ref[column, i, side * tiles + t]
                        total, mixed = tile_step(
                            query, ref, t * tile, tile, head_dim, limit, total, mixed
                        )
                is_edge = is_mid if column == 0 else jnp.logical_not(is_mid)

                @pl.when(is_edge)
                def _():
                    mixed_ref[here, :] = mixed
                    total_ref[here, :] = total

                @pl.when(jnp.logical_not(is_edge))
                def _():
                    done_ref[here, :] = (mixed / jnp.sum(total, axis=-1, keepdims=True)).astype(
                        jnp.bfloat16
                    )

    vmem = pl.BlockSpec(memory_space=pltpu.VMEM)
    smem = pl.BlockSpec(memory_space=pltpu.SMEM)
    return pl.pallas_call(
        kernel,
        in_specs=[smem, smem] + [vmem] * 4,
        out_specs=[vmem] * 3,
        out_shape=[
            jax.ShapeDtypeStruct((tokens, head_dim), jnp.bfloat16),
            jax.ShapeDtypeStruct((tokens, head_dim), jnp.float32),
            jax.ShapeDtypeStruct((tokens, 128), jnp.float32),
        ],
        compiler_params=pltpu.CompilerParams(vmem_limit_bytes=40 << 20),
        cost_estimate=COST,
        name="attend_pair",
    )(place, limits, *queries, *rows)


def attend_halo(place, limits, queries, halo, done, mixed, total):
    tokens, head_dim = queries[0].shape
    tiles = limits.shape[1]
    tile = tokens // tiles

    def kernel(place_ref, limit_ref, q0_ref, q1_ref, halo_ref, done_ref, mixed_ref, total_ref, keep_ref, send_ref):
        is_mid = (place_ref[0] == 1) | (place_ref[0] == 2)
        column = jnp.where(is_mid, 0, 1)
        for i in range(tiles):
            here = slice(i * tile, (i + 1) * tile)
            query = jnp.where(is_mid, q0_ref[here, :], q1_ref[here, :])
            sums, rows = total_ref[here, :], mixed_ref[here, :]
            for t in range(tiles):
                limit = limit_ref[column, i, 2 * tiles + t]
                sums, rows = tile_step(query, halo_ref, t * tile, tile, head_dim, limit, sums, rows)
            edge = (rows / jnp.sum(sums, axis=-1, keepdims=True)).astype(jnp.bfloat16)
            outer = done_ref[here, :]
            keep_ref[here, :] = jnp.where(is_mid, edge, outer)
            send_ref[here, :] = jnp.where(is_mid, outer, edge)

    vmem = pl.BlockSpec(memory_space=pltpu.VMEM)
    smem = pl.BlockSpec(memory_space=pltpu.SMEM)
    out = jax.ShapeDtypeStruct((tokens, head_dim), jnp.bfloat16)
    return pl.pallas_call(
        kernel,
        in_specs=[smem, smem] + [vmem] * 6,
        out_specs=[vmem, vmem],
        out_shape=[out, out],
        compiler_params=pltpu.CompilerParams(vmem_limit_bytes=40 << 20),
        cost_estimate=COST,
        name="attend_halo",
    )(place, limits, *queries, halo, done, mixed, total)


def assemble(heads, parts):
    tokens, head_dim = parts[0].shape

    def kernel(head_ref, *refs):
        for i, ref in enumerate(refs[:-1]):
            refs[-1][:, pl.ds(pl.multiple_of(head_ref[i] * head_dim, 128), head_dim)] = ref[...]

    vmem = pl.BlockSpec(memory_space=pltpu.VMEM)
    return pl.pallas_call(
        kernel,
        in_specs=[pl.BlockSpec(memory_space=pltpu.SMEM)] + [vmem] * len(parts),
        out_specs=vmem,
        out_shape=jax.ShapeDtypeStruct((tokens, head_dim * len(parts)), jnp.bfloat16),
        cost_estimate=COST,
        name="assemble",
    )(heads, *parts)


def seen(lists, columns, tile_dev):
    tiles = (columns[:, None] * tile_dev + jnp.arange(tile_dev, dtype=jnp.int32)).reshape(-1)
    listed = jnp.any(
        (lists[:, :, None] == tiles[None, None, :]) & (lists[:, :, None] >= 0), axis=1
    )
    return jnp.where(listed, 0.0, HIDDEN).astype(jnp.float32)


def per_device(frames, modulation, w_qkv, b_qkv, qk_gain, block_lists):
    sizes = tuple(lax.axis_size(a) for a in ("groups", "seq", "fsdp", "head"))
    head_dim = qk_gain.shape[1]
    width_cols = w_qkv.shape[2]
    tokens = frames.shape[0]
    if sizes != (2, 4, 2, 2) or width_cols != 4 * head_dim:
        return general(frames, modulation, w_qkv, b_qkv, qk_gain, block_lists)

    y, z, x, core = (lax.axis_index(a).astype(jnp.int32) for a in ("groups", "seq", "fsdp", "head"))
    rows = w_qkv.shape[0]
    quarter = tokens // 4
    tile_dev = block_lists.shape[0]

    def to(axis, value, bit):
        return lax.ppermute(value, axis, [(i, i ^ bit) for i in range(lax.axis_size(axis))])

    side = z % 2
    mine, twin = 2 * side + y, 2 * side + 1 - y
    other = 2 * (1 - side) + y
    w = jnp.transpose(w_qkv, (1, 0, 2))

    def cut(first, count, head):
        parts = [
            lax.dynamic_slice(w, (j, 0, head * head_dim), (1, rows, head_dim))[0]
            for j in range(first, first + count)
        ]
        return jnp.concatenate(parts, axis=1)

    def biases(first, count, head):
        return lax.dynamic_slice(b_qkv, (first, head * head_dim), (count, head_dim)).reshape(1, -1)

    KV, Q = (1, 2), (0, 1)
    q_at = 2 * x + core
    place = jnp.stack([z, q_at])

    near = jnp.stack([z, z ^ 1, jnp.where(z < 2, 2, 1)])
    is_mid = (z == 1) | (z == 2)
    line = Line()

    raw = lax.dynamic_slice(frames, (q_at * quarter, 0), (quarter, frames.shape[1]))
    same, cross, own_twin, got = {}, {}, {}, {}
    for part in (KV, Q):
        same[part], cross[part] = cut(*part, mine), cut(*part, other)
    cuts = line.reached(raw, *same.values(), *cross.values())
    raw_other = to("seq", cuts[0][0], 1)
    for i, part in enumerate((KV, Q)):
        got[part] = [
            to("seq", cuts[1 + i][0], 2),
            to("seq", cuts[3 + i][0], 3),
            to("seq", cuts[3 + i][0], 1),
        ]
    lists_other = to("seq", block_lists, 1)
    (frames,) = line.after(frames)
    own_x = line.reached(normalize(frames, modulation, 128, LONG))
    line.drop(*cuts)

    (raw_other,) = line.after(raw_other)
    near_q = line.reached(normalize(raw_other, modulation, 96))
    far_q = to("fsdp", near_q[0][0], 1)
    near_c = to("head", near_q[0][0], 1)

    def swaps(part):
        arrived, back = [], []
        for value in got[part]:
            box = line.reached(value)[0]
            (ready,) = line.after(box[0])
            box[0] = ready
            arrived.append(box)
            back.append(to("groups", ready, 1))
        return arrived, back

    for part in (KV, Q):
        own_twin[part] = cut(*part, twin)

    def run(part, head, boxes, norms, own, far, cost=COST):
        mine_w = (same if head is mine else own_twin)[part]
        (mine_w,) = line.after(mine_w)
        two, three, one = (box[0] for box in boxes)
        return line.reached(
            *project(
                place, own_x[0][0] if own else None, [b[0] for b in quarters] if far else [],
                [mine_w, one, two, three], biases(*part, head), qk_gain, norms, cost,
            )
        )

    quarters = []
    kv_boxes, kv_back = swaps(KV)
    rows_mine = run(KV, mine, kv_boxes, (1, None), True, False, LONG)
    far_box = line.reached(far_q)
    (far_ready,) = line.after(far_box[0][0])
    far_box[0][0] = far_ready
    far_c = to("head", far_ready, 1)
    quarters = near_q + line.reached(near_c) + far_box + line.reached(far_c)
    rows_mine += run(KV, mine, kv_boxes, (1, None), False, True)
    line.drop(*kv_boxes)

    def send_edge(rows):
        return to("seq", jnp.where(is_mid, rows[0][0], rows[1][0]), 2)

    halo_mine = send_edge(rows_mine)
    q_boxes, q_back = swaps(Q)
    q_mine = run(Q, mine, q_boxes, (0,), True, True)
    line.drop(*q_boxes)
    kv_boxes = line.reached(*kv_back)
    rows_twin = run(KV, twin, kv_boxes, (1, None), True, True)
    line.drop(*kv_boxes)
    halo_twin = send_edge(rows_twin)

    limits = jnp.stack([seen(v, near, tile_dev) for v in (block_lists, lists_other)])

    def pair(q, rows):
        (limit,) = line.after(limits)
        return line.reached(*attend_pair(place, limit, [b[0] for b in q], [b[0] for b in rows]))

    parts_mine = pair(q_mine, rows_mine)
    q_boxes = line.reached(*q_back)
    q_twin = run(Q, twin, q_boxes, (0,), True, True)
    line.drop(*q_boxes, *own_x, *quarters)
    parts_twin = pair(q_twin, rows_twin)
    line.drop(*rows_mine, *rows_twin)

    keeps, sends = [], []
    for q, halo, parts in ((q_mine, halo_mine, parts_mine), (q_twin, halo_twin, parts_twin)):
        (limit,) = line.after(limits)
        keep, send = attend_halo(place, limit, [b[0] for b in q], halo, *(b[0] for b in parts))
        line.reached(keep)
        keeps.append(keep)
        sends.append(to("seq", send, 1))
    across = 2 * (1 - side)
    heads = jnp.stack([mine, twin, across + y, across + 1 - y])
    return assemble(heads, [*keeps, *sends])


def solution(mesh):
    placed = (
        P(("groups", "seq"), None),
        P("groups", None),
        P("seq", None, ("fsdp", "head")),
        P(None, ("fsdp", "head")),
        P(),
        P(("groups", "seq"), None),
    )
    return jax.shard_map(
        per_device,
        mesh=mesh,
        in_specs=placed,
        out_specs=P(("groups", "seq"), ("fsdp", "head")),
        check_vma=False,
    )
```

```python
import math

import jax
import jax.numpy as jnp
from jax import lax
from jax.experimental import pallas as pl
from jax.experimental.pallas import tpu as pltpu
from jax.sharding import PartitionSpec as P

EPS = 1e-06
HIDDEN = -1e30
COST = pl.CostEstimate(flops=1 << 20, bytes_accessed=1 << 10, transcendentals=0)
MIDDLE = pl.CostEstimate(flops=1 << 33, bytes_accessed=1 << 10, transcendentals=0)
LONG = pl.CostEstimate(flops=1 << 37, bytes_accessed=1 << 10, transcendentals=0)


def with_halo(shard, sides, width):
    for axis, dim in sides:
        devices, length = (lax.axis_size(axis), shard.shape[dim])
        up = [(i, (i + 1) % devices) for i in range(devices - 1)]
        down = [(j, i) for i, j in up]
        last = lax.slice_in_dim(shard, length - width, length, axis=dim)
        first = lax.slice_in_dim(shard, 0, width, axis=dim)
        before = lax.ppermute(last, axis, up)
        after = lax.ppermute(first, axis, down)
        shard = jnp.concatenate([before, shard, after], axis=dim)
    return shard


def normed_heads(tensor, gain_row, head_dim):
    shaped = tensor.reshape(tensor.shape[0], tensor.shape[1] // head_dim, head_dim)
    scaled = (
        shaped * lax.rsqrt(jnp.mean(shaped * shaped, axis=-1, keepdims=True) + EPS) * gain_row
    )
    return scaled.astype(jnp.bfloat16)


def visible_tiles(block_lists):
    position = lax.axis_index("seq")
    tile_dev = block_lists.shape[0]
    candidates = (position - 1) * tile_dev + jnp.arange(3 * tile_dev, dtype=jnp.int32)
    matches = (block_lists[:, :, None] == candidates[None, None, :]) & (
        block_lists[:, :, None] >= 0
    )
    return jnp.any(matches, axis=1)


def general(frames, modulation, w_qkv, b_qkv, qk_gain, block_lists):
    inputs = frames.astype(jnp.float32)
    average = jnp.mean(inputs, axis=-1, keepdims=True)
    centred = inputs - average
    variance = jnp.mean(centred * centred, axis=-1, keepdims=True)
    normed = centred * lax.rsqrt(variance + EPS) * (1.0 + modulation[0]) + modulation[1]
    normed = normed.astype(jnp.bfloat16)
    tokens = normed.shape[0]
    width_cols = w_qkv.shape[2]
    head_dim = qk_gain.shape[1]
    heads = width_cols // head_dim
    projected = jnp.einsum(
        "td,djc->tjc",
        normed,
        lax.all_gather(w_qkv, "seq", axis=0, tiled=True),
        preferred_element_type=jnp.float32,
    )
    projected = projected + b_qkv
    queries = normed_heads(projected[:, 0], qk_gain[0], head_dim)
    key_rows = normed_heads(projected[:, 1], qk_gain[1], head_dim)
    values = projected[:, 2].astype(jnp.bfloat16).reshape(tokens, heads, head_dim)
    stacked = jnp.stack([key_rows, values], axis=0)
    neighbourhood = with_halo(stacked, (("seq", 1),), tokens)
    tile_len = tokens // block_lists.shape[0]
    allowed_keys = jnp.repeat(
        jnp.repeat(visible_tiles(block_lists), tile_len, axis=0), tile_len, axis=1
    )
    factor = 1.0 / math.sqrt(head_dim)
    scores = (
        jnp.einsum("qhd,khd->hqk", queries, neighbourhood[0], preferred_element_type=jnp.float32)
        * factor
    )
    weights = jnp.where(allowed_keys[None, :, :], jnp.exp(scores), 0.0)
    totals = jnp.sum(weights, axis=-1)
    mixture = jnp.einsum(
        "hqk,khd->qhd",
        weights.astype(jnp.bfloat16),
        neighbourhood[1],
        preferred_element_type=jnp.float32,
    )
    result = (mixture / jnp.transpose(totals)[:, :, None]).astype(jnp.bfloat16)
    return result.reshape(tokens, width_cols)


class Line:
    def __init__(self):
        self.held = []

    def reached(self, *values):
        boxes = [[v] for v in values]
        self.held += boxes
        return boxes

    def after(self, *values):
        out = lax.optimization_barrier((*values, *(box[0] for box in self.held)))
        for box, value in zip(self.held, out[len(values) :]):
            box[0] = value
        return out[: len(values)]

    def drop(self, *boxes):
        self.held = [box for box in self.held if all(box is not b for b in boxes)]
        return [box[0] for box in boxes]


def norm_kernel(x_ref, mod_ref, o_ref):
    x = x_ref[...].astype(jnp.float32)
    centred = x - jnp.mean(x, axis=-1, keepdims=True)
    variance = jnp.mean(centred * centred, axis=-1, keepdims=True)
    scaled = centred * lax.rsqrt(variance + EPS) * (1.0 + mod_ref[0:1, :]) + mod_ref[1:2, :]
    o_ref[...] = scaled.astype(jnp.bfloat16)


def normalize(frames, modulation, rows, cost=COST):
    tokens, width = frames.shape
    return pl.pallas_call(
        norm_kernel,
        grid=(tokens // rows,),
        in_specs=[
            pl.BlockSpec((rows, width), lambda i: (i, 0)),
            pl.BlockSpec((2, width), lambda i: (0, 0)),
        ],
        out_specs=pl.BlockSpec((rows, width), lambda i: (i, 0)),
        out_shape=jax.ShapeDtypeStruct((tokens, width), jnp.bfloat16),
        cost_estimate=cost,
        name="normalize",
    )(frames, modulation)


def cut_heads(at, w, groups, cost=COST):
    rows = w.shape[1]
    head_dim = 128
    widths = [head_dim * len(js) for _, js in groups]

    def kernel(at_ref, w_ref, *out_refs):
        for (index, js), ref in zip(groups, out_refs):
            cols = pl.ds(pl.multiple_of(at_ref[index] * head_dim, 128), head_dim)
            for i, j in enumerate(js):
                ref[:, i * head_dim : (i + 1) * head_dim] = w_ref[j, :, cols]

    return pl.pallas_call(
        kernel,
        in_specs=[pl.BlockSpec(memory_space=pltpu.SMEM), pl.BlockSpec()],
        out_specs=[pl.BlockSpec()] * len(groups),
        out_shape=[jax.ShapeDtypeStruct((rows, n), jnp.bfloat16) for n in widths],
        compiler_params=pltpu.CompilerParams(vmem_limit_bytes=24 << 20),
        cost_estimate=cost,
        name="cut_heads",
    )(at, w)


def see(at, lists, tile_dev):
    def kernel(at_ref, lists_ref, o_ref):
        lists = lists_ref[...]
        z = at_ref[0]
        lane = lax.broadcasted_iota(jnp.int32, o_ref.shape, 1)
        out = jnp.full(o_ref.shape, HIDDEN, jnp.float32)
        for c, column in enumerate((z, z ^ 1, jnp.where(z < 2, 2, 1))):
            for t in range(tile_dev):
                hit = (lists == column * tile_dev + t).astype(jnp.float32)
                listed = jnp.max(hit, axis=1, keepdims=True) > 0.0
                out = jnp.where((lane == c * tile_dev + t) & listed, 0.0, out)
        o_ref[...] = out

    return pl.pallas_call(
        kernel,
        in_specs=[pl.BlockSpec(memory_space=pltpu.SMEM), pl.BlockSpec()],
        out_specs=pl.BlockSpec(),
        out_shape=jax.ShapeDtypeStruct((lists.shape[0], 128), jnp.float32),
        cost_estimate=COST,
        name="see",
    )(at, lists)


def project(at, head_index, first, own_x, quarters, weights, bias, gain, norms, cost=COST):
    rows, cols = weights[0].shape
    head_dim = gain.shape[1]
    sources = [own_x] if quarters is None else list(quarters)
    tokens = own_x.shape[0] if quarters is None else 4 * quarters[0].shape[0]
    width = sources[0].shape[1]
    step = 256

    def kernel(at_ref, *refs):
        x_refs, weight_refs = refs[: len(sources)], refs[len(sources) : len(sources) + 4]
        b_ref, g_ref, out_ref = refs[len(sources) + 4 :]
        z, q = at_ref[0], at_ref[1]
        here = pl.ds(pl.multiple_of(at_ref[head_index] * head_dim, 128), head_dim)

        def piece(ref, to_row):
            total = None
            for s in range(4):
                cut = pl.multiple_of((z ^ s) * rows, 128)
                part = jnp.dot(
                    ref[:, pl.ds(cut, rows)],
                    weight_refs[s][...],
                    preferred_element_type=jnp.float32,
                )
                total = part if total is None else total + part
            for i, row in enumerate(norms):
                part = total[:, i * head_dim : (i + 1) * head_dim]
                part = part + b_ref[first + i : first + i + 1, here]
                if row is not None:
                    mean = jnp.mean(part * part, axis=-1, keepdims=True)
                    part = part * lax.rsqrt(mean + EPS) * g_ref[row : row + 1, :]
                out_ref[pl.ds(to_row, ref.shape[0]), i * head_dim : (i + 1) * head_dim] = (
                    part.astype(jnp.bfloat16)
                )

        if quarters is None:
            piece(x_refs[0], 0)
        else:
            for i, ref in enumerate(x_refs):
                piece(ref, pl.multiple_of((q ^ i) * ref.shape[0], 64))

    smem = pl.BlockSpec(memory_space=pltpu.SMEM)
    if quarters is None:
        grid = (tokens // step,)
        fixed = lambda shape: pl.BlockSpec(shape, lambda i: (0,) * len(shape))
        x_specs = [pl.BlockSpec((step, width), lambda i: (i, 0))]
        out_spec = pl.BlockSpec((step, cols), lambda i: (i, 0))
    else:
        grid = ()
        fixed = lambda shape: pl.BlockSpec()
        x_specs = [pl.BlockSpec()] * 4
        out_spec = pl.BlockSpec()
    return pl.pallas_call(
        kernel,
        grid=grid,
        in_specs=[smem, *x_specs, *(fixed(w.shape) for w in weights), fixed(bias.shape), fixed(gain.shape)],
        out_specs=out_spec,
        out_shape=jax.ShapeDtypeStruct((tokens, cols), jnp.bfloat16),
        compiler_params=pltpu.CompilerParams(vmem_limit_bytes=40 << 20),
        cost_estimate=cost,
        name="project",
    )(at, *sources, *weights, bias, gain)


def tile_step(query, rows_ref, at, tile, head_dim, limit, total, mixed):
    scale = math.log2(math.e) / math.sqrt(head_dim)
    keys = rows_ref[at : at + tile, :head_dim]
    values = rows_ref[at : at + tile, head_dim:]
    scores = lax.dot_general(
        query, keys, (((1,), (1,)), ((), ())), preferred_element_type=jnp.float32
    )
    weights = jnp.exp2(scores * scale + limit)
    for c in range(tile // 128):
        total = total + weights[:, c * 128 : (c + 1) * 128]
    mixed = mixed + jnp.dot(
        weights.astype(jnp.bfloat16), values, preferred_element_type=jnp.float32
    )
    return total, mixed


def attend_pair(place, limits, queries, rows):
    tokens, head_dim = queries[0].shape
    tiles = limits[0].shape[0]
    tile = tokens // tiles

    def kernel(place_ref, limit0_ref, limit1_ref, q0_ref, q1_ref, rows0_ref, rows1_ref, done_ref, mixed_ref, total_ref):
        is_mid = (place_ref[0] == 1) | (place_ref[0] == 2)
        for column, q_ref in enumerate((q0_ref, q1_ref)):
            for i in range(tiles):
                here = slice(i * tile, (i + 1) * tile)
                query = q_ref[here, :]
                total = jnp.zeros((tile, 128), jnp.float32)
                mixed = jnp.zeros((tile, head_dim), jnp.float32)
                for side, ref in enumerate((rows0_ref, rows1_ref)):
                    for t in range(tiles):
                        limit = (limit0_ref, limit1_ref)[column][i, (side ^ column) * tiles + t]
                        total, mixed = tile_step(
                            query, ref, t * tile, tile, head_dim, limit, total, mixed
                        )
                is_edge = is_mid if column == 0 else jnp.logical_not(is_mid)

                @pl.when(is_edge)
                def _():
                    mixed_ref[here, :] = mixed
                    total_ref[here, :] = total

                @pl.when(jnp.logical_not(is_edge))
                def _():
                    done_ref[here, :] = (mixed / jnp.sum(total, axis=-1, keepdims=True)).astype(
                        jnp.bfloat16
                    )

    vmem = pl.BlockSpec()
    smem = pl.BlockSpec(memory_space=pltpu.SMEM)
    return pl.pallas_call(
        kernel,
        in_specs=[smem, smem, smem] + [vmem] * 4,
        out_specs=[vmem] * 3,
        out_shape=[
            jax.ShapeDtypeStruct((tokens, head_dim), jnp.bfloat16),
            jax.ShapeDtypeStruct((tokens, head_dim), jnp.float32),
            jax.ShapeDtypeStruct((tokens, 128), jnp.float32),
        ],
        compiler_params=pltpu.CompilerParams(vmem_limit_bytes=40 << 20),
        cost_estimate=COST,
        name="attend_pair",
    )(place, *limits, *queries, *rows)


def attend_halo(place, limits, queries, halo, done, mixed, total):
    tokens, head_dim = queries[0].shape
    tiles = limits[0].shape[0]
    tile = tokens // tiles

    def kernel(place_ref, limit0_ref, limit1_ref, q0_ref, q1_ref, halo_ref, done_ref, mixed_ref, total_ref, keep_ref, send_ref):
        is_mid = (place_ref[0] == 1) | (place_ref[0] == 2)
        for i in range(tiles):
            here = slice(i * tile, (i + 1) * tile)
            query = jnp.where(is_mid, q0_ref[here, :], q1_ref[here, :])
            sums, rows = total_ref[here, :], mixed_ref[here, :]
            for t in range(tiles):
                limit = jnp.where(is_mid, limit0_ref[i, 2 * tiles + t], limit1_ref[i, 2 * tiles + t])
                sums, rows = tile_step(query, halo_ref, t * tile, tile, head_dim, limit, sums, rows)
            edge = (rows / jnp.sum(sums, axis=-1, keepdims=True)).astype(jnp.bfloat16)
            outer = done_ref[here, :]
            keep_ref[here, :] = jnp.where(is_mid, edge, outer)
            send_ref[here, :] = jnp.where(is_mid, outer, edge)

    vmem = pl.BlockSpec()
    smem = pl.BlockSpec(memory_space=pltpu.SMEM)
    out = jax.ShapeDtypeStruct((tokens, head_dim), jnp.bfloat16)
    return pl.pallas_call(
        kernel,
        in_specs=[smem, smem, smem] + [vmem] * 6,
        out_specs=[vmem, vmem],
        out_shape=[out, out],
        compiler_params=pltpu.CompilerParams(vmem_limit_bytes=40 << 20),
        cost_estimate=COST,
        name="attend_halo",
    )(place, *limits, *queries, halo, done, mixed, total)


def assemble(at, parts, carried=None, heads=4):
    indices, arrays = zip(*parts)
    tokens, head_dim = arrays[0].shape
    carried = () if carried is None else (carried,)

    def kernel(at_ref, *refs):
        out_ref, sems = refs[-2:]
        copies = []
        for i, (index, ref) in enumerate(zip(indices, refs)):
            cols = pl.ds(pl.multiple_of(at_ref[index] * head_dim, 128), head_dim)
            copies.append(pltpu.make_async_copy(ref, out_ref.at[:, cols], sems.at[i]))
            copies[-1].start()
        for copy in copies:
            copy.wait()

    anywhere = pl.BlockSpec(memory_space=pl.ANY)
    return pl.pallas_call(
        kernel,
        in_specs=[pl.BlockSpec(memory_space=pltpu.SMEM)] + [anywhere] * (len(arrays) + len(carried)),
        out_specs=anywhere,
        out_shape=jax.ShapeDtypeStruct((tokens, head_dim * heads), jnp.bfloat16),
        scratch_shapes=[pltpu.SemaphoreType.DMA((len(arrays),))],
        input_output_aliases={1 + len(arrays): 0} if carried else {},
        cost_estimate=COST,
        name="assemble",
    )(at, *arrays, *carried)


def per_device(frames, modulation, w_qkv, b_qkv, qk_gain, block_lists):
    sizes = tuple(lax.axis_size(a) for a in ("groups", "seq", "fsdp", "head"))
    head_dim = qk_gain.shape[1]
    width_cols = w_qkv.shape[2]
    tokens = frames.shape[0]
    if sizes != (2, 4, 2, 2) or width_cols != 4 * head_dim:
        return general(frames, modulation, w_qkv, b_qkv, qk_gain, block_lists)

    y, z, x, core = (lax.axis_index(a).astype(jnp.int32) for a in ("groups", "seq", "fsdp", "head"))
    rows = w_qkv.shape[0]
    quarter = tokens // 4
    tile_dev = block_lists.shape[0]

    def to(axis, value, bit):
        return lax.ppermute(value, axis, [(i, i ^ bit) for i in range(lax.axis_size(axis))])

    side = z % 2
    mine, twin = 2 * side + y, 2 * side + 1 - y
    across = 2 * (1 - side)
    at = jnp.stack([z, 2 * x + core, mine, twin, across + y, across + 1 - y])
    MINE, TWIN, CROSS, CROSS_TWIN = 2, 3, 4, 5
    KV, Q = (1, 2), (0,)
    NORMS = {KV: (1, None), Q: (0,)}
    is_mid = (z == 1) | (z == 2)
    w = jnp.transpose(w_qkv, (1, 0, 2))
    line = Line()

    raw = lax.dynamic_slice(frames, (at[1] * quarter, 0), (quarter, frames.shape[1]))
    raw_other = to("seq", raw, 1)
    w, raw = lax.optimization_barrier((w, raw))
    cuts = cut_heads(at, w, [(MINE, KV), (CROSS, KV), (MINE, Q), (CROSS, Q)], LONG)
    cuts = line.reached(*cuts)
    own_w = {(MINE, KV): cuts[0], (MINE, Q): cuts[2]}
    got = {}
    for part, same, cross in ((KV, *cuts[:2]), (Q, *cuts[2:])):
        got[part] = [to("seq", same[0], 2), to("seq", cross[0], 3), to("seq", cross[0], 1)]
    frames, modulation = line.after(frames, modulation)
    own_x = line.reached(normalize(frames, modulation, 128, MIDDLE))
    line.drop(cuts[1], cuts[3])
    (w,) = line.after(w)
    for key, box in zip(((TWIN, KV), (TWIN, Q)), line.reached(*cut_heads(at, w, [(TWIN, KV), (TWIN, Q)]))):
        own_w[key] = box
    own_limit = line.reached(see(at, block_lists, tile_dev))
    far_limit = to("seq", own_limit[0][0], 1)

    (raw_other,) = line.after(raw_other)
    near_q = line.reached(normalize(raw_other, modulation, 96))
    far_q = to("fsdp", near_q[0][0], 1)
    near_c = to("head", near_q[0][0], 1)

    def arrive(value):
        box = line.reached(value)[0]
        (box[0],) = line.after(box[0])
        return box

    def swaps(part):
        boxes = [arrive(value) for value in got[part]]
        return boxes, [to("groups", box[0], 1) for box in boxes]

    def run(head, part, boxes, own, cost=COST):
        (own_part,) = line.after(own_w[head, part][0])
        own_w[head, part][0] = own_part
        two, three, one = (box[0] for box in boxes)
        return line.reached(
            project(
                at, head, part[0], own_x[0][0] if own else None,
                None if own else [b[0] for b in quarters],
                [own_part, one, two, three], b_qkv, qk_gain, NORMS[part], cost,
            )
        )

    def send_edge(rows):
        return to("seq", jnp.where(is_mid, rows[0][0], rows[1][0]), 2)

    kv_boxes, kv_back = swaps(KV)
    rows_mine = run(MINE, KV, kv_boxes, True, LONG)
    far_box = arrive(far_q)
    far_c = to("head", far_box[0], 1)
    kv_twin = line.reached(*kv_back)
    rows_twin = run(TWIN, KV, kv_twin, True, LONG)
    quarters = near_q + line.reached(near_c) + [far_box] + line.reached(far_c)
    rows_mine += run(MINE, KV, kv_boxes, False)
    halo_mine = send_edge(rows_mine)
    rows_twin += run(TWIN, KV, kv_twin, False)
    halo_twin = send_edge(rows_twin)
    line.drop(*kv_boxes, *kv_twin)
    q_boxes, q_back = swaps(Q)
    q_mine = run(MINE, Q, q_boxes, True)
    q_mine += run(MINE, Q, q_boxes, False)
    line.drop(*q_boxes)

    limits = own_limit + line.reached(far_limit)

    def pair(q, rows):
        parts = attend_pair(at, [b[0] for b in limits], [b[0] for b in q], [b[0] for b in rows])
        return line.reached(*parts)

    def finish(q, halo, parts):
        keep, send = attend_halo(
            at, [b[0] for b in limits], [b[0] for b in q], halo, *(b[0] for b in parts)
        )
        return line.reached(keep)[0], to("seq", send, 1)

    parts_mine = pair(q_mine, rows_mine)
    q_twin_w = line.reached(*q_back)
    q_twin = run(TWIN, Q, q_twin_w, True)
    q_twin += run(TWIN, Q, q_twin_w, False)
    line.drop(*q_twin_w, *own_x, *quarters, *rows_mine)
    (halo_mine,) = line.after(halo_mine)
    keep_mine, back_mine = finish(q_mine, halo_mine, parts_mine)
    line.drop(*q_mine, *parts_mine)
    q_twin[0][0], q_twin[1][0] = line.after(q_twin[0][0], q_twin[1][0])
    parts_twin = pair(q_twin, rows_twin)
    (halo_twin,) = line.after(halo_twin)
    keep_twin, back_twin = finish(q_twin, halo_twin, parts_twin)
    parts = [(MINE, keep_mine[0]), (TWIN, keep_twin[0]), (CROSS, back_mine)]
    return assemble(at, [(CROSS_TWIN, back_twin)], assemble(at, parts))


def solution(mesh):
    placed = (
        P(("groups", "seq"), None),
        P("groups", None),
        P("seq", None, ("fsdp", "head")),
        P(None, ("fsdp", "head")),
        P(),
        P(("groups", "seq"), None),
    )
    return jax.shard_map(
        per_device,
        mesh=mesh,
        in_specs=placed,
        out_specs=P(("groups", "seq"), ("fsdp", "head")),
        check_vma=False,
    )
```

```python
import math

import jax
import jax.numpy as jnp
from jax import lax
from jax.experimental import pallas as pl
from jax.experimental.pallas import tpu as pltpu
from jax.sharding import PartitionSpec as P

EPS = 1e-06
HIDDEN = -1e30
COST = pl.CostEstimate(flops=1 << 20, bytes_accessed=1 << 10, transcendentals=0)
MIDDLE = pl.CostEstimate(flops=1 << 33, bytes_accessed=1 << 10, transcendentals=0)
LONG = pl.CostEstimate(flops=1 << 37, bytes_accessed=1 << 10, transcendentals=0)


def with_halo(shard, sides, width):
    for axis, dim in sides:
        devices, length = (lax.axis_size(axis), shard.shape[dim])
        up = [(i, (i + 1) % devices) for i in range(devices - 1)]
        down = [(j, i) for i, j in up]
        last = lax.slice_in_dim(shard, length - width, length, axis=dim)
        first = lax.slice_in_dim(shard, 0, width, axis=dim)
        before = lax.ppermute(last, axis, up)
        after = lax.ppermute(first, axis, down)
        shard = jnp.concatenate([before, shard, after], axis=dim)
    return shard


def normed_heads(tensor, gain_row, head_dim):
    shaped = tensor.reshape(tensor.shape[0], tensor.shape[1] // head_dim, head_dim)
    scaled = (
        shaped * lax.rsqrt(jnp.mean(shaped * shaped, axis=-1, keepdims=True) + EPS) * gain_row
    )
    return scaled.astype(jnp.bfloat16)


def visible_tiles(block_lists):
    position = lax.axis_index("seq")
    tile_dev = block_lists.shape[0]
    candidates = (position - 1) * tile_dev + jnp.arange(3 * tile_dev, dtype=jnp.int32)
    matches = (block_lists[:, :, None] == candidates[None, None, :]) & (
        block_lists[:, :, None] >= 0
    )
    return jnp.any(matches, axis=1)


def general(frames, modulation, w_qkv, b_qkv, qk_gain, block_lists):
    inputs = frames.astype(jnp.float32)
    average = jnp.mean(inputs, axis=-1, keepdims=True)
    centred = inputs - average
    variance = jnp.mean(centred * centred, axis=-1, keepdims=True)
    normed = centred * lax.rsqrt(variance + EPS) * (1.0 + modulation[0]) + modulation[1]
    normed = normed.astype(jnp.bfloat16)
    tokens = normed.shape[0]
    width_cols = w_qkv.shape[2]
    head_dim = qk_gain.shape[1]
    heads = width_cols // head_dim
    projected = jnp.einsum(
        "td,djc->tjc",
        normed,
        lax.all_gather(w_qkv, "seq", axis=0, tiled=True),
        preferred_element_type=jnp.float32,
    )
    projected = projected + b_qkv
    queries = normed_heads(projected[:, 0], qk_gain[0], head_dim)
    key_rows = normed_heads(projected[:, 1], qk_gain[1], head_dim)
    values = projected[:, 2].astype(jnp.bfloat16).reshape(tokens, heads, head_dim)
    stacked = jnp.stack([key_rows, values], axis=0)
    neighbourhood = with_halo(stacked, (("seq", 1),), tokens)
    tile_len = tokens // block_lists.shape[0]
    allowed_keys = jnp.repeat(
        jnp.repeat(visible_tiles(block_lists), tile_len, axis=0), tile_len, axis=1
    )
    factor = 1.0 / math.sqrt(head_dim)
    scores = (
        jnp.einsum("qhd,khd->hqk", queries, neighbourhood[0], preferred_element_type=jnp.float32)
        * factor
    )
    weights = jnp.where(allowed_keys[None, :, :], jnp.exp(scores), 0.0)
    totals = jnp.sum(weights, axis=-1)
    mixture = jnp.einsum(
        "hqk,khd->qhd",
        weights.astype(jnp.bfloat16),
        neighbourhood[1],
        preferred_element_type=jnp.float32,
    )
    result = (mixture / jnp.transpose(totals)[:, :, None]).astype(jnp.bfloat16)
    return result.reshape(tokens, width_cols)


class Line:
    def __init__(self):
        self.held = []

    def reached(self, *values):
        boxes = [[v] for v in values]
        self.held += boxes
        return boxes

    def after(self, *values):
        out = lax.optimization_barrier((*values, *(box[0] for box in self.held)))
        for box, value in zip(self.held, out[len(values) :]):
            box[0] = value
        return out[: len(values)]

    def drop(self, *boxes):
        self.held = [box for box in self.held if all(box is not b for b in boxes)]
        return [box[0] for box in boxes]


def norm_kernel(x_ref, mod_ref, o_ref):
    x = x_ref[...].astype(jnp.float32)
    centred = x - jnp.mean(x, axis=-1, keepdims=True)
    variance = jnp.mean(centred * centred, axis=-1, keepdims=True)
    scaled = centred * lax.rsqrt(variance + EPS) * (1.0 + mod_ref[0:1, :]) + mod_ref[1:2, :]
    o_ref[...] = scaled.astype(jnp.bfloat16)


def normalize(frames, modulation, rows, cost=COST):
    tokens, width = frames.shape
    return pl.pallas_call(
        norm_kernel,
        grid=(tokens // rows,),
        in_specs=[
            pl.BlockSpec((rows, width), lambda i: (i, 0)),
            pl.BlockSpec((2, width), lambda i: (0, 0)),
        ],
        out_specs=pl.BlockSpec((rows, width), lambda i: (i, 0)),
        out_shape=jax.ShapeDtypeStruct((tokens, width), jnp.bfloat16),
        cost_estimate=cost,
        name="normalize",
    )(frames, modulation)


def cut_heads(at, w, groups, cost=COST):
    rows = w.shape[1]
    head_dim = 128
    widths = [head_dim * len(js) for _, js in groups]

    def kernel(at_ref, w_ref, *out_refs):
        for (index, js), ref in zip(groups, out_refs):
            cols = pl.ds(pl.multiple_of(at_ref[index] * head_dim, 128), head_dim)
            for i, j in enumerate(js):
                ref[:, i * head_dim : (i + 1) * head_dim] = w_ref[j, :, cols]

    return pl.pallas_call(
        kernel,
        in_specs=[pl.BlockSpec(memory_space=pltpu.SMEM), pl.BlockSpec()],
        out_specs=[pl.BlockSpec()] * len(groups),
        out_shape=[jax.ShapeDtypeStruct((rows, n), jnp.bfloat16) for n in widths],
        compiler_params=pltpu.CompilerParams(vmem_limit_bytes=24 << 20),
        cost_estimate=cost,
        name="cut_heads",
    )(at, w)


def see(at, lists, tile_dev):
    def kernel(at_ref, lists_ref, o_ref):
        lists = lists_ref[...]
        z = at_ref[0]
        lane = lax.broadcasted_iota(jnp.int32, o_ref.shape, 1)
        out = jnp.full(o_ref.shape, HIDDEN, jnp.float32)
        for c, column in enumerate((z, z ^ 1, jnp.where(z < 2, 2, 1))):
            for t in range(tile_dev):
                hit = (lists == column * tile_dev + t).astype(jnp.float32)
                listed = jnp.max(hit, axis=1, keepdims=True) > 0.0
                out = jnp.where((lane == c * tile_dev + t) & listed, 0.0, out)
        o_ref[...] = out

    return pl.pallas_call(
        kernel,
        in_specs=[pl.BlockSpec(memory_space=pltpu.SMEM), pl.BlockSpec()],
        out_specs=pl.BlockSpec(),
        out_shape=jax.ShapeDtypeStruct((lists.shape[0], 128), jnp.float32),
        cost_estimate=COST,
        name="see",
    )(at, lists)


def project(at, head_index, first, own_x, quarters, weights, bias, gain, norms, cost=COST):
    rows, cols = weights[0].shape
    head_dim = gain.shape[1]
    sources = [own_x] if quarters is None else [part for _, _, part in quarters]
    tokens = own_x.shape[0] if quarters is None else sum(part.shape[0] for part in sources)
    width = sources[0].shape[1]
    step = 256

    def kernel(at_ref, *refs):
        x_refs, weight_refs = refs[: len(sources)], refs[len(sources) : len(sources) + 4]
        b_ref, g_ref, out_ref = refs[len(sources) + 4 :]
        z, q = at_ref[0], at_ref[1]
        here = pl.ds(pl.multiple_of(at_ref[head_index] * head_dim, 128), head_dim)

        def piece(ref, to_row):
            total = None
            for s in range(4):
                cut = pl.multiple_of((z ^ s) * rows, 128)
                part = jnp.dot(
                    ref[:, pl.ds(cut, rows)],
                    weight_refs[s][...],
                    preferred_element_type=jnp.float32,
                )
                total = part if total is None else total + part
            for i, row in enumerate(norms):
                part = total[:, i * head_dim : (i + 1) * head_dim]
                part = part + b_ref[first + i : first + i + 1, here]
                if row is not None:
                    mean = jnp.mean(part * part, axis=-1, keepdims=True)
                    part = part * lax.rsqrt(mean + EPS) * g_ref[row : row + 1, :]
                out_ref[pl.ds(to_row, ref.shape[0]), i * head_dim : (i + 1) * head_dim] = (
                    part.astype(jnp.bfloat16)
                )

        if quarters is None:
            piece(x_refs[0], 0)
        else:
            for (i, start, _), ref in zip(quarters, x_refs):
                piece(ref, pl.multiple_of((q ^ i) * (tokens // 4) + start, 64))

    smem = pl.BlockSpec(memory_space=pltpu.SMEM)
    if quarters is None:
        grid = (tokens // step,)
        fixed = lambda shape: pl.BlockSpec(shape, lambda i: (0,) * len(shape))
        x_specs = [pl.BlockSpec((step, width), lambda i: (i, 0))]
        out_spec = pl.BlockSpec((step, cols), lambda i: (i, 0))
    else:
        grid = ()
        fixed = lambda shape: pl.BlockSpec()
        x_specs = [pl.BlockSpec()] * len(sources)
        out_spec = pl.BlockSpec()
    return pl.pallas_call(
        kernel,
        grid=grid,
        in_specs=[smem, *x_specs, *(fixed(w.shape) for w in weights), fixed(bias.shape), fixed(gain.shape)],
        out_specs=out_spec,
        out_shape=jax.ShapeDtypeStruct((tokens, cols), jnp.bfloat16),
        compiler_params=pltpu.CompilerParams(vmem_limit_bytes=40 << 20),
        cost_estimate=cost,
        name="project",
    )(at, *sources, *weights, bias, gain)


def tile_step(query, rows_ref, at, tile, head_dim, limit, total, mixed):
    scale = math.log2(math.e) / math.sqrt(head_dim)
    keys = rows_ref[at : at + tile, :head_dim]
    values = rows_ref[at : at + tile, head_dim:]
    scores = lax.dot_general(
        query, keys, (((1,), (1,)), ((), ())), preferred_element_type=jnp.float32
    )
    weights = jnp.exp2(scores * scale + limit)
    for c in range(tile // 128):
        total = total + weights[:, c * 128 : (c + 1) * 128]
    mixed = mixed + jnp.dot(
        weights.astype(jnp.bfloat16), values, preferred_element_type=jnp.float32
    )
    return total, mixed


def attend_pair(place, limits, queries, rows):
    tokens, head_dim = queries[0].shape
    tiles = limits[0].shape[0]
    tile = tokens // tiles

    def kernel(place_ref, limit0_ref, limit1_ref, q0_ref, q1_ref, rows0_ref, rows1_ref, done_ref, mixed_ref, total_ref):
        is_mid = (place_ref[0] == 1) | (place_ref[0] == 2)
        for column, q_ref in enumerate((q0_ref, q1_ref)):
            for i in range(tiles):
                here = slice(i * tile, (i + 1) * tile)
                query = q_ref[here, :]
                total = jnp.zeros((tile, 128), jnp.float32)
                mixed = jnp.zeros((tile, head_dim), jnp.float32)
                for side, ref in enumerate((rows0_ref, rows1_ref)):
                    for t in range(tiles):
                        limit = (limit0_ref, limit1_ref)[column][i, (side ^ column) * tiles + t]
                        total, mixed = tile_step(
                            query, ref, t * tile, tile, head_dim, limit, total, mixed
                        )
                is_edge = is_mid if column == 0 else jnp.logical_not(is_mid)

                @pl.when(is_edge)
                def _():
                    mixed_ref[here, :] = mixed
                    total_ref[here, :] = total

                @pl.when(jnp.logical_not(is_edge))
                def _():
                    done_ref[here, :] = (mixed / jnp.sum(total, axis=-1, keepdims=True)).astype(
                        jnp.bfloat16
                    )

    vmem = pl.BlockSpec()
    smem = pl.BlockSpec(memory_space=pltpu.SMEM)
    return pl.pallas_call(
        kernel,
        in_specs=[smem, smem, smem] + [vmem] * 4,
        out_specs=[vmem] * 3,
        out_shape=[
            jax.ShapeDtypeStruct((tokens, head_dim), jnp.bfloat16),
            jax.ShapeDtypeStruct((tokens, head_dim), jnp.float32),
            jax.ShapeDtypeStruct((tokens, 128), jnp.float32),
        ],
        compiler_params=pltpu.CompilerParams(vmem_limit_bytes=40 << 20),
        cost_estimate=COST,
        name="attend_pair",
    )(place, *limits, *queries, *rows)


def attend_halo(place, limits, queries, halo, done, mixed, total):
    tokens, head_dim = queries[0].shape
    tiles = limits[0].shape[0]
    tile = tokens // tiles

    def kernel(place_ref, limit0_ref, limit1_ref, q0_ref, q1_ref, halo_ref, done_ref, mixed_ref, total_ref, keep_ref, send_ref):
        is_mid = (place_ref[0] == 1) | (place_ref[0] == 2)
        for i in range(tiles):
            here = slice(i * tile, (i + 1) * tile)
            query = jnp.where(is_mid, q0_ref[here, :], q1_ref[here, :])
            sums, rows = total_ref[here, :], mixed_ref[here, :]
            for t in range(tiles):
                limit = jnp.where(is_mid, limit0_ref[i, 2 * tiles + t], limit1_ref[i, 2 * tiles + t])
                sums, rows = tile_step(query, halo_ref, t * tile, tile, head_dim, limit, sums, rows)
            edge = (rows / jnp.sum(sums, axis=-1, keepdims=True)).astype(jnp.bfloat16)
            outer = done_ref[here, :]
            keep_ref[here, :] = jnp.where(is_mid, edge, outer)
            send_ref[here, :] = jnp.where(is_mid, outer, edge)

    vmem = pl.BlockSpec()
    smem = pl.BlockSpec(memory_space=pltpu.SMEM)
    out = jax.ShapeDtypeStruct((tokens, head_dim), jnp.bfloat16)
    return pl.pallas_call(
        kernel,
        in_specs=[smem, smem, smem] + [vmem] * 6,
        out_specs=[vmem, vmem],
        out_shape=[out, out],
        compiler_params=pltpu.CompilerParams(vmem_limit_bytes=40 << 20),
        cost_estimate=COST,
        name="attend_halo",
    )(place, *limits, *queries, halo, done, mixed, total)


def assemble(at, parts):
    indices, arrays = zip(*parts)
    tokens, head_dim = arrays[0].shape

    def kernel(at_ref, *refs):
        for index, ref in zip(indices, refs):
            cols = pl.ds(pl.multiple_of(at_ref[index] * head_dim, 128), head_dim)
            refs[-1][:, cols] = ref[...]

    return pl.pallas_call(
        kernel,
        in_specs=[pl.BlockSpec(memory_space=pltpu.SMEM)] + [pl.BlockSpec()] * len(arrays),
        out_specs=pl.BlockSpec(),
        out_shape=jax.ShapeDtypeStruct((tokens, head_dim * len(arrays)), jnp.bfloat16),
        cost_estimate=COST,
        name="assemble",
    )(at, *arrays)


def per_device(frames, modulation, w_qkv, b_qkv, qk_gain, block_lists):
    sizes = tuple(lax.axis_size(a) for a in ("groups", "seq", "fsdp", "head"))
    head_dim = qk_gain.shape[1]
    width_cols = w_qkv.shape[2]
    tokens = frames.shape[0]
    if sizes != (2, 4, 2, 2) or width_cols != 4 * head_dim:
        return general(frames, modulation, w_qkv, b_qkv, qk_gain, block_lists)

    y, z, x, core = (lax.axis_index(a).astype(jnp.int32) for a in ("groups", "seq", "fsdp", "head"))
    rows = w_qkv.shape[0]
    quarter = tokens // 4
    tile_dev = block_lists.shape[0]

    def to(axis, value, bit):
        return lax.ppermute(value, axis, [(i, i ^ bit) for i in range(lax.axis_size(axis))])

    side = z % 2
    mine, twin = 2 * side + y, 2 * side + 1 - y
    across = 2 * (1 - side)
    at = jnp.stack([z, 2 * x + core, mine, twin, across + y, across + 1 - y])
    MINE, TWIN, CROSS, CROSS_TWIN = 2, 3, 4, 5
    KV, Q = (1, 2), (0,)
    NORMS = {KV: (1, None), Q: (0,)}
    is_mid = (z == 1) | (z == 2)
    w = jnp.transpose(w_qkv, (1, 0, 2))
    line = Line()

    cutting = (0, 2 * quarter // 3, quarter)
    raws = [
        lax.dynamic_slice(frames, (at[1] * quarter + lo, 0), (hi - lo, frames.shape[1]))
        for lo, hi in zip(cutting, cutting[1:])
    ]
    raws_other = [to("seq", raw, 1) for raw in raws]
    w, *_ = lax.optimization_barrier((w, *raws))
    cuts = cut_heads(at, w, [(MINE, KV), (CROSS, KV), (MINE, Q), (CROSS, Q)], LONG)
    cuts = line.reached(*cuts)
    own_w = {(MINE, KV): cuts[0], (MINE, Q): cuts[2]}
    got = {}
    for part, same, cross in ((KV, *cuts[:2]), (Q, *cuts[2:])):
        got[part] = [to("seq", same[0], 2), to("seq", cross[0], 3), to("seq", cross[0], 1)]
    own_limit = line.reached(see(at, block_lists, tile_dev))
    far_limit = to("seq", own_limit[0][0], 1)
    frames, modulation = line.after(frames, modulation)
    own_x = line.reached(normalize(frames, modulation, 128, MIDDLE))
    line.drop(cuts[1], cuts[3])
    (w,) = line.after(w)
    for key, box in zip(((TWIN, KV), (TWIN, Q)), line.reached(*cut_heads(at, w, [(TWIN, KV), (TWIN, Q)]))):
        own_w[key] = box

    def arrive(value):
        box = line.reached(value)[0]
        (box[0],) = line.after(box[0])
        return box

    def take(i):
        (raw,) = line.after(raws_other[i])
        near = line.reached(normalize(raw, modulation, 64))[0]
        return near, to("head", near[0], 1), to("fsdp", near[0], 1)

    def swap(part, which, kept, back):
        kept[which] = arrive(got[part][which])
        back[which] = to("groups", kept[which][0], 1)

    def run(head, part, boxes, own, cost=COST):
        (own_part,) = line.after(own_w[head, part][0])
        own_w[head, part][0] = own_part
        two, three, one = (box[0] for box in boxes)
        return line.reached(
            project(
                at, head, part[0], own_x[0][0] if own else None,
                None if own else [(i, start, box[0]) for i, start, box in quarters],
                [own_part, one, two, three], b_qkv, qk_gain, NORMS[part], cost,
            )
        )

    def send_edge(rows):
        return to("seq", jnp.where(is_mid, rows[0][0], rows[1][0]), 2)

    kv_boxes, kv_back, q_boxes, q_back = ([None] * 3 for _ in range(4))
    near0, near_c0, far0 = take(0)
    swap(KV, 0, kv_boxes, kv_back)
    near1, near_c1, far1 = take(1)
    swap(KV, 1, kv_boxes, kv_back)
    swap(KV, 2, kv_boxes, kv_back)
    limits = own_limit + [arrive(far_limit)]
    far0 = arrive(far0)
    far_c0 = to("head", far0[0], 1)
    far1 = arrive(far1)
    far_c1 = to("head", far1[0], 1)
    for which in range(3):
        swap(Q, which, q_boxes, q_back)
    rows_mine = run(MINE, KV, kv_boxes, True, LONG)
    kv_twin = line.reached(*kv_back)
    rows_twin = run(TWIN, KV, kv_twin, True, LONG)
    near_c0, far_c0, near_c1, far_c1 = line.reached(near_c0, far_c0, near_c1, far_c1)
    quarters = [(0, 0, near0), (1, 0, near_c0), (2, 0, far0), (3, 0, far_c0)]
    quarters += [(i, cutting[1], box) for i, box in enumerate((near1, near_c1, far1, far_c1))]
    rows_mine += run(MINE, KV, kv_boxes, False)
    halo_mine = send_edge(rows_mine)
    rows_twin += run(TWIN, KV, kv_twin, False)
    halo_twin = send_edge(rows_twin)
    line.drop(*kv_boxes, *kv_twin)
    q_mine = run(MINE, Q, q_boxes, True)
    q_mine += run(MINE, Q, q_boxes, False)
    line.drop(*q_boxes)

    def pair(q, rows):
        parts = attend_pair(at, [b[0] for b in limits], [b[0] for b in q], [b[0] for b in rows])
        return line.reached(*parts)

    def finish(q, halo, parts):
        keep, send = attend_halo(
            at, [b[0] for b in limits], [b[0] for b in q], halo, *(b[0] for b in parts)
        )
        return line.reached(keep)[0], to("seq", send, 1)

    parts_mine = pair(q_mine, rows_mine)
    q_twin_w = line.reached(*q_back)
    q_twin = run(TWIN, Q, q_twin_w, True)
    q_twin += run(TWIN, Q, q_twin_w, False)
    line.drop(*q_twin_w, *own_x, *(box for *_, box in quarters), *rows_mine)
    (halo_mine,) = line.after(halo_mine)
    keep_mine, back_mine = finish(q_mine, halo_mine, parts_mine)
    line.drop(*q_mine, *parts_mine)
    q_twin[0][0], q_twin[1][0] = line.after(q_twin[0][0], q_twin[1][0])
    parts_twin = pair(q_twin, rows_twin)
    (halo_twin,) = line.after(halo_twin)
    keep_twin, back_twin = finish(q_twin, halo_twin, parts_twin)
    parts = [(MINE, keep_mine[0]), (TWIN, keep_twin[0]), (CROSS, back_mine), (CROSS_TWIN, back_twin)]
    return assemble(at, parts)


def solution(mesh):
    placed = (
        P(("groups", "seq"), None),
        P("groups", None),
        P("seq", None, ("fsdp", "head")),
        P(None, ("fsdp", "head")),
        P(),
        P(("groups", "seq"), None),
    )
    return jax.shard_map(
        per_device,
        mesh=mesh,
        in_specs=placed,
        out_specs=P(("groups", "seq"), ("fsdp", "head")),
        check_vma=False,
    )
```

```python
import math

import jax
import jax.numpy as jnp
from jax import lax
from jax.experimental import pallas as pl
from jax.experimental.pallas import tpu as pltpu
from jax.sharding import PartitionSpec as P

EPS = 1e-06
HIDDEN = -1e30
COST = pl.CostEstimate(flops=1 << 20, bytes_accessed=1 << 10, transcendentals=0)
SPACE = pl.CostEstimate(flops=1 << 34, bytes_accessed=1 << 10, transcendentals=0)
SPACE1 = pl.CostEstimate(flops=1 << 32, bytes_accessed=1 << 10, transcendentals=0)
SPACE2 = pl.CostEstimate(flops=1 << 32, bytes_accessed=1 << 10, transcendentals=0)
LONG = pl.CostEstimate(flops=1 << 37, bytes_accessed=1 << 10, transcendentals=0)


def with_halo(shard, sides, width):
    for axis, dim in sides:
        devices, length = (lax.axis_size(axis), shard.shape[dim])
        up = [(i, (i + 1) % devices) for i in range(devices - 1)]
        down = [(j, i) for i, j in up]
        last = lax.slice_in_dim(shard, length - width, length, axis=dim)
        first = lax.slice_in_dim(shard, 0, width, axis=dim)
        before = lax.ppermute(last, axis, up)
        after = lax.ppermute(first, axis, down)
        shard = jnp.concatenate([before, shard, after], axis=dim)
    return shard


def normed_heads(tensor, gain_row, head_dim):
    shaped = tensor.reshape(tensor.shape[0], tensor.shape[1] // head_dim, head_dim)
    scaled = (
        shaped * lax.rsqrt(jnp.mean(shaped * shaped, axis=-1, keepdims=True) + EPS) * gain_row
    )
    return scaled.astype(jnp.bfloat16)


def visible_tiles(block_lists):
    position = lax.axis_index("seq")
    tile_dev = block_lists.shape[0]
    candidates = (position - 1) * tile_dev + jnp.arange(3 * tile_dev, dtype=jnp.int32)
    matches = (block_lists[:, :, None] == candidates[None, None, :]) & (
        block_lists[:, :, None] >= 0
    )
    return jnp.any(matches, axis=1)


def general(frames, modulation, w_qkv, b_qkv, qk_gain, block_lists):
    inputs = frames.astype(jnp.float32)
    average = jnp.mean(inputs, axis=-1, keepdims=True)
    centred = inputs - average
    variance = jnp.mean(centred * centred, axis=-1, keepdims=True)
    normed = centred * lax.rsqrt(variance + EPS) * (1.0 + modulation[0]) + modulation[1]
    normed = normed.astype(jnp.bfloat16)
    tokens = normed.shape[0]
    width_cols = w_qkv.shape[2]
    head_dim = qk_gain.shape[1]
    heads = width_cols // head_dim
    projected = jnp.einsum(
        "td,djc->tjc",
        normed,
        lax.all_gather(w_qkv, "seq", axis=0, tiled=True),
        preferred_element_type=jnp.float32,
    )
    projected = projected + b_qkv
    queries = normed_heads(projected[:, 0], qk_gain[0], head_dim)
    key_rows = normed_heads(projected[:, 1], qk_gain[1], head_dim)
    values = projected[:, 2].astype(jnp.bfloat16).reshape(tokens, heads, head_dim)
    stacked = jnp.stack([key_rows, values], axis=0)
    neighbourhood = with_halo(stacked, (("seq", 1),), tokens)
    tile_len = tokens // block_lists.shape[0]
    allowed_keys = jnp.repeat(
        jnp.repeat(visible_tiles(block_lists), tile_len, axis=0), tile_len, axis=1
    )
    factor = 1.0 / math.sqrt(head_dim)
    scores = (
        jnp.einsum("qhd,khd->hqk", queries, neighbourhood[0], preferred_element_type=jnp.float32)
        * factor
    )
    weights = jnp.where(allowed_keys[None, :, :], jnp.exp(scores), 0.0)
    totals = jnp.sum(weights, axis=-1)
    mixture = jnp.einsum(
        "hqk,khd->qhd",
        weights.astype(jnp.bfloat16),
        neighbourhood[1],
        preferred_element_type=jnp.float32,
    )
    result = (mixture / jnp.transpose(totals)[:, :, None]).astype(jnp.bfloat16)
    return result.reshape(tokens, width_cols)


class Line:
    def __init__(self):
        self.held = []

    def reached(self, *values):
        boxes = [[v] for v in values]
        self.held += boxes
        return boxes

    def after(self, *values):
        out = lax.optimization_barrier((*values, *(box[0] for box in self.held)))
        for box, value in zip(self.held, out[len(values) :]):
            box[0] = value
        return out[: len(values)]

    def drop(self, *boxes):
        self.held = [box for box in self.held if all(box is not b for b in boxes)]
        return [box[0] for box in boxes]


def norm_kernel(x_ref, mod_ref, o_ref):
    x = x_ref[...].astype(jnp.float32)
    centred = x - jnp.mean(x, axis=-1, keepdims=True)
    variance = jnp.mean(centred * centred, axis=-1, keepdims=True)
    scaled = centred * lax.rsqrt(variance + EPS) * (1.0 + mod_ref[0:1, :]) + mod_ref[1:2, :]
    o_ref[...] = scaled.astype(jnp.bfloat16)


def normalize(frames, modulation, rows, cost=COST):
    tokens, width = frames.shape
    return pl.pallas_call(
        norm_kernel,
        grid=(tokens // rows,),
        in_specs=[
            pl.BlockSpec((rows, width), lambda i: (i, 0)),
            pl.BlockSpec((2, width), lambda i: (0, 0)),
        ],
        out_specs=pl.BlockSpec((rows, width), lambda i: (i, 0)),
        out_shape=jax.ShapeDtypeStruct((tokens, width), jnp.bfloat16),
        cost_estimate=cost,
        name="normalize",
    )(frames, modulation)


def cut_heads(at, w, groups, cost=COST):
    rows = w.shape[1]
    head_dim = 128
    widths = [head_dim * len(js) for _, js in groups]

    def kernel(at_ref, w_ref, *out_refs):
        for (index, js), ref in zip(groups, out_refs):
            cols = pl.ds(pl.multiple_of(at_ref[index] * head_dim, 128), head_dim)
            for i, j in enumerate(js):
                ref[:, i * head_dim : (i + 1) * head_dim] = w_ref[j, :, cols]

    return pl.pallas_call(
        kernel,
        in_specs=[pl.BlockSpec(memory_space=pltpu.SMEM), pl.BlockSpec()],
        out_specs=[pl.BlockSpec()] * len(groups),
        out_shape=[jax.ShapeDtypeStruct((rows, n), jnp.bfloat16) for n in widths],
        compiler_params=pltpu.CompilerParams(vmem_limit_bytes=24 << 20),
        cost_estimate=cost,
        name="cut_heads",
    )(at, w)


def see(at, lists, tile_dev):
    def kernel(at_ref, lists_ref, o_ref):
        lists = lists_ref[...]
        z = at_ref[0]
        lane = lax.broadcasted_iota(jnp.int32, o_ref.shape, 1)
        out = jnp.full(o_ref.shape, HIDDEN, jnp.float32)
        for c, column in enumerate((z, z ^ 1, jnp.where(z < 2, 2, 1))):
            for t in range(tile_dev):
                hit = (lists == column * tile_dev + t).astype(jnp.float32)
                listed = jnp.max(hit, axis=1, keepdims=True) > 0.0
                out = jnp.where((lane == c * tile_dev + t) & listed, 0.0, out)
        o_ref[...] = out

    return pl.pallas_call(
        kernel,
        in_specs=[pl.BlockSpec(memory_space=pltpu.SMEM), pl.BlockSpec()],
        out_specs=pl.BlockSpec(),
        out_shape=jax.ShapeDtypeStruct((lists.shape[0], 128), jnp.float32),
        cost_estimate=COST,
        name="see",
    )(at, lists)


def project(at, part, source, pieces, weights, bias, gain, norms, cost=COST):
    rows, cols = weights[0][0].shape
    head_dim = gain.shape[1]
    sources = [source] if pieces is None else [piece for _, _, piece in pieces]
    tokens = sum(piece.shape[0] for piece in sources)
    width = sources[0].shape[1]
    count = len(sources)
    step = 256
    join = cols < 256

    def kernel(at_ref, *refs):
        x_refs, flat = refs[:count], refs[count : count + 8]
        weight_refs = (flat[:4], flat[4:])
        b_ref, g_ref, *out_refs = refs[count + 8 : count + 12]
        z, q = at_ref[0], at_ref[1]

        def block(ref, row, to_row):
            totals = [None, None]
            for s in range(4):
                cut = pl.multiple_of((z ^ s) * rows, 128)
                x = ref[pl.ds(row, step), pl.ds(cut, rows)]
                if join:
                    w = jnp.concatenate([weight_refs[0][s][...], weight_refs[1][s][...]], axis=1)
                    both = jnp.dot(x, w, preferred_element_type=jnp.float32)
                    parts = [both[:, :cols], both[:, cols:]]
                else:
                    parts = [
                        jnp.dot(x, w[s][...], preferred_element_type=jnp.float32)
                        for w in weight_refs
                    ]
                totals = [p if t is None else t + p for t, p in zip(totals, parts)]
            for h, (total, out_ref) in enumerate(zip(totals, out_refs)):
                here = pl.ds(pl.multiple_of(at_ref[2 + h] * head_dim, 128), head_dim)
                for i, norm in enumerate(norms):
                    value = total[:, i * head_dim : (i + 1) * head_dim]
                    value = value + b_ref[part[i] : part[i] + 1, here]
                    if norm is not None:
                        mean = jnp.mean(value * value, axis=-1, keepdims=True)
                        value = value * lax.rsqrt(mean + EPS) * g_ref[norm : norm + 1, :]
                    out_ref[to_row : to_row + step, i * head_dim : (i + 1) * head_dim] = (
                        value.astype(jnp.bfloat16)
                    )

        if pieces is None:
            block(x_refs[0], 0, 0)
        else:
            x_ref, sems = refs[-2:]
            copies = []
            for n, ((i, start, _), ref) in enumerate(zip(pieces, x_refs)):
                row = pl.multiple_of((q ^ i) * (tokens // 4) + start, 32)
                target = x_ref.at[pl.ds(row, ref.shape[0]), :]
                copies.append(pltpu.make_async_copy(ref, target, sems.at[n]))
                copies[-1].start()
            for copy in copies:
                copy.wait()
            for r in range(0, tokens, step):
                block(x_ref, r, r)

    smem = pl.BlockSpec(memory_space=pltpu.SMEM)
    if pieces is None:
        grid = (tokens // step,)
        fixed = lambda shape: pl.BlockSpec(shape, lambda i: (0,) * len(shape))
        x_specs = [pl.BlockSpec((step, width), lambda i: (i, 0))]
        out_spec = pl.BlockSpec((step, cols), lambda i: (i, 0))
        scratch = []
    else:
        grid = ()
        fixed = lambda shape: pl.BlockSpec()
        x_specs = [pl.BlockSpec(memory_space=pl.ANY)] * count
        out_spec = pl.BlockSpec()
        scratch = [pltpu.VMEM((tokens, width), jnp.bfloat16), pltpu.SemaphoreType.DMA((count,))]
    flat = [*weights[0], *weights[1]]
    return pl.pallas_call(
        kernel,
        grid=grid,
        in_specs=[smem, *x_specs, *(fixed(w.shape) for w in flat), fixed(bias.shape), fixed(gain.shape)],
        out_specs=[out_spec] * 2,
        out_shape=[jax.ShapeDtypeStruct((tokens, cols), jnp.bfloat16)] * 2,
        scratch_shapes=scratch,
        compiler_params=pltpu.CompilerParams(vmem_limit_bytes=40 << 20),
        cost_estimate=cost,
        name="project",
    )(at, *sources, *flat, bias, gain)


def tile_step(query, rows_ref, at, tile, head_dim, limit, total, mixed):
    scale = math.log2(math.e) / math.sqrt(head_dim)
    keys = rows_ref[at : at + tile, :head_dim]
    values = rows_ref[at : at + tile, head_dim:]
    scores = lax.dot_general(
        query, keys, (((1,), (1,)), ((), ())), preferred_element_type=jnp.float32
    )
    weights = jnp.exp2(scores * scale + limit)
    for c in range(tile // 128):
        total = total + weights[:, c * 128 : (c + 1) * 128]
    mixed = mixed + jnp.dot(
        weights.astype(jnp.bfloat16), values, preferred_element_type=jnp.float32
    )
    return total, mixed


def attend_pair(place, limits, queries, rows):
    tokens, head_dim = queries[0].shape
    tiles = limits[0].shape[0]
    tile = tokens // tiles

    def kernel(place_ref, limit0_ref, limit1_ref, q0_ref, q1_ref, rows0_ref, rows1_ref, done_ref, mixed_ref, total_ref):
        is_mid = (place_ref[0] == 1) | (place_ref[0] == 2)
        for column, q_ref in enumerate((q0_ref, q1_ref)):
            for i in range(tiles):
                here = slice(i * tile, (i + 1) * tile)
                query = q_ref[here, :]
                total = jnp.zeros((tile, 128), jnp.float32)
                mixed = jnp.zeros((tile, head_dim), jnp.float32)
                for side, ref in enumerate((rows0_ref, rows1_ref)):
                    for t in range(tiles):
                        limit = (limit0_ref, limit1_ref)[column][i, (side ^ column) * tiles + t]
                        total, mixed = tile_step(
                            query, ref, t * tile, tile, head_dim, limit, total, mixed
                        )
                is_edge = is_mid if column == 0 else jnp.logical_not(is_mid)

                @pl.when(is_edge)
                def _():
                    mixed_ref[here, :] = mixed
                    total_ref[here, :] = total

                @pl.when(jnp.logical_not(is_edge))
                def _():
                    done_ref[here, :] = (mixed / jnp.sum(total, axis=-1, keepdims=True)).astype(
                        jnp.bfloat16
                    )

    vmem = pl.BlockSpec()
    smem = pl.BlockSpec(memory_space=pltpu.SMEM)
    return pl.pallas_call(
        kernel,
        in_specs=[smem, smem, smem] + [vmem] * 4,
        out_specs=[vmem] * 3,
        out_shape=[
            jax.ShapeDtypeStruct((tokens, head_dim), jnp.bfloat16),
            jax.ShapeDtypeStruct((tokens, head_dim), jnp.float32),
            jax.ShapeDtypeStruct((tokens, 128), jnp.float32),
        ],
        compiler_params=pltpu.CompilerParams(vmem_limit_bytes=40 << 20),
        cost_estimate=COST,
        name="attend_pair",
    )(place, *limits, *queries, *rows)


def attend_halo(place, limits, queries, halo, done, mixed, total):
    tokens, head_dim = queries[0].shape
    tiles = limits[0].shape[0]
    tile = tokens // tiles

    def kernel(place_ref, limit0_ref, limit1_ref, q0_ref, q1_ref, halo_ref, done_ref, mixed_ref, total_ref, keep_ref, send_ref):
        is_mid = (place_ref[0] == 1) | (place_ref[0] == 2)
        for i in range(tiles):
            here = slice(i * tile, (i + 1) * tile)
            query = jnp.where(is_mid, q0_ref[here, :], q1_ref[here, :])
            sums, rows = total_ref[here, :], mixed_ref[here, :]
            for t in range(tiles):
                limit = jnp.where(is_mid, limit0_ref[i, 2 * tiles + t], limit1_ref[i, 2 * tiles + t])
                sums, rows = tile_step(query, halo_ref, t * tile, tile, head_dim, limit, sums, rows)
            edge = (rows / jnp.sum(sums, axis=-1, keepdims=True)).astype(jnp.bfloat16)
            outer = done_ref[here, :]
            keep_ref[here, :] = jnp.where(is_mid, edge, outer)
            send_ref[here, :] = jnp.where(is_mid, outer, edge)

    vmem = pl.BlockSpec()
    smem = pl.BlockSpec(memory_space=pltpu.SMEM)
    out = jax.ShapeDtypeStruct((tokens, head_dim), jnp.bfloat16)
    return pl.pallas_call(
        kernel,
        in_specs=[smem, smem, smem] + [vmem] * 6,
        out_specs=[vmem, vmem],
        out_shape=[out, out],
        compiler_params=pltpu.CompilerParams(vmem_limit_bytes=40 << 20),
        cost_estimate=COST,
        name="attend_halo",
    )(place, *limits, *queries, halo, done, mixed, total)


def assemble(at, parts):
    indices, arrays = zip(*parts)
    tokens, head_dim = arrays[0].shape

    def kernel(at_ref, *refs):
        for index, ref in zip(indices, refs):
            cols = pl.ds(pl.multiple_of(at_ref[index] * head_dim, 128), head_dim)
            refs[-1][:, cols] = ref[...]

    return pl.pallas_call(
        kernel,
        in_specs=[pl.BlockSpec(memory_space=pltpu.SMEM)] + [pl.BlockSpec()] * len(arrays),
        out_specs=pl.BlockSpec(),
        out_shape=jax.ShapeDtypeStruct((tokens, head_dim * len(arrays)), jnp.bfloat16),
        cost_estimate=COST,
        name="assemble",
    )(at, *arrays)


def per_device(frames, modulation, w_qkv, b_qkv, qk_gain, block_lists):
    sizes = tuple(lax.axis_size(a) for a in ("groups", "seq", "fsdp", "head"))
    head_dim = qk_gain.shape[1]
    width_cols = w_qkv.shape[2]
    tokens = frames.shape[0]
    if sizes != (2, 4, 2, 2) or width_cols != 4 * head_dim:
        return general(frames, modulation, w_qkv, b_qkv, qk_gain, block_lists)

    y, z, x, core = (lax.axis_index(a).astype(jnp.int32) for a in ("groups", "seq", "fsdp", "head"))
    rows = w_qkv.shape[0]
    quarter = tokens // 4
    tile_dev = block_lists.shape[0]

    def to(axis, value, bit):
        return lax.ppermute(value, axis, [(i, i ^ bit) for i in range(lax.axis_size(axis))])

    side = z % 2
    mine, twin = 2 * side + y, 2 * side + 1 - y
    across = 2 * (1 - side)
    at = jnp.stack([z, 2 * x + core, mine, twin, across + y, across + 1 - y])
    MINE, TWIN, CROSS, CROSS_TWIN = 2, 3, 4, 5
    KV, Q = (1, 2), (0,)
    NORMS = {KV: (1, None), Q: (0,)}
    is_mid = (z == 1) | (z == 2)
    w = jnp.transpose(w_qkv, (1, 0, 2))
    line = Line()

    cutting = (0, quarter // 2, quarter)
    raws = [
        lax.dynamic_slice(frames, (at[1] * quarter + lo, 0), (hi - lo, frames.shape[1]))
        for lo, hi in zip(cutting, cutting[1:])
    ]
    raws_other = [to("seq", raw, 1) for raw in raws]
    frames, modulation, *_ = lax.optimization_barrier((frames, modulation, *raws))
    own_x = line.reached(normalize(frames, modulation, 128, LONG))
    (w,) = line.after(w)
    cuts = cut_heads(at, w, [(MINE, KV), (CROSS, KV), (MINE, Q), (CROSS, Q)])
    cuts = line.reached(*cuts)
    own_w = {(MINE, KV): cuts[0], (MINE, Q): cuts[2]}
    got = {}
    for part, same, cross in ((KV, *cuts[:2]), (Q, *cuts[2:])):
        got[part] = [to("seq", same[0], 2), to("seq", cross[0], 3), to("seq", cross[0], 1)]
    (block_lists,) = line.after(block_lists)
    own_limit = line.reached(see(at, block_lists, tile_dev))
    far_limit = to("seq", own_limit[0][0], 1)
    line.drop(cuts[1], cuts[3])

    def arrive(value):
        box = line.reached(value)[0]
        (box[0],) = line.after(box[0])
        return box

    def take(i):
        (raw,) = line.after(raws_other[i])
        near = line.reached(normalize(raw, modulation, 96))[0]
        return near, to("head", near[0], 1), to("fsdp", near[0], 1)

    def swap(part, which, kept, back):
        kept[which] = arrive(got[part][which])
        back[which] = to("groups", kept[which][0], 1)

    def run(part, kept, back, own, cost=COST):
        sets = []
        for head, boxes in ((MINE, kept), (TWIN, back)):
            box = own_w[head, part]
            (box[0],) = line.after(box[0])
            two, three, one = (b[0] for b in boxes)
            sets.append([box[0], one, two, three])
        return line.reached(
            *project(
                at, part, own_x[0][0], None if own else [(i, start, box[0]) for i, start, box in pieces],
                sets, b_qkv, qk_gain, NORMS[part], cost,
            )
        )

    def send_edge(own, far):
        return to("seq", jnp.where(is_mid, own[0], far[0]), 2)

    kv_kept, kv_back, q_kept, q_back = ([None] * 3 for _ in range(4))
    near0, near_c0, far0 = take(0)
    swap(KV, 0, kv_kept, kv_back)
    near1, near_c1, far1 = take(1)
    swap(KV, 1, kv_kept, kv_back)
    kv_back[0] = arrive(kv_back[0])
    swap(KV, 2, kv_kept, kv_back)
    (w,) = line.after(w)
    spaced = line.reached(*cut_heads(at, w, [(TWIN, KV), (TWIN, Q)], SPACE))
    own_w[TWIN, KV], own_w[TWIN, Q] = spaced
    far0 = arrive(far0)
    far_c0 = to("head", far0[0], 1)
    far1 = arrive(far1)
    far_c1 = to("head", far1[0], 1)
    limits = own_limit + [arrive(far_limit)]
    for which in range(3):
        swap(Q, which, q_kept, q_back)
    kv_back[1:] = [arrive(value) for value in kv_back[1:]]
    own_mine, own_twin = run(KV, kv_kept, kv_back, True, SPACE1)
    near_c0, far_c0, near_c1, far_c1 = line.reached(near_c0, far_c0, near_c1, far_c1)
    pieces = [(i, 0, box) for i, box in enumerate((near0, near_c0, far0, far_c0))]
    pieces += [(i, cutting[1], box) for i, box in enumerate((near1, near_c1, far1, far_c1))]
    far_mine, far_twin = run(KV, kv_kept, kv_back, False, SPACE2)
    halo_mine = send_edge(own_mine, far_mine)
    halo_twin = send_edge(own_twin, far_twin)
    line.drop(*kv_kept, *kv_back)
    q_back = line.reached(*q_back)
    q_own = run(Q, q_kept, q_back, True)
    q_far = run(Q, q_kept, q_back, False)
    line.drop(*q_kept, *q_back, *own_x, *(box for *_, box in pieces))

    def pair(h, rows):
        parts = attend_pair(
            at, [b[0] for b in limits], [q_own[h][0], q_far[h][0]], [b[0] for b in rows]
        )
        return line.reached(*parts)

    def finish(h, halo, parts):
        (halo,) = line.after(halo)
        keep, send = attend_halo(
            at, [b[0] for b in limits], [q_own[h][0], q_far[h][0]], halo, *(b[0] for b in parts)
        )
        return line.reached(keep)[0], to("seq", send, 1)

    parts_mine = pair(0, (own_mine, far_mine))
    keep_mine, back_mine = finish(0, halo_mine, parts_mine)
    line.drop(*parts_mine)
    q_own[1][0], q_far[1][0] = line.after(q_own[1][0], q_far[1][0])
    parts_twin = pair(1, (own_twin, far_twin))
    back_mine = arrive(back_mine)
    keep_twin, back_twin = finish(1, halo_twin, parts_twin)
    parts = [(MINE, keep_mine[0]), (TWIN, keep_twin[0]), (CROSS, back_mine[0]), (CROSS_TWIN, back_twin)]
    return assemble(at, parts)


def solution(mesh):
    placed = (
        P(("groups", "seq"), None),
        P("groups", None),
        P("seq", None, ("fsdp", "head")),
        P(None, ("fsdp", "head")),
        P(),
        P(("groups", "seq"), None),
    )
    return jax.shard_map(
        per_device,
        mesh=mesh,
        in_specs=placed,
        out_specs=P(("groups", "seq"), ("fsdp", "head")),
        check_vma=False,
    )
```

```python
import math

import jax
import jax.numpy as jnp
from jax import lax
from jax.experimental import pallas as pl
from jax.experimental.pallas import tpu as pltpu
from jax.sharding import PartitionSpec as P

EPS = 1e-06
VMEM = 60 << 20
HIDDEN = -1e30
COST = pl.CostEstimate(flops=1 << 20, bytes_accessed=1 << 10, transcendentals=0)


def with_halo(shard, sides, width):
    for axis, dim in sides:
        devices, length = (lax.axis_size(axis), shard.shape[dim])
        up = [(i, (i + 1) % devices) for i in range(devices - 1)]
        down = [(j, i) for i, j in up]
        last = lax.slice_in_dim(shard, length - width, length, axis=dim)
        first = lax.slice_in_dim(shard, 0, width, axis=dim)
        before = lax.ppermute(last, axis, up)
        after = lax.ppermute(first, axis, down)
        shard = jnp.concatenate([before, shard, after], axis=dim)
    return shard


def normed_heads(tensor, gain_row, head_dim):
    shaped = tensor.reshape(tensor.shape[0], tensor.shape[1] // head_dim, head_dim)
    scaled = (
        shaped * lax.rsqrt(jnp.mean(shaped * shaped, axis=-1, keepdims=True) + EPS) * gain_row
    )
    return scaled.astype(jnp.bfloat16)


def visible_tiles(block_lists):
    position = lax.axis_index("seq")
    tile_dev = block_lists.shape[0]
    candidates = (position - 1) * tile_dev + jnp.arange(3 * tile_dev, dtype=jnp.int32)
    matches = (block_lists[:, :, None] == candidates[None, None, :]) & (
        block_lists[:, :, None] >= 0
    )
    return jnp.any(matches, axis=1)


def general(frames, modulation, w_qkv, b_qkv, qk_gain, block_lists):
    inputs = frames.astype(jnp.float32)
    average = jnp.mean(inputs, axis=-1, keepdims=True)
    centred = inputs - average
    variance = jnp.mean(centred * centred, axis=-1, keepdims=True)
    normed = centred * lax.rsqrt(variance + EPS) * (1.0 + modulation[0]) + modulation[1]
    normed = normed.astype(jnp.bfloat16)
    tokens = normed.shape[0]
    width_cols = w_qkv.shape[2]
    head_dim = qk_gain.shape[1]
    heads = width_cols // head_dim
    projected = jnp.einsum(
        "td,djc->tjc",
        normed,
        lax.all_gather(w_qkv, "seq", axis=0, tiled=True),
        preferred_element_type=jnp.float32,
    )
    projected = projected + b_qkv
    queries = normed_heads(projected[:, 0], qk_gain[0], head_dim)
    key_rows = normed_heads(projected[:, 1], qk_gain[1], head_dim)
    values = projected[:, 2].astype(jnp.bfloat16).reshape(tokens, heads, head_dim)
    stacked = jnp.stack([key_rows, values], axis=0)
    neighbourhood = with_halo(stacked, (("seq", 1),), tokens)
    tile_len = tokens // block_lists.shape[0]
    allowed_keys = jnp.repeat(
        jnp.repeat(visible_tiles(block_lists), tile_len, axis=0), tile_len, axis=1
    )
    factor = 1.0 / math.sqrt(head_dim)
    scores = (
        jnp.einsum("qhd,khd->hqk", queries, neighbourhood[0], preferred_element_type=jnp.float32)
        * factor
    )
    weights = jnp.where(allowed_keys[None, :, :], jnp.exp(scores), 0.0)
    totals = jnp.sum(weights, axis=-1)
    mixture = jnp.einsum(
        "hqk,khd->qhd",
        weights.astype(jnp.bfloat16),
        neighbourhood[1],
        preferred_element_type=jnp.float32,
    )
    result = (mixture / jnp.transpose(totals)[:, :, None]).astype(jnp.bfloat16)
    return result.reshape(tokens, width_cols)


class Line:
    def __init__(self):
        self.held = []

    def reached(self, *values):
        boxes = [[v] for v in values]
        self.held += boxes
        return boxes

    def after(self, *values):
        out = lax.optimization_barrier((*values, *(box[0] for box in self.held)))
        for box, value in zip(self.held, out[len(values) :]):
            box[0] = value
        return out[: len(values)]

    def drop(self, *boxes):
        self.held = [box for box in self.held if all(box is not b for b in boxes)]
        return [box[0] for box in boxes]


def norm_kernel(x_ref, mod_ref, o_ref):
    x = x_ref[...].astype(jnp.float32)
    centred = x - jnp.mean(x, axis=-1, keepdims=True)
    variance = jnp.mean(centred * centred, axis=-1, keepdims=True)
    scaled = centred * lax.rsqrt(variance + EPS) * (1.0 + mod_ref[0:1, :]) + mod_ref[1:2, :]
    o_ref[...] = scaled.astype(jnp.bfloat16)


def normalize(frames, modulation, rows):
    tokens, width = frames.shape
    return pl.pallas_call(
        norm_kernel,
        grid=(tokens // rows,),
        in_specs=[
            pl.BlockSpec((rows, width), lambda i: (i, 0)),
            pl.BlockSpec((2, width), lambda i: (0, 0)),
        ],
        out_specs=pl.BlockSpec((rows, width), lambda i: (i, 0)),
        out_shape=jax.ShapeDtypeStruct((tokens, width), jnp.bfloat16),
        cost_estimate=COST,
        name="normalize",
    )(frames, modulation)


def cut_heads(at, w):
    rows = w.shape[1]
    head_dim = 128

    def kernel(at_ref, w_ref, *out_refs):
        for j, ref in enumerate(out_refs):
            for target in range(4):
                cols = pl.ds(pl.multiple_of(at_ref[6 + target % 2] * head_dim, 128), head_dim)
                ref[target] = w_ref[j, :, cols]

    return pl.pallas_call(
        kernel,
        in_specs=[pl.BlockSpec(memory_space=pltpu.SMEM), pl.BlockSpec()],
        out_specs=[pl.BlockSpec()] * 3,
        out_shape=[jax.ShapeDtypeStruct((4, rows, head_dim), jnp.bfloat16)] * 3,
        compiler_params=pltpu.CompilerParams(vmem_limit_bytes=VMEM),
        cost_estimate=COST,
        name="cut_heads",
    )(at, w)


def see(at, lists, tile_dev):
    def kernel(at_ref, lists_ref, o_ref):
        lists = lists_ref[...]
        z = at_ref[0]
        lane = lax.broadcasted_iota(jnp.int32, o_ref.shape, 1)
        out = jnp.full(o_ref.shape, HIDDEN, jnp.float32)
        for c, column in enumerate((z, z ^ 1, jnp.where(z < 2, 2, 1))):
            for t in range(tile_dev):
                hit = (lists == column * tile_dev + t).astype(jnp.float32)
                listed = jnp.max(hit, axis=1, keepdims=True) > 0.0
                out = jnp.where((lane == c * tile_dev + t) & listed, 0.0, out)
        o_ref[...] = out

    return pl.pallas_call(
        kernel,
        in_specs=[pl.BlockSpec(memory_space=pltpu.SMEM), pl.BlockSpec()],
        out_specs=pl.BlockSpec(),
        out_shape=jax.ShapeDtypeStruct((lists.shape[0], 128), jnp.float32),
        cost_estimate=COST,
        name="see",
    )(at, lists)


def project(at, head, part, source, pieces, weights, bias, gain):
    shards, rows, head_dim = weights[0].shape
    cols = head_dim * len(part)
    sources = [source] if pieces is None else [piece for _, _, piece in pieces]
    tokens = sum(piece.shape[0] for piece in sources)
    width = sources[0].shape[1]
    count = len(sources)
    step = 256

    def kernel(at_ref, *refs):
        x_refs, weight_refs = refs[:count], refs[count : count + len(part)]
        b_ref, g_ref, out_ref = refs[count + len(part) : count + len(part) + 3]
        here = pl.ds(pl.multiple_of(at_ref[head] * head_dim, 128), head_dim)

        def block(ref, row):
            total = None
            for s in range(shards):
                w = jnp.concatenate([ref[s] for ref in weight_refs], axis=1)
                x = ref[row : row + step, s * rows : (s + 1) * rows]
                product = jnp.dot(x, w, preferred_element_type=jnp.float32)
                total = product if total is None else total + product
            for i, j in enumerate(part):
                value = total[:, i * head_dim : (i + 1) * head_dim] + b_ref[j : j + 1, here]
                if j < 2:
                    mean = jnp.mean(value * value, axis=-1, keepdims=True)
                    value = value * lax.rsqrt(mean + EPS) * g_ref[j : j + 1, :]
                out_ref[row : row + step, i * head_dim : (i + 1) * head_dim] = value.astype(
                    jnp.bfloat16
                )

        if pieces is None:
            block(x_refs[0], 0)
        else:
            x_ref, sems = refs[-2:]
            q = at_ref[1]
            copies = []
            for n, ((i, start, _), ref) in enumerate(zip(pieces, x_refs)):
                row = pl.multiple_of((q ^ i) * (tokens // 4) + start, 16)
                target = x_ref.at[pl.ds(row, ref.shape[0]), :]
                copies.append(pltpu.make_async_copy(ref, target, sems.at[n]))
                copies[-1].start()
            for copy in copies:
                copy.wait()
            for r in range(0, tokens, step):
                block(x_ref, r)

    smem = pl.BlockSpec(memory_space=pltpu.SMEM)
    if pieces is None:
        grid = (tokens // step,)
        fixed = lambda shape: pl.BlockSpec(shape, lambda i: (0,) * len(shape))
        x_specs = [pl.BlockSpec((step, width), lambda i: (i, 0))]
        out_spec = pl.BlockSpec((step, cols), lambda i: (i, 0))
        scratch = []
    else:
        grid = ()
        fixed = lambda shape: pl.BlockSpec()
        x_specs = [pl.BlockSpec(memory_space=pl.ANY)] * count
        out_spec = pl.BlockSpec()
        scratch = [pltpu.VMEM((tokens, width), jnp.bfloat16), pltpu.SemaphoreType.DMA((count,))]
    return pl.pallas_call(
        kernel,
        grid=grid,
        in_specs=[smem, *x_specs, *(fixed(w.shape) for w in weights), fixed(bias.shape), fixed(gain.shape)],
        out_specs=out_spec,
        out_shape=jax.ShapeDtypeStruct((tokens, cols), jnp.bfloat16),
        scratch_shapes=scratch,
        compiler_params=pltpu.CompilerParams(vmem_limit_bytes=VMEM),
        cost_estimate=COST,
        name="project",
    )(at, *sources, *weights, bias, gain)


def tile_step(query, rows_ref, at, tile, head_dim, limit, total, mixed):
    scale = math.log2(math.e) / math.sqrt(head_dim)
    keys = rows_ref[at : at + tile, :head_dim]
    values = rows_ref[at : at + tile, head_dim:]
    scores = lax.dot_general(
        query, keys, (((1,), (1,)), ((), ())), preferred_element_type=jnp.float32
    )
    weights = jnp.exp2(scores * scale + limit)
    for c in range(tile // 128):
        total = total + weights[:, c * 128 : (c + 1) * 128]
    mixed = mixed + jnp.dot(
        weights.astype(jnp.bfloat16), values, preferred_element_type=jnp.float32
    )
    return total, mixed


def attend_pair(place, limits, queries, rows):
    tokens, head_dim = queries[0].shape
    tiles = limits[0].shape[0]
    tile = tokens // tiles

    def kernel(place_ref, limit0_ref, limit1_ref, q0_ref, q1_ref, rows0_ref, rows1_ref, done_ref, mixed_ref, total_ref):
        is_mid = (place_ref[0] == 1) | (place_ref[0] == 2)
        for column, q_ref in enumerate((q0_ref, q1_ref)):
            for i in range(tiles):
                here = slice(i * tile, (i + 1) * tile)
                query = q_ref[here, :]
                total = jnp.zeros((tile, 128), jnp.float32)
                mixed = jnp.zeros((tile, head_dim), jnp.float32)
                for side, ref in enumerate((rows0_ref, rows1_ref)):
                    for t in range(tiles):
                        limit = (limit0_ref, limit1_ref)[column][i, (side ^ column) * tiles + t]
                        total, mixed = tile_step(
                            query, ref, t * tile, tile, head_dim, limit, total, mixed
                        )
                is_edge = is_mid if column == 0 else jnp.logical_not(is_mid)

                @pl.when(is_edge)
                def _():
                    mixed_ref[here, :] = mixed
                    total_ref[here, :] = total

                @pl.when(jnp.logical_not(is_edge))
                def _():
                    done_ref[here, :] = (mixed / jnp.sum(total, axis=-1, keepdims=True)).astype(
                        jnp.bfloat16
                    )

    vmem = pl.BlockSpec()
    smem = pl.BlockSpec(memory_space=pltpu.SMEM)
    return pl.pallas_call(
        kernel,
        in_specs=[smem, smem, smem] + [vmem] * 4,
        out_specs=[vmem] * 3,
        out_shape=[
            jax.ShapeDtypeStruct((tokens, head_dim), jnp.bfloat16),
            jax.ShapeDtypeStruct((tokens, head_dim), jnp.float32),
            jax.ShapeDtypeStruct((tokens, 128), jnp.float32),
        ],
        compiler_params=pltpu.CompilerParams(vmem_limit_bytes=VMEM),
        cost_estimate=COST,
        name="attend_pair",
    )(place, *limits, *queries, *rows)


def attend_halo(place, limits, queries, halo, done, mixed, total):
    tokens, head_dim = queries[0].shape
    tiles = limits[0].shape[0]
    tile = tokens // tiles

    def kernel(place_ref, limit0_ref, limit1_ref, q0_ref, q1_ref, halo_ref, done_ref, mixed_ref, total_ref, keep_ref, send_ref):
        is_mid = (place_ref[0] == 1) | (place_ref[0] == 2)
        for i in range(tiles):
            here = slice(i * tile, (i + 1) * tile)
            query = jnp.where(is_mid, q0_ref[here, :], q1_ref[here, :])
            sums, rows = total_ref[here, :], mixed_ref[here, :]
            for t in range(tiles):
                limit = jnp.where(is_mid, limit0_ref[i, 2 * tiles + t], limit1_ref[i, 2 * tiles + t])
                sums, rows = tile_step(query, halo_ref, t * tile, tile, head_dim, limit, sums, rows)
            edge = (rows / jnp.sum(sums, axis=-1, keepdims=True)).astype(jnp.bfloat16)
            outer = done_ref[here, :]
            keep_ref[here, :] = jnp.where(is_mid, edge, outer)
            send_ref[here, :] = jnp.where(is_mid, outer, edge)

    vmem = pl.BlockSpec()
    smem = pl.BlockSpec(memory_space=pltpu.SMEM)
    out = jax.ShapeDtypeStruct((tokens, head_dim), jnp.bfloat16)
    return pl.pallas_call(
        kernel,
        in_specs=[smem, smem, smem] + [vmem] * 6,
        out_specs=[vmem, vmem],
        out_shape=[out, out],
        compiler_params=pltpu.CompilerParams(vmem_limit_bytes=VMEM),
        cost_estimate=COST,
        name="attend_halo",
    )(place, *limits, *queries, halo, done, mixed, total)


def assemble(at, parts):
    indices, arrays = zip(*parts)
    tokens, head_dim = arrays[0].shape

    def kernel(at_ref, *refs):
        for index, ref in zip(indices, refs):
            cols = pl.ds(pl.multiple_of(at_ref[index] * head_dim, 128), head_dim)
            refs[-1][:, cols] = ref[...]

    return pl.pallas_call(
        kernel,
        in_specs=[pl.BlockSpec(memory_space=pltpu.SMEM)] + [pl.BlockSpec()] * len(arrays),
        out_specs=pl.BlockSpec(),
        out_shape=jax.ShapeDtypeStruct((tokens, head_dim * len(arrays)), jnp.bfloat16),
        cost_estimate=COST,
        name="assemble",
    )(at, *arrays)


def per_device(frames, modulation, w_qkv, b_qkv, qk_gain, block_lists):
    sizes = tuple(lax.axis_size(a) for a in ("groups", "seq", "fsdp", "head"))
    head_dim = qk_gain.shape[1]
    width_cols = w_qkv.shape[2]
    tokens = frames.shape[0]
    if sizes != (2, 4, 2, 2) or width_cols != 4 * head_dim:
        return general(frames, modulation, w_qkv, b_qkv, qk_gain, block_lists)

    y, z, x, core = (lax.axis_index(a).astype(jnp.int32) for a in ("groups", "seq", "fsdp", "head"))
    rows = w_qkv.shape[0]
    quarter = tokens // 4
    tile_dev = block_lists.shape[0]

    def to(axis, value, bit):
        return lax.ppermute(value, axis, [(i, i ^ bit) for i in range(lax.axis_size(axis))])

    side = z % 2
    mine, twin = 2 * side + y, 2 * side + 1 - y
    across = 2 * (1 - side)
    at = jnp.stack([z, 2 * x + core, mine, twin, across + y, across + 1 - y, y, 2 + y])
    MINE, TWIN, CROSS, CROSS_TWIN = 2, 3, 4, 5
    is_mid = (z == 1) | (z == 2)
    w = jnp.transpose(w_qkv, (1, 0, 2))
    line = Line()

    cutting = (0, quarter * 5 // 12, quarter)
    raws = [
        lax.dynamic_slice(frames, (at[1] * quarter + lo, 0), (hi - lo, frames.shape[1]))
        for lo, hi in zip(cutting, cutting[1:])
    ]
    raws_other = [to("seq", raw, 1) for raw in raws]
    (w, *_) = lax.optimization_barrier((w, *raws))
    cuts = line.reached(*cut_heads(at, w))

    def exchange(value):
        return lax.all_to_all(value, "seq", split_axis=0, concat_axis=0, tiled=True)

    arrived_k = exchange(cuts[1][0])
    own_limit = line.reached(see(at, block_lists, tile_dev))
    far_limit = to("seq", own_limit[0][0], 1)
    frames, modulation = line.after(frames, modulation)
    own_x = line.reached(normalize(frames, modulation, 128))
    line.drop(cuts[1])

    def arrive(value):
        box = line.reached(value)[0]
        (box[0],) = line.after(box[0])
        return box

    def take(i):
        (raw,) = line.after(raws_other[i])
        near = line.reached(normalize(raw, modulation, raw.shape[0]))[0]
        return near, to("head", near[0], 1), to("fsdp", near[0], 1)

    def run(head, part, weights, own):
        return line.reached(
            project(
                at, head, part, own_x[0][0],
                None if own else [(i, start, box[0]) for i, start, box in pieces],
                [box[0] for box in weights], b_qkv, qk_gain,
            )
        )[0]

    def send_edge(own, far):
        return to("seq", jnp.where(is_mid, own[0], far[0]), 2)

    near0, near_c0, far0 = take(0)
    k_mine = arrive(arrived_k)
    k_twin = to("groups", k_mine[0], 1)
    far0 = arrive(far0)
    far_c0 = to("head", far0[0], 1)
    near1, near_c1, far1 = take(1)
    (cuts[2][0],) = line.after(cuts[2][0])
    arrived_v = exchange(cuts[2][0])
    near_c0 = arrive(near_c0)
    k_twin = arrive(k_twin)
    v_mine = arrive(arrived_v)
    v_twin = to("groups", v_mine[0], 1)
    (cuts[0][0],) = line.after(cuts[0][0])
    arrived_q = exchange(cuts[0][0])
    line.drop(cuts[0], cuts[2])
    own_mine = run(MINE, (1, 2), [k_mine, v_mine], True)
    near_c1, far_c0 = arrive(near_c1), arrive(far_c0)
    far1 = arrive(far1)
    far_c1 = to("head", far1[0], 1)
    limits = own_limit + [arrive(far_limit)]
    far_c1 = arrive(far_c1)
    pieces = [(i, 0, box) for i, box in enumerate((near0, near_c0, far0, far_c0))]
    pieces += [(i, cutting[1], box) for i, box in enumerate((near1, near_c1, far1, far_c1))]
    far_mine = run(MINE, (1, 2), [k_mine, v_mine], False)
    halo_mine = send_edge(own_mine, far_mine)
    v_twin = arrive(v_twin)
    far_twin = run(TWIN, (1, 2), [k_twin, v_twin], False)
    own_twin = run(TWIN, (1, 2), [k_twin, v_twin], True)
    halo_twin = send_edge(own_twin, far_twin)
    line.drop(k_mine, v_mine, k_twin, v_twin)
    q_mine = arrive(arrived_q)
    q_twin = to("groups", q_mine[0], 1)
    queries = {0: [run(MINE, (0,), [q_mine], own) for own in (True, False)]}
    line.drop(q_mine)

    def pair(h, rows):
        (queries[h][0][0],) = line.after(queries[h][0][0])
        parts = attend_pair(
            at, [b[0] for b in limits], [b[0] for b in queries[h]], [b[0] for b in rows]
        )
        return line.reached(*parts)

    def finish(h, halo, parts):
        (halo,) = line.after(halo)
        keep, send = attend_halo(
            at, [b[0] for b in limits], [b[0] for b in queries[h]], halo, *(b[0] for b in parts)
        )
        return line.reached(keep)[0], to("seq", send, 1)

    parts_mine = pair(0, (own_mine, far_mine))
    q_twin = arrive(q_twin)
    queries[1] = [run(TWIN, (0,), [q_twin], own) for own in (True, False)]
    line.drop(q_twin, *own_x, *(box for *_, box in pieces))
    keep_mine, back_mine = finish(0, halo_mine, parts_mine)
    line.drop(*parts_mine)
    parts_twin = pair(1, (own_twin, far_twin))
    back_mine = arrive(back_mine)
    keep_twin, back_twin = finish(1, halo_twin, parts_twin)
    parts = [(MINE, keep_mine[0]), (TWIN, keep_twin[0]), (CROSS, back_mine[0]), (CROSS_TWIN, back_twin)]
    return assemble(at, parts)


def solution(mesh):
    placed = (
        P(("groups", "seq"), None),
        P("groups", None),
        P("seq", None, ("fsdp", "head")),
        P(None, ("fsdp", "head")),
        P(),
        P(("groups", "seq"), None),
    )
    return jax.shard_map(
        per_device,
        mesh=mesh,
        in_specs=placed,
        out_specs=P(("groups", "seq"), ("fsdp", "head")),
        check_vma=False,
    )
```

```python
import math

import jax
import jax.numpy as jnp
from jax import lax
from jax.experimental import pallas as pl
from jax.experimental.pallas import tpu as pltpu
from jax.sharding import PartitionSpec as P

EPS = 1e-06
VMEM = 28 << 20
FIRST = 8
HIDDEN = -1e30
SPACE = pl.CostEstimate(flops=1 << 36, bytes_accessed=1 << 10, transcendentals=0)
COST = pl.CostEstimate(flops=1 << 20, bytes_accessed=1 << 10, transcendentals=0)


def with_halo(shard, sides, width):
    for axis, dim in sides:
        devices, length = (lax.axis_size(axis), shard.shape[dim])
        up = [(i, (i + 1) % devices) for i in range(devices - 1)]
        down = [(j, i) for i, j in up]
        last = lax.slice_in_dim(shard, length - width, length, axis=dim)
        first = lax.slice_in_dim(shard, 0, width, axis=dim)
        before = lax.ppermute(last, axis, up)
        after = lax.ppermute(first, axis, down)
        shard = jnp.concatenate([before, shard, after], axis=dim)
    return shard


def normed_heads(tensor, gain_row, head_dim):
    shaped = tensor.reshape(tensor.shape[0], tensor.shape[1] // head_dim, head_dim)
    scaled = (
        shaped * lax.rsqrt(jnp.mean(shaped * shaped, axis=-1, keepdims=True) + EPS) * gain_row
    )
    return scaled.astype(jnp.bfloat16)


def visible_tiles(block_lists):
    position = lax.axis_index("seq")
    tile_dev = block_lists.shape[0]
    candidates = (position - 1) * tile_dev + jnp.arange(3 * tile_dev, dtype=jnp.int32)
    matches = (block_lists[:, :, None] == candidates[None, None, :]) & (
        block_lists[:, :, None] >= 0
    )
    return jnp.any(matches, axis=1)


def general(frames, modulation, w_qkv, b_qkv, qk_gain, block_lists):
    inputs = frames.astype(jnp.float32)
    average = jnp.mean(inputs, axis=-1, keepdims=True)
    centred = inputs - average
    variance = jnp.mean(centred * centred, axis=-1, keepdims=True)
    normed = centred * lax.rsqrt(variance + EPS) * (1.0 + modulation[0]) + modulation[1]
    normed = normed.astype(jnp.bfloat16)
    tokens = normed.shape[0]
    width_cols = w_qkv.shape[2]
    head_dim = qk_gain.shape[1]
    heads = width_cols // head_dim
    projected = jnp.einsum(
        "td,djc->tjc",
        normed,
        lax.all_gather(w_qkv, "seq", axis=0, tiled=True),
        preferred_element_type=jnp.float32,
    )
    projected = projected + b_qkv
    queries = normed_heads(projected[:, 0], qk_gain[0], head_dim)
    key_rows = normed_heads(projected[:, 1], qk_gain[1], head_dim)
    values = projected[:, 2].astype(jnp.bfloat16).reshape(tokens, heads, head_dim)
    stacked = jnp.stack([key_rows, values], axis=0)
    neighbourhood = with_halo(stacked, (("seq", 1),), tokens)
    tile_len = tokens // block_lists.shape[0]
    allowed_keys = jnp.repeat(
        jnp.repeat(visible_tiles(block_lists), tile_len, axis=0), tile_len, axis=1
    )
    factor = 1.0 / math.sqrt(head_dim)
    scores = (
        jnp.einsum("qhd,khd->hqk", queries, neighbourhood[0], preferred_element_type=jnp.float32)
        * factor
    )
    weights = jnp.where(allowed_keys[None, :, :], jnp.exp(scores), 0.0)
    totals = jnp.sum(weights, axis=-1)
    mixture = jnp.einsum(
        "hqk,khd->qhd",
        weights.astype(jnp.bfloat16),
        neighbourhood[1],
        preferred_element_type=jnp.float32,
    )
    result = (mixture / jnp.transpose(totals)[:, :, None]).astype(jnp.bfloat16)
    return result.reshape(tokens, width_cols)


class Line:
    def __init__(self):
        self.held = []

    def reached(self, *values):
        boxes = [[v] for v in values]
        self.held += boxes
        return boxes

    def after(self, *values):
        out = lax.optimization_barrier((*values, *(box[0] for box in self.held)))
        for box, value in zip(self.held, out[len(values) :]):
            box[0] = value
        return out[: len(values)]

    def drop(self, *boxes):
        self.held = [box for box in self.held if all(box is not b for b in boxes)]
        return [box[0] for box in boxes]


def norm_kernel(x_ref, mod_ref, o_ref):
    x = x_ref[...].astype(jnp.float32)
    centred = x - jnp.mean(x, axis=-1, keepdims=True)
    variance = jnp.mean(centred * centred, axis=-1, keepdims=True)
    scaled = centred * lax.rsqrt(variance + EPS) * (1.0 + mod_ref[0:1, :]) + mod_ref[1:2, :]
    o_ref[...] = scaled.astype(jnp.bfloat16)


def normalize(frames, modulation, rows):
    tokens, width = frames.shape
    return pl.pallas_call(
        norm_kernel,
        grid=(tokens // rows,),
        in_specs=[
            pl.BlockSpec((rows, width), lambda i: (i, 0)),
            pl.BlockSpec((2, width), lambda i: (0, 0)),
        ],
        out_specs=pl.BlockSpec((rows, width), lambda i: (i, 0)),
        out_shape=jax.ShapeDtypeStruct((tokens, width), jnp.bfloat16),
        cost_estimate=COST,
        name="normalize",
    )(frames, modulation)


def cut_heads(at, w, groups, cost=None):
    rows = w.shape[1]
    head_dim = 128
    shapes = [(len(indices), rows, head_dim * len(js)) for indices, js in groups]

    def kernel(at_ref, w_ref, *out_refs):
        for (indices, js), ref in zip(groups, out_refs):
            for n, index in enumerate(indices):
                cols = pl.ds(pl.multiple_of(at_ref[index] * head_dim, 128), head_dim)
                for i, j in enumerate(js):
                    ref[n, :, i * head_dim : (i + 1) * head_dim] = w_ref[j, :, cols]

    return pl.pallas_call(
        kernel,
        in_specs=[pl.BlockSpec(memory_space=pltpu.SMEM), pl.BlockSpec()],
        out_specs=[pl.BlockSpec()] * len(groups),
        out_shape=[jax.ShapeDtypeStruct(shape, jnp.bfloat16) for shape in shapes],
        compiler_params=pltpu.CompilerParams(vmem_limit_bytes=VMEM),
        cost_estimate=cost or COST,
        name="cut_heads",
    )(at, w)


def see(at, lists, tile_dev):
    def kernel(at_ref, lists_ref, o_ref):
        lists = lists_ref[...]
        z = at_ref[0]
        lane = lax.broadcasted_iota(jnp.int32, o_ref.shape, 1)
        out = jnp.full(o_ref.shape, HIDDEN, jnp.float32)
        for c, column in enumerate((z, z ^ 1, jnp.where(z < 2, 2, 1))):
            for t in range(tile_dev):
                hit = (lists == column * tile_dev + t).astype(jnp.float32)
                listed = jnp.max(hit, axis=1, keepdims=True) > 0.0
                out = jnp.where((lane == c * tile_dev + t) & listed, 0.0, out)
        o_ref[...] = out

    return pl.pallas_call(
        kernel,
        in_specs=[pl.BlockSpec(memory_space=pltpu.SMEM), pl.BlockSpec()],
        out_specs=pl.BlockSpec(),
        out_shape=jax.ShapeDtypeStruct((lists.shape[0], 128), jnp.float32),
        cost_estimate=COST,
        name="see",
    )(at, lists)


def project(at, part, source, pieces, weights, bias, gain, cost=None):
    *_, rows, cols = weights[0][0].shape
    head_dim = gain.shape[1]
    sources = [source] if pieces is None else [array for array, _ in pieces]
    tokens = sum(piece.shape[0] for piece in sources)
    width = sources[0].shape[1]
    count = len(sources)
    each = len(weights[0])
    step = 256

    def kernel(at_ref, *refs):
        x_refs, flat = refs[:count], refs[count : count + 2 * each]
        weight_refs = (flat[:each], flat[each:])
        b_ref, g_ref, *out_refs = refs[count + 2 * each : count + 2 * each + 4]
        z, q = at_ref[0], at_ref[1]

        def block(ref, row):
            total = None
            for s in range(4):
                if each == 1:
                    w = [refs[0][s] for refs in weight_refs]
                    x = ref[pl.ds(row, step), s * rows : (s + 1) * rows]
                else:
                    w = [refs[s][0] for refs in weight_refs]
                    x = ref[pl.ds(row, step), pl.ds(pl.multiple_of((z ^ s) * rows, 128), rows)]
                product = jnp.dot(
                    x, jnp.concatenate(w, axis=1), preferred_element_type=jnp.float32
                )
                total = product if total is None else total + product
            for h, out_ref in enumerate(out_refs):
                here = pl.ds(pl.multiple_of(at_ref[2 + h] * head_dim, 128), head_dim)
                for i, j in enumerate(part):
                    first = h * cols + i * head_dim
                    value = total[:, first : first + head_dim] + b_ref[j : j + 1, here]
                    if j < 2:
                        mean = jnp.mean(value * value, axis=-1, keepdims=True)
                        value = value * lax.rsqrt(mean + EPS) * g_ref[j : j + 1, :]
                    out_ref[pl.ds(row, step), i * head_dim : (i + 1) * head_dim] = value.astype(
                        jnp.bfloat16
                    )

        if pieces is None:
            block(x_refs[0], 0)
        else:
            x_ref, sems = refs[-2:]
            copies = []
            for (_, parts), ref in zip(pieces, x_refs):
                for i, start, first, size in parts:
                    row = pl.multiple_of((q ^ i) * (tokens // 4) + start, 16)
                    copies.append(
                        pltpu.make_async_copy(
                            ref.at[pl.ds(first, size), :],
                            x_ref.at[pl.ds(row, size), :],
                            sems.at[len(copies)],
                        )
                    )
                    copies[-1].start()
            for copy in copies:
                copy.wait()
            for r in range(0, tokens, step):
                block(x_ref, r)

    smem = pl.BlockSpec(memory_space=pltpu.SMEM)
    if pieces is None:
        grid = (tokens // step,)
        fixed = lambda shape: pl.BlockSpec(shape, lambda i: (0,) * len(shape))
        x_specs = [pl.BlockSpec((step, width), lambda i: (i, 0))]
        out_spec = pl.BlockSpec((step, cols), lambda i: (i, 0))
        scratch = []
    else:
        grid = ()
        fixed = lambda shape: pl.BlockSpec()
        x_specs = [pl.BlockSpec(memory_space=pl.ANY)] * count
        out_spec = pl.BlockSpec()
        copies = sum(len(parts) for _, parts in pieces)
        scratch = [pltpu.VMEM((tokens, width), jnp.bfloat16), pltpu.SemaphoreType.DMA((copies,))]
    flat = [*weights[0], *weights[1]]
    return pl.pallas_call(
        kernel,
        grid=grid,
        in_specs=[smem, *x_specs, *(fixed(w.shape) for w in flat), fixed(bias.shape), fixed(gain.shape)],
        out_specs=[out_spec] * 2,
        out_shape=[jax.ShapeDtypeStruct((tokens, cols), jnp.bfloat16)] * 2,
        scratch_shapes=scratch,
        compiler_params=pltpu.CompilerParams(vmem_limit_bytes=VMEM),
        cost_estimate=cost or COST,
        name="project",
    )(at, *sources, *flat, bias, gain)


def tile_step(query, rows_ref, at, tile, head_dim, limit, total, mixed):
    scale = math.log2(math.e) / math.sqrt(head_dim)
    keys = rows_ref[at : at + tile, :head_dim]
    values = rows_ref[at : at + tile, head_dim:]
    scores = lax.dot_general(
        query, keys, (((1,), (1,)), ((), ())), preferred_element_type=jnp.float32
    )
    weights = jnp.exp2(scores * scale + limit)
    for c in range(tile // 128):
        total = total + weights[:, c * 128 : (c + 1) * 128]
    mixed = mixed + jnp.dot(
        weights.astype(jnp.bfloat16), values, preferred_element_type=jnp.float32
    )
    return total, mixed


def attend_pair(place, limits, queries, rows):
    tokens, head_dim = queries[0].shape
    tiles = limits[0].shape[0]
    tile = tokens // tiles

    def kernel(place_ref, limit0_ref, limit1_ref, q0_ref, q1_ref, rows0_ref, rows1_ref, done_ref, mixed_ref, total_ref):
        is_mid = (place_ref[0] == 1) | (place_ref[0] == 2)
        for column, q_ref in enumerate((q0_ref, q1_ref)):
            for i in range(tiles):
                here = slice(i * tile, (i + 1) * tile)
                query = q_ref[here, :]
                total = jnp.zeros((tile, 128), jnp.float32)
                mixed = jnp.zeros((tile, head_dim), jnp.float32)
                for side, ref in enumerate((rows0_ref, rows1_ref)):
                    for t in range(tiles):
                        limit = (limit0_ref, limit1_ref)[column][i, (side ^ column) * tiles + t]
                        total, mixed = tile_step(
                            query, ref, t * tile, tile, head_dim, limit, total, mixed
                        )
                is_edge = is_mid if column == 0 else jnp.logical_not(is_mid)

                @pl.when(is_edge)
                def _():
                    mixed_ref[here, :] = mixed
                    total_ref[here, :] = total

                @pl.when(jnp.logical_not(is_edge))
                def _():
                    done_ref[here, :] = (mixed / jnp.sum(total, axis=-1, keepdims=True)).astype(
                        jnp.bfloat16
                    )

    vmem = pl.BlockSpec()
    smem = pl.BlockSpec(memory_space=pltpu.SMEM)
    return pl.pallas_call(
        kernel,
        in_specs=[smem, smem, smem] + [vmem] * 4,
        out_specs=[vmem] * 3,
        out_shape=[
            jax.ShapeDtypeStruct((tokens, head_dim), jnp.bfloat16),
            jax.ShapeDtypeStruct((tokens, head_dim), jnp.float32),
            jax.ShapeDtypeStruct((tokens, 128), jnp.float32),
        ],
        compiler_params=pltpu.CompilerParams(vmem_limit_bytes=VMEM),
        cost_estimate=COST,
        name="attend_pair",
    )(place, *limits, *queries, *rows)


def attend_halo(place, limits, queries, halo, done, mixed, total):
    tokens, head_dim = queries[0].shape
    tiles = limits[0].shape[0]
    tile = tokens // tiles

    def kernel(place_ref, limit0_ref, limit1_ref, q0_ref, q1_ref, halo_ref, done_ref, mixed_ref, total_ref, keep_ref, send_ref):
        is_mid = (place_ref[0] == 1) | (place_ref[0] == 2)
        for i in range(tiles):
            here = slice(i * tile, (i + 1) * tile)
            query = jnp.where(is_mid, q0_ref[here, :], q1_ref[here, :])
            sums, rows = total_ref[here, :], mixed_ref[here, :]
            for t in range(tiles):
                limit = jnp.where(is_mid, limit0_ref[i, 2 * tiles + t], limit1_ref[i, 2 * tiles + t])
                sums, rows = tile_step(query, halo_ref, t * tile, tile, head_dim, limit, sums, rows)
            edge = (rows / jnp.sum(sums, axis=-1, keepdims=True)).astype(jnp.bfloat16)
            outer = done_ref[here, :]
            keep_ref[here, :] = jnp.where(is_mid, edge, outer)
            send_ref[here, :] = jnp.where(is_mid, outer, edge)

    vmem = pl.BlockSpec()
    smem = pl.BlockSpec(memory_space=pltpu.SMEM)
    out = jax.ShapeDtypeStruct((tokens, head_dim), jnp.bfloat16)
    return pl.pallas_call(
        kernel,
        in_specs=[smem, smem, smem] + [vmem] * 6,
        out_specs=[vmem, vmem],
        out_shape=[out, out],
        compiler_params=pltpu.CompilerParams(vmem_limit_bytes=VMEM),
        cost_estimate=COST,
        name="attend_halo",
    )(place, *limits, *queries, halo, done, mixed, total)


def assemble(at, parts):
    indices, arrays = zip(*parts)
    tokens, head_dim = arrays[0].shape

    def kernel(at_ref, *refs):
        for index, ref in zip(indices, refs):
            cols = pl.ds(pl.multiple_of(at_ref[index] * head_dim, 128), head_dim)
            refs[-1][:, cols] = ref[...]

    return pl.pallas_call(
        kernel,
        in_specs=[pl.BlockSpec(memory_space=pltpu.SMEM)] + [pl.BlockSpec()] * len(arrays),
        out_specs=pl.BlockSpec(),
        out_shape=jax.ShapeDtypeStruct((tokens, head_dim * len(arrays)), jnp.bfloat16),
        cost_estimate=COST,
        name="assemble",
    )(at, *arrays)


def per_device(frames, modulation, w_qkv, b_qkv, qk_gain, block_lists):
    sizes = tuple(lax.axis_size(a) for a in ("groups", "seq", "fsdp", "head"))
    head_dim = qk_gain.shape[1]
    width_cols = w_qkv.shape[2]
    tokens = frames.shape[0]
    if sizes != (2, 4, 2, 2) or width_cols != 4 * head_dim:
        return general(frames, modulation, w_qkv, b_qkv, qk_gain, block_lists)

    y, z, x, core = (lax.axis_index(a).astype(jnp.int32) for a in ("groups", "seq", "fsdp", "head"))
    rows = w_qkv.shape[0]
    quarter = tokens // 4
    tile_dev = block_lists.shape[0]

    def to(axis, value, bit):
        return lax.ppermute(value, axis, [(i, i ^ bit) for i in range(lax.axis_size(axis))])

    side = z % 2
    mine, twin = 2 * side + y, 2 * side + 1 - y
    across = 2 * (1 - side)
    at = jnp.stack([z, 2 * x + core, mine, twin, across + y, across + 1 - y, y, 2 + y])
    MINE, TWIN, CROSS, CROSS_TWIN = 2, 3, 4, 5
    is_mid = (z == 1) | (z == 2)
    w = jnp.transpose(w_qkv, (1, 0, 2))
    line = Line()

    def arrive(value):
        box = line.reached(value)[0]
        (box[0],) = line.after(box[0])
        return box

    cutting = (0, quarter * FIRST // 12, quarter)
    raws = [
        lax.dynamic_slice(frames, (at[1] * quarter + lo, 0), (hi - lo, frames.shape[1]))
        for lo, hi in zip(cutting, cutting[1:])
    ]
    raws_other = [to("seq", raw, 1) for raw in raws]
    (w, *_) = lax.optimization_barrier((w, *raws))
    same, cross, q_sent = line.reached(
        *cut_heads(at, w, [((MINE,), (1, 2)), ((CROSS,), (1, 2)), ((6, 7, 6, 7), (0,))])
    )
    got = [to("seq", same[0], 2), to("seq", cross[0], 3), to("seq", cross[0], 1)]
    own_limit = line.reached(see(at, block_lists, tile_dev))
    far_limit = to("seq", own_limit[0][0], 1)
    frames, modulation = line.after(frames, modulation)
    own_x = line.reached(normalize(frames, modulation, 128))
    line.drop(cross)

    def take(i):
        (raw,) = line.after(raws_other[i])
        near = line.reached(normalize(raw, modulation, raw.shape[0]))[0]
        return near, to("fsdp", near[0], 1)

    def spread(near, far):
        far = arrive(far)
        both = jnp.concatenate([near[0], far[0]], axis=0)
        return far, to("head", both, 1)

    def swap(which):
        kept = arrive(got[which])
        return kept, to("groups", kept[0], 1)

    def run(part, weights, own, cost=None):
        sets = [[box[0] for box in boxes] for boxes in weights]
        return line.reached(
            *project(
                at, part, own_x[0][0], None if own else [(box[0], parts) for box, parts in pieces],
                sets, b_qkv, qk_gain, cost,
            )
        )

    def send_edge(own, far):
        return to("seq", jnp.where(is_mid, own[0], far[0]), 2)

    near0, far0 = take(0)
    two_mine, two_twin = swap(0)
    near1, far1 = take(1)
    three_mine, three_twin = swap(1)
    (q_sent[0],) = line.after(q_sent[0])
    q_got = lax.all_to_all(q_sent[0], "seq", split_axis=0, concat_axis=0, tiled=True)
    line.drop(q_sent)
    one_mine, one_twin = swap(2)
    (w,) = line.after(w)
    own_kv = [same, line.reached(*cut_heads(at, w, [((TWIN,), (1, 2))], SPACE))[0]]
    far0, core0 = spread(near0, far0)
    two_twin = arrive(two_twin)
    far1, core1 = spread(near1, far1)
    three_twin = arrive(three_twin)
    one_twin = arrive(one_twin)
    kv_w = [[own_kv[0], one_mine, two_mine, three_mine], [own_kv[1], one_twin, two_twin, three_twin]]
    own_mine, own_twin = run((1, 2), kv_w, True, SPACE)
    limits = own_limit + [arrive(far_limit)]
    core0 = arrive(core0)
    q_mine = arrive(q_got)
    q_twin = to("groups", q_mine[0], 1)
    core1 = arrive(core1)
    n0, n1 = cutting[1], quarter - cutting[1]
    pieces = [
        (near0, [(0, 0, 0, n0)]),
        (far0, [(2, 0, 0, n0)]),
        (core0, [(1, 0, 0, n0), (3, 0, n0, n0)]),
        (near1, [(0, n0, 0, n1)]),
        (far1, [(2, n0, 0, n1)]),
        (core1, [(1, n0, 0, n1), (3, n0, n1, n1)]),
    ]
    far_mine, far_twin = run((1, 2), kv_w, False)
    halo_mine = send_edge(own_mine, far_mine)
    halo_twin = send_edge(own_twin, far_twin)
    line.drop(*kv_w[0], *kv_w[1])
    q_twin = arrive(q_twin)
    q_own = run((0,), [[q_mine], [q_twin]], True)
    q_far = run((0,), [[q_mine], [q_twin]], False)
    line.drop(q_mine, q_twin, *own_x, *(box for box, _ in pieces))

    def pair(h, rows):
        (q_own[h][0],) = line.after(q_own[h][0])
        parts = attend_pair(
            at, [b[0] for b in limits], [q_own[h][0], q_far[h][0]], [b[0] for b in rows]
        )
        return line.reached(*parts)

    def finish(h, halo, parts):
        (halo,) = line.after(halo)
        keep, send = attend_halo(
            at, [b[0] for b in limits], [q_own[h][0], q_far[h][0]], halo, *(b[0] for b in parts)
        )
        return line.reached(keep)[0], to("seq", send, 1)

    parts_mine = pair(0, (own_mine, far_mine))
    parts_twin = pair(1, (own_twin, far_twin))
    keep_mine, back_mine = finish(0, halo_mine, parts_mine)
    line.drop(*parts_mine)
    keep_twin, back_twin = finish(1, halo_twin, parts_twin)
    parts = [(MINE, keep_mine[0]), (TWIN, keep_twin[0]), (CROSS, back_mine), (CROSS_TWIN, back_twin)]
    return assemble(at, parts)


def solution(mesh):
    placed = (
        P(("groups", "seq"), None),
        P("groups", None),
        P("seq", None, ("fsdp", "head")),
        P(None, ("fsdp", "head")),
        P(),
        P(("groups", "seq"), None),
    )
    return jax.shard_map(
        per_device,
        mesh=mesh,
        in_specs=placed,
        out_specs=P(("groups", "seq"), ("fsdp", "head")),
        check_vma=False,
    )
```

```python
import math

import jax
import jax.numpy as jnp
from jax import lax
from jax.experimental import pallas as pl
from jax.experimental.pallas import tpu as pltpu
from jax.sharding import PartitionSpec as P

EPS = 1e-06
VMEM = 28 << 20
WHOLE = 60 << 20
FIRST = 8
HIDDEN = -1e30
SPACE = pl.CostEstimate(flops=1 << 36, bytes_accessed=1 << 10, transcendentals=0)
COST = pl.CostEstimate(flops=1 << 20, bytes_accessed=1 << 10, transcendentals=0)


def with_halo(shard, sides, width):
    for axis, dim in sides:
        devices, length = (lax.axis_size(axis), shard.shape[dim])
        up = [(i, (i + 1) % devices) for i in range(devices - 1)]
        down = [(j, i) for i, j in up]
        last = lax.slice_in_dim(shard, length - width, length, axis=dim)
        first = lax.slice_in_dim(shard, 0, width, axis=dim)
        before = lax.ppermute(last, axis, up)
        after = lax.ppermute(first, axis, down)
        shard = jnp.concatenate([before, shard, after], axis=dim)
    return shard


def normed_heads(tensor, gain_row, head_dim):
    shaped = tensor.reshape(tensor.shape[0], tensor.shape[1] // head_dim, head_dim)
    scaled = (
        shaped * lax.rsqrt(jnp.mean(shaped * shaped, axis=-1, keepdims=True) + EPS) * gain_row
    )
    return scaled.astype(jnp.bfloat16)


def visible_tiles(block_lists):
    position = lax.axis_index("seq")
    tile_dev = block_lists.shape[0]
    candidates = (position - 1) * tile_dev + jnp.arange(3 * tile_dev, dtype=jnp.int32)
    matches = (block_lists[:, :, None] == candidates[None, None, :]) & (
        block_lists[:, :, None] >= 0
    )
    return jnp.any(matches, axis=1)


def general(frames, modulation, w_qkv, b_qkv, qk_gain, block_lists):
    inputs = frames.astype(jnp.float32)
    average = jnp.mean(inputs, axis=-1, keepdims=True)
    centred = inputs - average
    variance = jnp.mean(centred * centred, axis=-1, keepdims=True)
    normed = centred * lax.rsqrt(variance + EPS) * (1.0 + modulation[0]) + modulation[1]
    normed = normed.astype(jnp.bfloat16)
    tokens = normed.shape[0]
    width_cols = w_qkv.shape[2]
    head_dim = qk_gain.shape[1]
    heads = width_cols // head_dim
    projected = jnp.einsum(
        "td,djc->tjc",
        normed,
        lax.all_gather(w_qkv, "seq", axis=0, tiled=True),
        preferred_element_type=jnp.float32,
    )
    projected = projected + b_qkv
    queries = normed_heads(projected[:, 0], qk_gain[0], head_dim)
    key_rows = normed_heads(projected[:, 1], qk_gain[1], head_dim)
    values = projected[:, 2].astype(jnp.bfloat16).reshape(tokens, heads, head_dim)
    stacked = jnp.stack([key_rows, values], axis=0)
    neighbourhood = with_halo(stacked, (("seq", 1),), tokens)
    tile_len = tokens // block_lists.shape[0]
    allowed_keys = jnp.repeat(
        jnp.repeat(visible_tiles(block_lists), tile_len, axis=0), tile_len, axis=1
    )
    factor = 1.0 / math.sqrt(head_dim)
    scores = (
        jnp.einsum("qhd,khd->hqk", queries, neighbourhood[0], preferred_element_type=jnp.float32)
        * factor
    )
    weights = jnp.where(allowed_keys[None, :, :], jnp.exp(scores), 0.0)
    totals = jnp.sum(weights, axis=-1)
    mixture = jnp.einsum(
        "hqk,khd->qhd",
        weights.astype(jnp.bfloat16),
        neighbourhood[1],
        preferred_element_type=jnp.float32,
    )
    result = (mixture / jnp.transpose(totals)[:, :, None]).astype(jnp.bfloat16)
    return result.reshape(tokens, width_cols)


class Line:
    def __init__(self):
        self.held = []

    def reached(self, *values):
        boxes = [[v] for v in values]
        self.held += boxes
        return boxes

    def after(self, *values):
        out = lax.optimization_barrier((*values, *(box[0] for box in self.held)))
        for box, value in zip(self.held, out[len(values) :]):
            box[0] = value
        return out[: len(values)]

    def drop(self, *boxes):
        self.held = [box for box in self.held if all(box is not b for b in boxes)]
        return [box[0] for box in boxes]


def norm_kernel(x_ref, mod_ref, o_ref):
    x = x_ref[...].astype(jnp.float32)
    centred = x - jnp.mean(x, axis=-1, keepdims=True)
    variance = jnp.mean(centred * centred, axis=-1, keepdims=True)
    scaled = centred * lax.rsqrt(variance + EPS) * (1.0 + mod_ref[0:1, :]) + mod_ref[1:2, :]
    o_ref[...] = scaled.astype(jnp.bfloat16)


def normalize(frames, modulation, rows):
    tokens, width = frames.shape
    return pl.pallas_call(
        norm_kernel,
        grid=(tokens // rows,),
        in_specs=[
            pl.BlockSpec((rows, width), lambda i: (i, 0)),
            pl.BlockSpec((2, width), lambda i: (0, 0)),
        ],
        out_specs=pl.BlockSpec((rows, width), lambda i: (i, 0)),
        out_shape=jax.ShapeDtypeStruct((tokens, width), jnp.bfloat16),
        cost_estimate=COST,
        name="normalize",
    )(frames, modulation)


def cut_heads(at, w, groups, cost=None):
    rows = w.shape[1]
    head_dim = 128
    shapes = [(len(indices), rows, head_dim * len(js)) for indices, js in groups]

    def kernel(at_ref, w_ref, *out_refs):
        for (indices, js), ref in zip(groups, out_refs):
            for n, index in enumerate(indices):
                cols = pl.ds(pl.multiple_of(at_ref[index] * head_dim, 128), head_dim)
                for i, j in enumerate(js):
                    ref[n, :, i * head_dim : (i + 1) * head_dim] = w_ref[j, :, cols]

    return pl.pallas_call(
        kernel,
        in_specs=[pl.BlockSpec(memory_space=pltpu.SMEM), pl.BlockSpec()],
        out_specs=[pl.BlockSpec()] * len(groups),
        out_shape=[jax.ShapeDtypeStruct(shape, jnp.bfloat16) for shape in shapes],
        compiler_params=pltpu.CompilerParams(vmem_limit_bytes=VMEM),
        cost_estimate=cost or COST,
        name="cut_heads",
    )(at, w)


def see(at, lists, tile_dev):
    def kernel(at_ref, lists_ref, o_ref):
        lists = lists_ref[...]
        z = at_ref[0]
        lane = lax.broadcasted_iota(jnp.int32, o_ref.shape, 1)
        out = jnp.full(o_ref.shape, HIDDEN, jnp.float32)
        for c, column in enumerate((z, z ^ 1, jnp.where(z < 2, 2, 1))):
            for t in range(tile_dev):
                hit = (lists == column * tile_dev + t).astype(jnp.float32)
                listed = jnp.max(hit, axis=1, keepdims=True) > 0.0
                out = jnp.where((lane == c * tile_dev + t) & listed, 0.0, out)
        o_ref[...] = out

    return pl.pallas_call(
        kernel,
        in_specs=[pl.BlockSpec(memory_space=pltpu.SMEM), pl.BlockSpec()],
        out_specs=pl.BlockSpec(),
        out_shape=jax.ShapeDtypeStruct((lists.shape[0], 128), jnp.float32),
        cost_estimate=COST,
        name="see",
    )(at, lists)


def project(at, heads, part, own, pieces, weights, bias, gain, cost=None):
    *_, rows, cols = weights[0][0].shape
    head_dim = gain.shape[1]
    sources = [own] if pieces is None else [array for array, _ in pieces]
    tokens = sum(piece.shape[0] for piece in sources)
    width = sources[0].shape[1]
    count = len(sources)
    each = len(weights[0])
    step = 256
    flat = [array for arrays in weights for array in arrays]
    moves = tokens // step if pieces is None else sum(len(parts) for _, parts in pieces)

    def kernel(at_ref, *refs):
        x_refs, flat_refs = refs[:count], refs[count : count + len(flat)]
        b_ref, g_ref, *out_refs = refs[count + len(flat) : count + len(flat) + 2 + len(heads)]
        x_ref, w_ref, x_sems, w_sems = refs[-4:]
        z, q = at_ref[0], at_ref[1]
        loads = []
        for n, ref in enumerate(flat_refs):
            target = w_ref.at[n // each] if each == 1 else w_ref.at[n // each, pl.ds(n % each, 1)]
            loads.append(pltpu.make_async_copy(ref, target, w_sems.at[n]))
        copies = []
        if pieces is None:
            for r in range(tokens // step):
                at_rows = pl.ds(r * step, step)
                copies.append(
                    pltpu.make_async_copy(x_refs[0].at[at_rows], x_ref.at[at_rows], x_sems.at[r])
                )
        else:
            for (_, parts), ref in zip(pieces, x_refs):
                for i, start, first, size in parts:
                    row = pl.multiple_of((q ^ i) * (tokens // 4) + start, 16)
                    copies.append(
                        pltpu.make_async_copy(
                            ref.at[pl.ds(first, size)],
                            x_ref.at[pl.ds(row, size)],
                            x_sems.at[len(copies)],
                        )
                    )
        for copy in loads + copies:
            copy.start()
        for copy in loads:
            copy.wait()
        if pieces is not None:
            for copy in copies:
                copy.wait()
        for r in range(tokens // step):
            if pieces is None:
                copies[r].wait()
            here = slice(r * step, (r + 1) * step)
            total = None
            for s in range(4):
                first = s * rows if each == 1 else pl.multiple_of((z ^ s) * rows, 128)
                product = jnp.dot(
                    x_ref[here, pl.ds(first, rows)],
                    jnp.concatenate([w_ref[h, s] for h in range(len(heads))], axis=1),
                    preferred_element_type=jnp.float32,
                )
                total = product if total is None else total + product
            for h, (head, out_ref) in enumerate(zip(heads, out_refs)):
                lanes = pl.ds(pl.multiple_of(at_ref[head] * head_dim, 128), head_dim)
                for i, j in enumerate(part):
                    first = h * cols + i * head_dim
                    value = total[:, first : first + head_dim] + b_ref[j : j + 1, lanes]
                    if j < 2:
                        mean = jnp.mean(value * value, axis=-1, keepdims=True)
                        value = value * lax.rsqrt(mean + EPS) * g_ref[j : j + 1, :]
                    out_ref[here, i * head_dim : (i + 1) * head_dim] = value.astype(jnp.bfloat16)

    hbm = pl.BlockSpec(memory_space=pltpu.HBM)
    return pl.pallas_call(
        kernel,
        in_specs=[pl.BlockSpec(memory_space=pltpu.SMEM)]
        + [hbm] * (count + len(flat))
        + [pl.BlockSpec()] * 2,
        out_specs=[pl.BlockSpec()] * len(heads),
        out_shape=[jax.ShapeDtypeStruct((tokens, cols), jnp.bfloat16)] * len(heads),
        scratch_shapes=[
            pltpu.VMEM((tokens, width), jnp.bfloat16),
            pltpu.VMEM((len(heads), 4, rows, cols), jnp.bfloat16),
            pltpu.SemaphoreType.DMA((moves,)),
            pltpu.SemaphoreType.DMA((len(flat),)),
        ],
        compiler_params=pltpu.CompilerParams(vmem_limit_bytes=WHOLE),
        cost_estimate=cost or COST,
        name="project",
    )(at, *sources, *flat, bias, gain)


def take_rows(at, frames, sizes):
    width = frames.shape[1]
    quarter = sum(sizes)

    def kernel(at_ref, x_ref, *out_refs):
        first = 0
        for ref in out_refs:
            ref[...] = x_ref[first : first + ref.shape[0], :]
            first += ref.shape[0]

    return pl.pallas_call(
        kernel,
        grid_spec=pltpu.PrefetchScalarGridSpec(
            num_scalar_prefetch=1,
            grid=(1,),
            in_specs=[pl.BlockSpec((quarter, width), lambda i, at: (at[1], 0))],
            out_specs=[pl.BlockSpec((size, width), lambda i, at: (0, 0)) for size in sizes],
        ),
        out_shape=[jax.ShapeDtypeStruct((size, width), jnp.bfloat16) for size in sizes],
        cost_estimate=COST,
        name="take_rows",
    )(at, frames)


def tile_step(query, rows_ref, at, tile, head_dim, limit, total, mixed):
    scale = math.log2(math.e) / math.sqrt(head_dim)
    keys = rows_ref[at : at + tile, :head_dim]
    values = rows_ref[at : at + tile, head_dim:]
    scores = lax.dot_general(
        query, keys, (((1,), (1,)), ((), ())), preferred_element_type=jnp.float32
    )
    weights = jnp.exp2(scores * scale + limit)
    for c in range(tile // 128):
        total = total + weights[:, c * 128 : (c + 1) * 128]
    mixed = mixed + jnp.dot(
        weights.astype(jnp.bfloat16), values, preferred_element_type=jnp.float32
    )
    return total, mixed


def attend_pair(place, limits, queries, rows):
    tokens, head_dim = queries[0].shape
    tiles = limits[0].shape[0]
    tile = tokens // tiles

    def kernel(place_ref, limit0_ref, limit1_ref, q0_ref, q1_ref, rows0_ref, rows1_ref, done_ref, mixed_ref, total_ref):
        is_mid = (place_ref[0] == 1) | (place_ref[0] == 2)
        for column, q_ref in enumerate((q0_ref, q1_ref)):
            for i in range(tiles):
                here = slice(i * tile, (i + 1) * tile)
                query = q_ref[here, :]
                total = jnp.zeros((tile, 128), jnp.float32)
                mixed = jnp.zeros((tile, head_dim), jnp.float32)
                for side, ref in enumerate((rows0_ref, rows1_ref)):
                    for t in range(tiles):
                        limit = (limit0_ref, limit1_ref)[column][i, (side ^ column) * tiles + t]
                        total, mixed = tile_step(
                            query, ref, t * tile, tile, head_dim, limit, total, mixed
                        )
                is_edge = is_mid if column == 0 else jnp.logical_not(is_mid)

                @pl.when(is_edge)
                def _():
                    mixed_ref[here, :] = mixed
                    total_ref[here, :] = total

                @pl.when(jnp.logical_not(is_edge))
                def _():
                    done_ref[here, :] = (mixed / jnp.sum(total, axis=-1, keepdims=True)).astype(
                        jnp.bfloat16
                    )

    vmem = pl.BlockSpec()
    smem = pl.BlockSpec(memory_space=pltpu.SMEM)
    return pl.pallas_call(
        kernel,
        in_specs=[smem, smem, smem] + [vmem] * 4,
        out_specs=[vmem] * 3,
        out_shape=[
            jax.ShapeDtypeStruct((tokens, head_dim), jnp.bfloat16),
            jax.ShapeDtypeStruct((tokens, head_dim), jnp.float32),
            jax.ShapeDtypeStruct((tokens, 128), jnp.float32),
        ],
        compiler_params=pltpu.CompilerParams(vmem_limit_bytes=VMEM),
        cost_estimate=COST,
        name="attend_pair",
    )(place, *limits, *queries, *rows)


def attend_halo(place, limits, queries, halo, done, mixed, total):
    tokens, head_dim = queries[0].shape
    tiles = limits[0].shape[0]
    tile = tokens // tiles

    def kernel(place_ref, limit0_ref, limit1_ref, q0_ref, q1_ref, halo_ref, done_ref, mixed_ref, total_ref, keep_ref, send_ref):
        is_mid = (place_ref[0] == 1) | (place_ref[0] == 2)
        for i in range(tiles):
            here = slice(i * tile, (i + 1) * tile)
            query = jnp.where(is_mid, q0_ref[here, :], q1_ref[here, :])
            sums, rows = total_ref[here, :], mixed_ref[here, :]
            for t in range(tiles):
                limit = jnp.where(is_mid, limit0_ref[i, 2 * tiles + t], limit1_ref[i, 2 * tiles + t])
                sums, rows = tile_step(query, halo_ref, t * tile, tile, head_dim, limit, sums, rows)
            edge = (rows / jnp.sum(sums, axis=-1, keepdims=True)).astype(jnp.bfloat16)
            outer = done_ref[here, :]
            keep_ref[here, :] = jnp.where(is_mid, edge, outer)
            send_ref[here, :] = jnp.where(is_mid, outer, edge)

    vmem = pl.BlockSpec()
    smem = pl.BlockSpec(memory_space=pltpu.SMEM)
    out = jax.ShapeDtypeStruct((tokens, head_dim), jnp.bfloat16)
    return pl.pallas_call(
        kernel,
        in_specs=[smem, smem, smem] + [vmem] * 6,
        out_specs=[vmem, vmem],
        out_shape=[out, out],
        compiler_params=pltpu.CompilerParams(vmem_limit_bytes=VMEM),
        cost_estimate=COST,
        name="attend_halo",
    )(place, *limits, *queries, halo, done, mixed, total)


def assemble(at, parts):
    indices, arrays = zip(*parts)
    tokens, head_dim = arrays[0].shape

    def kernel(at_ref, *refs):
        for index, ref in zip(indices, refs):
            cols = pl.ds(pl.multiple_of(at_ref[index] * head_dim, 128), head_dim)
            refs[-1][:, cols] = ref[...]

    return pl.pallas_call(
        kernel,
        in_specs=[pl.BlockSpec(memory_space=pltpu.SMEM)] + [pl.BlockSpec()] * len(arrays),
        out_specs=pl.BlockSpec(),
        out_shape=jax.ShapeDtypeStruct((tokens, head_dim * len(arrays)), jnp.bfloat16),
        cost_estimate=COST,
        name="assemble",
    )(at, *arrays)


def per_device(frames, modulation, w_qkv, b_qkv, qk_gain, block_lists):
    sizes = tuple(lax.axis_size(a) for a in ("groups", "seq", "fsdp", "head"))
    head_dim = qk_gain.shape[1]
    width_cols = w_qkv.shape[2]
    tokens = frames.shape[0]
    if sizes != (2, 4, 2, 2) or width_cols != 4 * head_dim:
        return general(frames, modulation, w_qkv, b_qkv, qk_gain, block_lists)

    y, z, x, core = (lax.axis_index(a).astype(jnp.int32) for a in ("groups", "seq", "fsdp", "head"))
    rows = w_qkv.shape[0]
    quarter = tokens // 4
    tile_dev = block_lists.shape[0]

    def to(axis, value, bit):
        return lax.ppermute(value, axis, [(i, i ^ bit) for i in range(lax.axis_size(axis))])

    side = z % 2
    mine, twin = 2 * side + y, 2 * side + 1 - y
    across = 2 * (1 - side)
    at = jnp.stack([z, 2 * x + core, mine, twin, across + y, across + 1 - y, y, 2 + y])
    MINE, TWIN, CROSS, CROSS_TWIN = 2, 3, 4, 5
    is_mid = (z == 1) | (z == 2)
    w = jnp.transpose(w_qkv, (1, 0, 2))
    line = Line()

    def arrive(value):
        box = line.reached(value)[0]
        (box[0],) = line.after(box[0])
        return box

    cutting = (0, quarter * FIRST // 12, quarter)
    raws = take_rows(at, frames, [hi - lo for lo, hi in zip(cutting, cutting[1:])])
    raws_other = [to("seq", raw, 1) for raw in raws]
    (w, *_) = lax.optimization_barrier((w, *raws))
    same, cross, q_sent = line.reached(
        *cut_heads(at, w, [((MINE,), (1, 2)), ((CROSS,), (1, 2)), ((6, 7, 6, 7), (0,))])
    )
    got = [to("seq", same[0], 2), to("seq", cross[0], 3), to("seq", cross[0], 1)]
    own_limit = line.reached(see(at, block_lists, tile_dev))
    far_limit = to("seq", own_limit[0][0], 1)
    frames, modulation = line.after(frames, modulation)
    own_x = line.reached(normalize(frames, modulation, 128))
    line.drop(cross)

    def take(i):
        (raw,) = line.after(raws_other[i])
        near = line.reached(normalize(raw, modulation, raw.shape[0]))[0]
        return near, to("fsdp", near[0], 1)

    def spread(near, far):
        far = arrive(far)
        both = jnp.concatenate([near[0], far[0]], axis=0)
        return far, to("head", both, 1)

    def swap(which):
        kept = arrive(got[which])
        return kept, to("groups", kept[0], 1)

    def run(heads, part, weights, own, cost=None):
        sets = [[box[0] for box in boxes] for boxes in weights]
        return line.reached(
            *project(
                at, heads, part, own_x[0][0], None if own else [(box[0], parts) for box, parts in pieces],
                sets, b_qkv, qk_gain, cost,
            )
        )

    def send_edge(own, far):
        return to("seq", jnp.where(is_mid, own[0], far[0]), 2)

    near0, far0 = take(0)
    two_mine, two_twin = swap(0)
    near1, far1 = take(1)
    (q_sent[0],) = line.after(q_sent[0])
    q_got = lax.all_to_all(q_sent[0], "seq", split_axis=0, concat_axis=0, tiled=True)
    line.drop(q_sent)
    limits = own_limit + [arrive(far_limit)]
    three_mine, three_twin = swap(1)
    one_mine, one_twin = swap(2)
    (w,) = line.after(w)
    own_kv = [same, line.reached(*cut_heads(at, w, [((TWIN,), (1, 2))], SPACE))[0]]
    far0, core0 = spread(near0, far0)
    two_twin = arrive(two_twin)
    three_twin = arrive(three_twin)
    far1, core1 = spread(near1, far1)
    w_mine = [own_kv[0], one_mine, two_mine, three_mine]
    (own_mine,) = run((MINE,), (1, 2), [w_mine], True, SPACE)
    q_mine = arrive(q_got)
    q_twin = to("groups", q_mine[0], 1)
    core0 = arrive(core0)
    core1 = arrive(core1)
    n0, n1 = cutting[1], quarter - cutting[1]
    pieces = [
        (near0, [(0, 0, 0, n0)]),
        (far0, [(2, 0, 0, n0)]),
        (core0, [(1, 0, 0, n0), (3, 0, n0, n0)]),
        (near1, [(0, n0, 0, n1)]),
        (far1, [(2, n0, 0, n1)]),
        (core1, [(1, n0, 0, n1), (3, n0, n1, n1)]),
    ]
    (far_mine,) = run((MINE,), (1, 2), [w_mine], False)
    halo_mine = send_edge(own_mine, far_mine)
    one_twin = arrive(one_twin)
    w_twin = [own_kv[1], one_twin, two_twin, three_twin]
    (far_twin,) = run((TWIN,), (1, 2), [w_twin], False)
    (own_twin,) = run((TWIN,), (1, 2), [w_twin], True)
    halo_twin = send_edge(own_twin, far_twin)
    line.drop(*w_mine, *w_twin)
    q_twin = arrive(q_twin)
    q_own = run((MINE, TWIN), (0,), [[q_mine], [q_twin]], True)
    q_far = run((MINE, TWIN), (0,), [[q_mine], [q_twin]], False)
    line.drop(q_mine, q_twin, *own_x, *(box for box, _ in pieces))

    def pair(h, rows):
        (q_own[h][0],) = line.after(q_own[h][0])
        parts = attend_pair(
            at, [b[0] for b in limits], [q_own[h][0], q_far[h][0]], [b[0] for b in rows]
        )
        return line.reached(*parts)

    def finish(h, halo, parts):
        (halo,) = line.after(halo)
        keep, send = attend_halo(
            at, [b[0] for b in limits], [q_own[h][0], q_far[h][0]], halo, *(b[0] for b in parts)
        )
        return line.reached(keep)[0], to("seq", send, 1)

    parts_mine = pair(0, (own_mine, far_mine))
    keep_mine, back_mine = finish(0, halo_mine, parts_mine)
    line.drop(*parts_mine)
    parts_twin = pair(1, (own_twin, far_twin))
    keep_twin, back_twin = finish(1, halo_twin, parts_twin)
    parts = [(MINE, keep_mine[0]), (TWIN, keep_twin[0]), (CROSS, back_mine), (CROSS_TWIN, back_twin)]
    return assemble(at, parts)


def solution(mesh):
    placed = (
        P(("groups", "seq"), None),
        P("groups", None),
        P("seq", None, ("fsdp", "head")),
        P(None, ("fsdp", "head")),
        P(),
        P(("groups", "seq"), None),
    )
    return jax.shard_map(
        per_device,
        mesh=mesh,
        in_specs=placed,
        out_specs=P(("groups", "seq"), ("fsdp", "head")),
        check_vma=False,
    )
```

```python
import math

import jax
import jax.numpy as jnp
from jax import lax
from jax.experimental import pallas as pl
from jax.experimental.pallas import tpu as pltpu
from jax.sharding import PartitionSpec as P

EPS = 1e-06
VMEM = 28 << 20
WHOLE = 60 << 20
FIRST = 8
HIDDEN = -1e30
SPACE = pl.CostEstimate(flops=1 << 36, bytes_accessed=1 << 10, transcendentals=0)
COST = pl.CostEstimate(flops=1 << 20, bytes_accessed=1 << 10, transcendentals=0)


def with_halo(shard, sides, width):
    for axis, dim in sides:
        devices, length = (lax.axis_size(axis), shard.shape[dim])
        up = [(i, (i + 1) % devices) for i in range(devices - 1)]
        down = [(j, i) for i, j in up]
        last = lax.slice_in_dim(shard, length - width, length, axis=dim)
        first = lax.slice_in_dim(shard, 0, width, axis=dim)
        before = lax.ppermute(last, axis, up)
        after = lax.ppermute(first, axis, down)
        shard = jnp.concatenate([before, shard, after], axis=dim)
    return shard


def normed_heads(tensor, gain_row, head_dim):
    shaped = tensor.reshape(tensor.shape[0], tensor.shape[1] // head_dim, head_dim)
    scaled = (
        shaped * lax.rsqrt(jnp.mean(shaped * shaped, axis=-1, keepdims=True) + EPS) * gain_row
    )
    return scaled.astype(jnp.bfloat16)


def visible_tiles(block_lists):
    position = lax.axis_index("seq")
    tile_dev = block_lists.shape[0]
    candidates = (position - 1) * tile_dev + jnp.arange(3 * tile_dev, dtype=jnp.int32)
    matches = (block_lists[:, :, None] == candidates[None, None, :]) & (
        block_lists[:, :, None] >= 0
    )
    return jnp.any(matches, axis=1)


def general(frames, modulation, w_qkv, b_qkv, qk_gain, block_lists):
    inputs = frames.astype(jnp.float32)
    average = jnp.mean(inputs, axis=-1, keepdims=True)
    centred = inputs - average
    variance = jnp.mean(centred * centred, axis=-1, keepdims=True)
    normed = centred * lax.rsqrt(variance + EPS) * (1.0 + modulation[0]) + modulation[1]
    normed = normed.astype(jnp.bfloat16)
    tokens = normed.shape[0]
    width_cols = w_qkv.shape[2]
    head_dim = qk_gain.shape[1]
    heads = width_cols // head_dim
    projected = jnp.einsum(
        "td,djc->tjc",
        normed,
        lax.all_gather(w_qkv, "seq", axis=0, tiled=True),
        preferred_element_type=jnp.float32,
    )
    projected = projected + b_qkv
    queries = normed_heads(projected[:, 0], qk_gain[0], head_dim)
    key_rows = normed_heads(projected[:, 1], qk_gain[1], head_dim)
    values = projected[:, 2].astype(jnp.bfloat16).reshape(tokens, heads, head_dim)
    stacked = jnp.stack([key_rows, values], axis=0)
    neighbourhood = with_halo(stacked, (("seq", 1),), tokens)
    tile_len = tokens // block_lists.shape[0]
    allowed_keys = jnp.repeat(
        jnp.repeat(visible_tiles(block_lists), tile_len, axis=0), tile_len, axis=1
    )
    factor = 1.0 / math.sqrt(head_dim)
    scores = (
        jnp.einsum("qhd,khd->hqk", queries, neighbourhood[0], preferred_element_type=jnp.float32)
        * factor
    )
    weights = jnp.where(allowed_keys[None, :, :], jnp.exp(scores), 0.0)
    totals = jnp.sum(weights, axis=-1)
    mixture = jnp.einsum(
        "hqk,khd->qhd",
        weights.astype(jnp.bfloat16),
        neighbourhood[1],
        preferred_element_type=jnp.float32,
    )
    result = (mixture / jnp.transpose(totals)[:, :, None]).astype(jnp.bfloat16)
    return result.reshape(tokens, width_cols)


class Line:
    def __init__(self):
        self.held = []

    def reached(self, *values):
        boxes = [[v] for v in values]
        self.held += boxes
        return boxes

    def after(self, *values):
        out = lax.optimization_barrier((*values, *(box[0] for box in self.held)))
        for box, value in zip(self.held, out[len(values) :]):
            box[0] = value
        return out[: len(values)]

    def drop(self, *boxes):
        self.held = [box for box in self.held if all(box is not b for b in boxes)]
        return [box[0] for box in boxes]


def norm_kernel(x_ref, mod_ref, o_ref):
    x = x_ref[...].astype(jnp.float32)
    centred = x - jnp.mean(x, axis=-1, keepdims=True)
    variance = jnp.mean(centred * centred, axis=-1, keepdims=True)
    scaled = centred * lax.rsqrt(variance + EPS) * (1.0 + mod_ref[0:1, :]) + mod_ref[1:2, :]
    o_ref[...] = scaled.astype(jnp.bfloat16)


def normalize(frames, modulation, rows):
    tokens, width = frames.shape
    return pl.pallas_call(
        norm_kernel,
        grid=(tokens // rows,),
        in_specs=[
            pl.BlockSpec((rows, width), lambda i: (i, 0)),
            pl.BlockSpec((2, width), lambda i: (0, 0)),
        ],
        out_specs=pl.BlockSpec((rows, width), lambda i: (i, 0)),
        out_shape=jax.ShapeDtypeStruct((tokens, width), jnp.bfloat16),
        cost_estimate=COST,
        name="normalize",
    )(frames, modulation)


def cut_heads(at, w, groups, cost=None):
    rows = w.shape[1]
    head_dim = 128
    shapes = [(len(indices), rows, head_dim * len(js)) for indices, js in groups]

    def kernel(at_ref, w_ref, *out_refs):
        for (indices, js), ref in zip(groups, out_refs):
            for n, index in enumerate(indices):
                cols = pl.ds(pl.multiple_of(at_ref[index] * head_dim, 128), head_dim)
                for i, j in enumerate(js):
                    ref[n, :, i * head_dim : (i + 1) * head_dim] = w_ref[j, :, cols]

    return pl.pallas_call(
        kernel,
        in_specs=[pl.BlockSpec(memory_space=pltpu.SMEM), pl.BlockSpec()],
        out_specs=[pl.BlockSpec()] * len(groups),
        out_shape=[jax.ShapeDtypeStruct(shape, jnp.bfloat16) for shape in shapes],
        compiler_params=pltpu.CompilerParams(vmem_limit_bytes=VMEM),
        cost_estimate=cost or COST,
        name="cut_heads",
    )(at, w)


def see(at, lists, tile_dev):
    def kernel(at_ref, lists_ref, o_ref):
        lists = lists_ref[...]
        z = at_ref[0]
        lane = lax.broadcasted_iota(jnp.int32, o_ref.shape, 1)
        out = jnp.full(o_ref.shape, HIDDEN, jnp.float32)
        for c, column in enumerate((z, z ^ 1, jnp.where(z < 2, 2, 1))):
            for t in range(tile_dev):
                hit = (lists == column * tile_dev + t).astype(jnp.float32)
                listed = jnp.max(hit, axis=1, keepdims=True) > 0.0
                out = jnp.where((lane == c * tile_dev + t) & listed, 0.0, out)
        o_ref[...] = out

    return pl.pallas_call(
        kernel,
        in_specs=[pl.BlockSpec(memory_space=pltpu.SMEM), pl.BlockSpec()],
        out_specs=pl.BlockSpec(),
        out_shape=jax.ShapeDtypeStruct((lists.shape[0], 128), jnp.float32),
        cost_estimate=COST,
        name="see",
    )(at, lists)


def load_columns(at, own, pieces, x_ref, sems, step):
    count, tokens, _ = x_ref.shape
    copies = ([], [])
    for r in range(0, tokens if own is not None else 0, step):
        copies[0].append((own.at[pl.ds(r, step)], x_ref.at[0, pl.ds(r, step)]))
    for ref, parts in pieces:
        for i, start, first, size in parts:
            row = pl.multiple_of((at[1] ^ i) * (tokens // 4) + start, 16)
            copies[1].append((ref.at[pl.ds(first, size)], x_ref.at[count - 1, pl.ds(row, size)]))
    made, n = ([], []), 0
    for group, out in zip(copies, made):
        for source, target in group:
            out.append(pltpu.make_async_copy(source, target, sems.at[n]))
            n += 1
    return made


def normed(value, gain):
    mean = jnp.mean(value * value, axis=-1, keepdims=True)
    return value * lax.rsqrt(mean + EPS) * gain


def keys_values(at, head, own, pieces, weights, bias, gain, own_rows=None):
    _, rows, cols = weights[0].shape
    head_dim = gain.shape[1]
    arrays, parts = zip(*pieces) if pieces else ((), ())
    width = (arrays or (own,))[0].shape[1]
    tokens = own.shape[0] if own is not None else own_rows.shape[0]
    columns = [0] * (own is not None) + [1] * bool(pieces)
    step = 256
    moves = tokens // step + sum(map(len, parts))
    sources = [own] * (own is not None) + list(arrays)
    known = [] if own_rows is None else [own_rows]
    n_out = (own is not None) + 2 * bool(pieces)

    def kernel(at_ref, *refs):
        x_sources, weight_refs = refs[: len(sources)], refs[len(sources) : len(sources) + 4]
        b_ref, g_ref, *rest = refs[len(sources) + 4 :]
        own_in, out_refs = rest[: len(known)], rest[len(known) : len(known) + n_out]
        x_ref, w_ref, x_sems, w_sems = rest[-4:]
        z = at_ref[0]
        is_mid = (z == 1) | (z == 2)
        lanes = pl.ds(pl.multiple_of(at_ref[head] * head_dim, 128), head_dim)
        loads = [
            pltpu.make_async_copy(ref, w_ref.at[pl.ds(s, 1)], w_sems.at[s])
            for s, ref in enumerate(weight_refs)
        ]
        piece_refs = x_sources[len(sources) - len(arrays) :]
        own_moves, far_moves = load_columns(
            at_ref, x_sources[0] if 0 in columns else None, list(zip(piece_refs, parts)), x_ref, x_sems, step
        )
        for copy in [*loads, *own_moves, *far_moves]:
            copy.start()
        for copy in loads:
            copy.wait()
        for column in columns:
            if column:
                for copy in far_moves:
                    copy.wait()
            out_ref = out_refs[0 if column == 0 else -2]
            for r in range(tokens // step):
                if not column:
                    own_moves[r].wait()
                here = slice(r * step, (r + 1) * step)
                total = None
                for s in range(4):
                    first = pl.multiple_of((z ^ s) * rows, 128)
                    product = jnp.dot(
                        x_ref[columns.index(column), here, pl.ds(first, rows)], w_ref[s],
                        preferred_element_type=jnp.float32,
                    )
                    total = product if total is None else total + product
                key = normed(total[:, :head_dim] + b_ref[1:2, lanes], g_ref[1:2, :])
                out_ref[here, :head_dim] = key.astype(jnp.bfloat16)
                value = total[:, head_dim:] + b_ref[2:3, lanes]
                out_ref[here, head_dim:] = value.astype(jnp.bfloat16)
                if column:
                    own_ref = own_in[0] if known else out_refs[0]
                    out_refs[-1][here, :] = jnp.where(is_mid, own_ref[here, :], out_ref[here, :])

    hbm = pl.BlockSpec(memory_space=pltpu.HBM)
    out = jax.ShapeDtypeStruct((tokens, cols), jnp.bfloat16)
    return pl.pallas_call(
        kernel,
        in_specs=[pl.BlockSpec(memory_space=pltpu.SMEM)]
        + [hbm] * (len(sources) + 4)
        + [pl.BlockSpec()] * (2 + len(known)),
        out_specs=[pl.BlockSpec()] * n_out,
        out_shape=[out] * n_out,
        scratch_shapes=[
            pltpu.VMEM((len(columns), tokens, width), jnp.bfloat16),
            pltpu.VMEM((4, rows, cols), jnp.bfloat16),
            pltpu.SemaphoreType.DMA((moves,)),
            pltpu.SemaphoreType.DMA((4,)),
        ],
        compiler_params=pltpu.CompilerParams(vmem_limit_bytes=WHOLE),
        cost_estimate=SPACE,
        name="keys_values",
    )(at, *sources, *weights, bias, gain, *known)


def take_rows(at, frames, sizes):
    width = frames.shape[1]
    quarter = sum(sizes)

    def kernel(at_ref, x_ref, *out_refs):
        first = 0
        for ref in out_refs:
            ref[...] = x_ref[first : first + ref.shape[0], :]
            first += ref.shape[0]

    return pl.pallas_call(
        kernel,
        grid_spec=pltpu.PrefetchScalarGridSpec(
            num_scalar_prefetch=1,
            grid=(1,),
            in_specs=[pl.BlockSpec((quarter, width), lambda i, at: (at[1], 0))],
            out_specs=[pl.BlockSpec((size, width), lambda i, at: (0, 0)) for size in sizes],
        ),
        out_shape=[jax.ShapeDtypeStruct((size, width), jnp.bfloat16) for size in sizes],
        cost_estimate=COST,
        name="take_rows",
    )(at, frames)


def attend_pair(at, limits, own, pieces, weights, bias, gain, rows):
    tokens, width = own.shape
    head_dim = gain.shape[1]
    tiles = limits[0].shape[0]
    tile = tokens // tiles
    arrays, parts = zip(*pieces)
    step = 256
    moves = tokens // step + sum(map(len, parts))
    shard = weights[0].shape[1]

    def kernel(at_ref, limit0_ref, limit1_ref, own_ref, *refs):
        piece_refs, weight_refs = refs[: len(arrays)], refs[len(arrays) : len(arrays) + 2]
        row_refs = refs[len(arrays) + 2 : len(arrays) + 6]
        (b_ref, g_ref, edge_ref, done_ref, mixed_ref, total_ref,
         x_ref, w_ref, q_ref, kv_ref, x_sems, w_sems) = refs[len(arrays) + 6 :]
        z = at_ref[0]
        is_mid = (z == 1) | (z == 2)
        loads = [
            pltpu.make_async_copy(ref, w_ref.at[h], w_sems.at[h])
            for h, ref in enumerate(weight_refs)
        ]
        own_moves, far_moves = load_columns(at_ref, own_ref, list(zip(piece_refs, parts)), x_ref, x_sems, step)
        late = [
            pltpu.make_async_copy(ref, kv_ref.at[n // 2, n % 2], w_sems.at[2 + n])
            for n, ref in enumerate(row_refs)
        ]
        for copy in [*loads, *own_moves, *far_moves, *late]:
            copy.start()
        for copy in loads:
            copy.wait()
        for column in range(2):
            if column:
                for copy in far_moves:
                    copy.wait()
            for r in range(tokens // step):
                if not column:
                    own_moves[r].wait()
                here = slice(r * step, (r + 1) * step)
                total = None
                for s in range(4):
                    product = jnp.dot(
                        x_ref[column, here, s * shard : (s + 1) * shard],
                        jnp.concatenate([w_ref[0, s], w_ref[1, s]], axis=1),
                        preferred_element_type=jnp.float32,
                    )
                    total = product if total is None else total + product
                for h in range(2):
                    lanes = pl.ds(pl.multiple_of(at_ref[2 + h] * head_dim, 128), head_dim)
                    value = total[:, h * head_dim : (h + 1) * head_dim] + b_ref[0:1, lanes]
                    q_ref[h, column, here, :] = normed(value, g_ref[0:1, :]).astype(jnp.bfloat16)
        for copy in late:
            copy.wait()

        @pl.loop(0, 2)
        def _(h):
            for column in range(2):
                is_edge = is_mid if column == 0 else jnp.logical_not(is_mid)
                for i in range(tiles):
                    here = slice(i * tile, (i + 1) * tile)
                    query = q_ref[h, column, here, :]
                    total = jnp.zeros((tile, 128), jnp.float32)
                    mixed = jnp.zeros((tile, head_dim), jnp.float32)
                    for other in range(2):
                        for t in range(tiles):
                            limit = (limit0_ref, limit1_ref)[column][i, (other ^ column) * tiles + t]
                            total, mixed = tile_step(
                                query, kv_ref.at[h, other], t * tile, tile, head_dim, limit, total, mixed
                            )

                    @pl.when(is_edge)
                    def _():
                        edge_ref[h, here, :] = query
                        mixed_ref[h, here, :] = mixed
                        total_ref[h, here, :] = total

                    @pl.when(jnp.logical_not(is_edge))
                    def _():
                        rows = mixed / jnp.sum(total, axis=-1, keepdims=True)
                        done_ref[h, here, :] = rows.astype(jnp.bfloat16)

    smem = pl.BlockSpec(memory_space=pltpu.SMEM)
    hbm = pl.BlockSpec(memory_space=pltpu.HBM)
    shape = (2, tokens, head_dim)
    return pl.pallas_call(
        kernel,
        in_specs=[smem] * 3 + [hbm] * (1 + len(arrays) + 6) + [pl.BlockSpec()] * 2,
        out_specs=[pl.BlockSpec()] * 4,
        out_shape=[
            jax.ShapeDtypeStruct(shape, jnp.bfloat16),
            jax.ShapeDtypeStruct(shape, jnp.bfloat16),
            jax.ShapeDtypeStruct(shape, jnp.float32),
            jax.ShapeDtypeStruct((2, tokens, 128), jnp.float32),
        ],
        scratch_shapes=[
            pltpu.VMEM((2, tokens, width), jnp.bfloat16),
            pltpu.VMEM((2, 4, shard, head_dim), jnp.bfloat16),
            pltpu.VMEM((2, 2, tokens, head_dim), jnp.bfloat16),
            pltpu.VMEM((2, 2, tokens, 2 * head_dim), jnp.bfloat16),
            pltpu.SemaphoreType.DMA((moves,)),
            pltpu.SemaphoreType.DMA((6,)),
        ],
        compiler_params=pltpu.CompilerParams(vmem_limit_bytes=WHOLE),
        cost_estimate=COST,
        name="attend_pair",
    )(at, *limits, own, *arrays, *weights, *rows, bias, gain)


def attend_halo(at, h, limits, query, halo, done, mixed, total):
    _, tokens, head_dim = query.shape
    tiles = limits[0].shape[0]
    tile = tokens // tiles

    def kernel(at_ref, limit0_ref, limit1_ref, q_ref, halo_ref, done_ref, mixed_ref, total_ref, keep_ref, send_ref):
        is_mid = (at_ref[0] == 1) | (at_ref[0] == 2)
        for i in range(tiles):
            here = slice(i * tile, (i + 1) * tile)
            sums, rows = total_ref[0, here, :], mixed_ref[0, here, :]
            for t in range(tiles):
                limit = jnp.where(is_mid, limit0_ref[i, 2 * tiles + t], limit1_ref[i, 2 * tiles + t])
                sums, rows = tile_step(
                    q_ref[0, here, :], halo_ref, t * tile, tile, head_dim, limit, sums, rows
                )
            edge = (rows / jnp.sum(sums, axis=-1, keepdims=True)).astype(jnp.bfloat16)
            outer = done_ref[0, here, :]
            keep_ref[here, :] = jnp.where(is_mid, edge, outer)
            send_ref[here, :] = jnp.where(is_mid, outer, edge)

    smem = pl.BlockSpec(memory_space=pltpu.SMEM)
    one = pl.BlockSpec((1, tokens, head_dim), lambda i: (h, 0, 0))
    fixed = lambda shape: pl.BlockSpec(shape, lambda i: (0,) * len(shape))
    out = jax.ShapeDtypeStruct((tokens, head_dim), jnp.bfloat16)
    return pl.pallas_call(
        kernel,
        grid=(1,),
        in_specs=[smem] * 3 + [one, fixed(halo.shape), one, one, one],
        out_specs=[fixed(out.shape)] * 2,
        out_shape=[out] * 2,
        compiler_params=pltpu.CompilerParams(vmem_limit_bytes=VMEM),
        cost_estimate=SPACE,
        name="attend_halo",
    )(at, *limits, query, halo, done, mixed, total)


def assemble(at, parts, carried=None, cost=None, heads=4):
    (first, one), (second, two) = parts
    tokens, head_dim = one.shape
    carried = () if carried is None else (carried,)

    def kernel(at_ref, one_ref, two_ref, *rest):
        @pl.when(pl.program_id(0) == 0)
        def _():
            rest[-1][...] = one_ref[...]

        @pl.when(pl.program_id(0) == 1)
        def _():
            rest[-1][...] = two_ref[...]

    whole = pl.BlockSpec((tokens, head_dim), lambda i, at: (0, 0))
    return pl.pallas_call(
        kernel,
        grid_spec=pltpu.PrefetchScalarGridSpec(
            num_scalar_prefetch=1,
            grid=(2,),
            in_specs=[whole, whole] + [pl.BlockSpec(memory_space=pl.ANY)] * len(carried),
            out_specs=pl.BlockSpec(
                (tokens, head_dim), lambda i, at: (0, jnp.where(i == 0, at[first], at[second]))
            ),
        ),
        out_shape=jax.ShapeDtypeStruct((tokens, head_dim * heads), jnp.bfloat16),
        input_output_aliases={3: 0} if carried else {},
        cost_estimate=cost or COST,
        name="assemble",
    )(at, one, two, *carried)


def tile_step(query, rows_ref, at, tile, head_dim, limit, total, mixed):
    scale = math.log2(math.e) / math.sqrt(head_dim)
    keys = rows_ref[at : at + tile, :head_dim]
    values = rows_ref[at : at + tile, head_dim:]
    scores = lax.dot_general(
        query, keys, (((1,), (1,)), ((), ())), preferred_element_type=jnp.float32
    )
    weights = jnp.exp2(scores * scale + limit)
    for c in range(tile // 128):
        total = total + weights[:, c * 128 : (c + 1) * 128]
    mixed = mixed + jnp.dot(
        weights.astype(jnp.bfloat16), values, preferred_element_type=jnp.float32
    )
    return total, mixed


def per_device(frames, modulation, w_qkv, b_qkv, qk_gain, block_lists):
    sizes = tuple(lax.axis_size(a) for a in ("groups", "seq", "fsdp", "head"))
    head_dim = qk_gain.shape[1]
    width_cols = w_qkv.shape[2]
    tokens = frames.shape[0]
    if sizes != (2, 4, 2, 2) or width_cols != 4 * head_dim:
        return general(frames, modulation, w_qkv, b_qkv, qk_gain, block_lists)

    y, z, x, core = (lax.axis_index(a).astype(jnp.int32) for a in ("groups", "seq", "fsdp", "head"))
    rows = w_qkv.shape[0]
    quarter = tokens // 4
    tile_dev = block_lists.shape[0]

    def to(axis, value, bit):
        return lax.ppermute(value, axis, [(i, i ^ bit) for i in range(lax.axis_size(axis))])

    side = z % 2
    mine, twin = 2 * side + y, 2 * side + 1 - y
    across = 2 * (1 - side)
    at = jnp.stack([z, 2 * x + core, mine, twin, across + y, across + 1 - y, y, 2 + y])
    MINE, TWIN, CROSS, CROSS_TWIN = 2, 3, 4, 5
    is_mid = (z == 1) | (z == 2)
    w = jnp.transpose(w_qkv, (1, 0, 2))
    line = Line()

    def arrive(value):
        box = line.reached(value)[0]
        (box[0],) = line.after(box[0])
        return box

    cutting = (0, quarter * FIRST // 12, quarter)
    raws = take_rows(at, frames, [hi - lo for lo, hi in zip(cutting, cutting[1:])])
    raws_other = [to("seq", raw, 1) for raw in raws]
    (w, *_) = lax.optimization_barrier((w, *raws))
    same, cross, q_sent = line.reached(
        *cut_heads(at, w, [((MINE,), (1, 2)), ((CROSS,), (1, 2)), ((6, 7, 6, 7), (0,))])
    )
    got = [to("seq", same[0], 2), to("seq", cross[0], 3), to("seq", cross[0], 1)]
    own_limit = line.reached(see(at, block_lists, tile_dev))
    frames, modulation = line.after(frames, modulation)
    own_x = line.reached(normalize(frames, modulation, 128))
    line.drop(cross)

    def take(i):
        (raw,) = line.after(raws_other[i])
        near = line.reached(normalize(raw, modulation, raw.shape[0]))[0]
        return near, to("fsdp", near[0], 1)

    def spread(near, far):
        far = arrive(far)
        both = jnp.concatenate([near[0], far[0]], axis=0)
        return far, to("head", both, 1)

    def swap(which):
        kept = arrive(got[which])
        return kept, to("groups", kept[0], 1)

    near0, far0 = take(0)
    two_mine, two_twin = swap(0)
    near1, far1 = take(1)
    (q_sent[0],) = line.after(q_sent[0])
    q_got = lax.all_to_all(q_sent[0], "seq", split_axis=0, concat_axis=0, tiled=True)
    line.drop(q_sent)
    three_mine, three_twin = swap(1)
    one_mine, one_twin = swap(2)
    (w,) = line.after(w)
    own_kv = [same, line.reached(*cut_heads(at, w, [((TWIN,), (1, 2))], SPACE))[0]]
    far0, core0 = spread(near0, far0)
    two_twin = arrive(two_twin)
    three_twin = arrive(three_twin)
    far1, core1 = spread(near1, far1)
    w_mine = [own_kv[0], one_mine, two_mine, three_mine]

    def kv(head, boxes, own, pieces, own_rows=None):
        (boxes[0][0],) = line.after(boxes[0][0])
        weights = [box[0] for box in boxes]
        return keys_values(at, head, own, pieces, weights, b_qkv, qk_gain, own_rows)

    own_mine = line.reached(*kv(MINE, w_mine, own_x[0][0], None))[0]
    (own_limit[0][0],) = line.after(own_limit[0][0])
    far_limit = to("seq", own_limit[0][0], 1)
    q_mine = arrive(q_got)
    q_twin = to("groups", q_mine[0], 1)
    core0 = arrive(core0)
    core1 = arrive(core1)
    n0, n1 = cutting[1], quarter - cutting[1]
    pieces = [
        (near0, [(0, 0, 0, n0)]),
        (far0, [(2, 0, 0, n0)]),
        (core0, [(1, 0, 0, n0), (3, 0, n0, n0)]),
        (near1, [(0, n0, 0, n1)]),
        (far1, [(2, n0, 0, n1)]),
        (core1, [(1, n0, 0, n1), (3, n0, n1, n1)]),
    ]

    def column_arrays():
        return own_x[0][0], [(box[0], parts) for box, parts in pieces]

    far, edge = kv(MINE, w_mine, None, column_arrays()[1], own_mine[0])
    rows_mine, halo_mine = [own_mine, *line.reached(far)], to("seq", edge, 2)
    one_twin = arrive(one_twin)
    w_twin = [own_kv[1], one_twin, two_twin, three_twin]
    own, far, edge = kv(TWIN, w_twin, *column_arrays())
    rows_twin, halo_twin = line.reached(own, far), to("seq", edge, 2)
    line.drop(*w_mine, *w_twin)
    limits = own_limit + [arrive(far_limit)]
    q_twin = arrive(q_twin)
    parts = line.reached(
        *attend_pair(
            at, [b[0] for b in limits], *column_arrays(), [q_mine[0], q_twin[0]], b_qkv, qk_gain,
            [b[0] for b in (*rows_mine, *rows_twin)],
        )
    )
    line.drop(q_mine, q_twin, *own_x, *(box for box, _ in pieces), *rows_mine, *rows_twin)

    def finish(h, halo):
        (halo,) = line.after(halo)
        query, *rest = [b[0] for b in parts]
        keep, send = attend_halo(at, h, [b[0] for b in limits], query, halo, *rest)
        return line.reached(keep)[0], to("seq", send, 1)

    keep_mine, back_mine = finish(0, halo_mine)
    keep_twin, back_twin = finish(1, halo_twin)
    half_done = assemble(at, [(MINE, keep_mine[0]), (CROSS, back_mine)], None, SPACE)
    return assemble(at, [(TWIN, keep_twin[0]), (CROSS_TWIN, back_twin)], half_done)


def solution(mesh):
    placed = (
        P(("groups", "seq"), None),
        P("groups", None),
        P("seq", None, ("fsdp", "head")),
        P(None, ("fsdp", "head")),
        P(),
        P(("groups", "seq"), None),
    )
    return jax.shard_map(
        per_device,
        mesh=mesh,
        in_specs=placed,
        out_specs=P(("groups", "seq"), ("fsdp", "head")),
        check_vma=False,
    )
```

```python
import math

import jax
import jax.numpy as jnp
from jax import lax
from jax.experimental import pallas as pl
from jax.experimental.pallas import tpu as pltpu
from jax.sharding import PartitionSpec as P

EPS = 1e-06
VMEM = 28 << 20
WHOLE = 60 << 20
FIRST = 8
HIDDEN = -1e30
SPACE = pl.CostEstimate(flops=1 << 36, bytes_accessed=1 << 10, transcendentals=0)
COST = pl.CostEstimate(flops=1 << 20, bytes_accessed=1 << 10, transcendentals=0)


def with_halo(shard, sides, width):
    for axis, dim in sides:
        devices, length = (lax.axis_size(axis), shard.shape[dim])
        up = [(i, (i + 1) % devices) for i in range(devices - 1)]
        down = [(j, i) for i, j in up]
        last = lax.slice_in_dim(shard, length - width, length, axis=dim)
        first = lax.slice_in_dim(shard, 0, width, axis=dim)
        before = lax.ppermute(last, axis, up)
        after = lax.ppermute(first, axis, down)
        shard = jnp.concatenate([before, shard, after], axis=dim)
    return shard


def normed_heads(tensor, gain_row, head_dim):
    shaped = tensor.reshape(tensor.shape[0], tensor.shape[1] // head_dim, head_dim)
    scaled = (
        shaped * lax.rsqrt(jnp.mean(shaped * shaped, axis=-1, keepdims=True) + EPS) * gain_row
    )
    return scaled.astype(jnp.bfloat16)


def visible_tiles(block_lists):
    position = lax.axis_index("seq")
    tile_dev = block_lists.shape[0]
    candidates = (position - 1) * tile_dev + jnp.arange(3 * tile_dev, dtype=jnp.int32)
    matches = (block_lists[:, :, None] == candidates[None, None, :]) & (
        block_lists[:, :, None] >= 0
    )
    return jnp.any(matches, axis=1)


def general(frames, modulation, w_qkv, b_qkv, qk_gain, block_lists):
    inputs = frames.astype(jnp.float32)
    average = jnp.mean(inputs, axis=-1, keepdims=True)
    centred = inputs - average
    variance = jnp.mean(centred * centred, axis=-1, keepdims=True)
    normed = centred * lax.rsqrt(variance + EPS) * (1.0 + modulation[0]) + modulation[1]
    normed = normed.astype(jnp.bfloat16)
    tokens = normed.shape[0]
    width_cols = w_qkv.shape[2]
    head_dim = qk_gain.shape[1]
    heads = width_cols // head_dim
    projected = jnp.einsum(
        "td,djc->tjc",
        normed,
        lax.all_gather(w_qkv, "seq", axis=0, tiled=True),
        preferred_element_type=jnp.float32,
    )
    projected = projected + b_qkv
    queries = normed_heads(projected[:, 0], qk_gain[0], head_dim)
    key_rows = normed_heads(projected[:, 1], qk_gain[1], head_dim)
    values = projected[:, 2].astype(jnp.bfloat16).reshape(tokens, heads, head_dim)
    stacked = jnp.stack([key_rows, values], axis=0)
    neighbourhood = with_halo(stacked, (("seq", 1),), tokens)
    tile_len = tokens // block_lists.shape[0]
    allowed_keys = jnp.repeat(
        jnp.repeat(visible_tiles(block_lists), tile_len, axis=0), tile_len, axis=1
    )
    factor = 1.0 / math.sqrt(head_dim)
    scores = (
        jnp.einsum("qhd,khd->hqk", queries, neighbourhood[0], preferred_element_type=jnp.float32)
        * factor
    )
    weights = jnp.where(allowed_keys[None, :, :], jnp.exp(scores), 0.0)
    totals = jnp.sum(weights, axis=-1)
    mixture = jnp.einsum(
        "hqk,khd->qhd",
        weights.astype(jnp.bfloat16),
        neighbourhood[1],
        preferred_element_type=jnp.float32,
    )
    result = (mixture / jnp.transpose(totals)[:, :, None]).astype(jnp.bfloat16)
    return result.reshape(tokens, width_cols)


class Line:
    def __init__(self):
        self.held = []

    def reached(self, *values):
        boxes = [[v] for v in values]
        self.held += boxes
        return boxes

    def after(self, *values):
        out = lax.optimization_barrier((*values, *(box[0] for box in self.held)))
        for box, value in zip(self.held, out[len(values) :]):
            box[0] = value
        return out[: len(values)]

    def drop(self, *boxes):
        self.held = [box for box in self.held if all(box is not b for b in boxes)]
        return [box[0] for box in boxes]


def norm_kernel(x_ref, mod_ref, o_ref):
    x = x_ref[...].astype(jnp.float32)
    centred = x - jnp.mean(x, axis=-1, keepdims=True)
    variance = jnp.mean(centred * centred, axis=-1, keepdims=True)
    scaled = centred * lax.rsqrt(variance + EPS) * (1.0 + mod_ref[0:1, :]) + mod_ref[1:2, :]
    o_ref[...] = scaled.astype(jnp.bfloat16)


def normalize(frames, modulation, rows):
    tokens, width = frames.shape
    return pl.pallas_call(
        norm_kernel,
        grid=(tokens // rows,),
        in_specs=[
            pl.BlockSpec((rows, width), lambda i: (i, 0)),
            pl.BlockSpec((2, width), lambda i: (0, 0)),
        ],
        out_specs=pl.BlockSpec((rows, width), lambda i: (i, 0)),
        out_shape=jax.ShapeDtypeStruct((tokens, width), jnp.bfloat16),
        cost_estimate=COST,
        name="normalize",
    )(frames, modulation)


def cut_heads(at, w, groups, cost=None):
    rows = w.shape[1]
    head_dim = 128
    shapes = [(len(indices), rows, head_dim * len(js)) for indices, js in groups]

    def kernel(at_ref, w_ref, *out_refs):
        for (indices, js), ref in zip(groups, out_refs):
            for n, index in enumerate(indices):
                cols = pl.ds(pl.multiple_of(at_ref[index] * head_dim, 128), head_dim)
                for i, j in enumerate(js):
                    ref[n, :, i * head_dim : (i + 1) * head_dim] = w_ref[j, :, cols]

    return pl.pallas_call(
        kernel,
        in_specs=[pl.BlockSpec(memory_space=pltpu.SMEM), pl.BlockSpec()],
        out_specs=[pl.BlockSpec()] * len(groups),
        out_shape=[jax.ShapeDtypeStruct(shape, jnp.bfloat16) for shape in shapes],
        compiler_params=pltpu.CompilerParams(vmem_limit_bytes=VMEM),
        cost_estimate=cost or COST,
        name="cut_heads",
    )(at, w)


def see(at, lists, tile_dev):
    def kernel(at_ref, lists_ref, o_ref):
        lists = lists_ref[...]
        z = at_ref[0]
        lane = lax.broadcasted_iota(jnp.int32, o_ref.shape, 1)
        out = jnp.full(o_ref.shape, HIDDEN, jnp.float32)
        for c, column in enumerate((z, z ^ 1, jnp.where(z < 2, 2, 1))):
            for t in range(tile_dev):
                hit = (lists == column * tile_dev + t).astype(jnp.float32)
                listed = jnp.max(hit, axis=1, keepdims=True) > 0.0
                out = jnp.where((lane == c * tile_dev + t) & listed, 0.0, out)
        o_ref[...] = out

    return pl.pallas_call(
        kernel,
        in_specs=[pl.BlockSpec(memory_space=pltpu.SMEM), pl.BlockSpec()],
        out_specs=pl.BlockSpec(),
        out_shape=jax.ShapeDtypeStruct((lists.shape[0], 128), jnp.float32),
        cost_estimate=COST,
        name="see",
    )(at, lists)


def load_columns(at, own, pieces, x_ref, sems, step):
    count, tokens, _ = x_ref.shape
    copies = ([], [])
    for r in range(0, tokens if own is not None else 0, step):
        copies[0].append((own.at[pl.ds(r, step)], x_ref.at[0, pl.ds(r, step)]))
    for ref, parts in pieces:
        for i, start, first, size in parts:
            row = pl.multiple_of((at[1] ^ i) * (tokens // 4) + start, 16)
            copies[1].append((ref.at[pl.ds(first, size)], x_ref.at[count - 1, pl.ds(row, size)]))
    made, n = ([], []), 0
    for group, out in zip(copies, made):
        for source, target in group:
            out.append(pltpu.make_async_copy(source, target, sems.at[n]))
            n += 1
    return made


def start(copies):
    for copy in copies:
        copy.start()


def start_next(waves, n):
    if n + 1 < len(waves):
        start(waves[n + 1])
    for copy in waves[n]:
        copy.wait()


def normed(value, gain):
    mean = jnp.mean(value * value, axis=-1, keepdims=True)
    return value * lax.rsqrt(mean + EPS) * gain


def keys_values(at, head, own, pieces, weights, bias, gain, own_rows=None):
    _, rows, cols = weights[0].shape
    head_dim = gain.shape[1]
    arrays, parts = zip(*pieces) if pieces else ((), ())
    width = (arrays or (own,))[0].shape[1]
    tokens = own.shape[0] if own is not None else own_rows.shape[0]
    columns = [0] * (own is not None) + [1] * bool(pieces)
    step = 256
    moves = tokens // step + sum(map(len, parts))
    sources = [own] * (own is not None) + list(arrays)
    known = [] if own_rows is None else [own_rows]
    n_out = (own is not None) + 2 * bool(pieces)

    def kernel(at_ref, *refs):
        x_sources, weight_refs = refs[: len(sources)], refs[len(sources) : len(sources) + 4]
        b_ref, g_ref, *rest = refs[len(sources) + 4 :]
        own_in, out_refs = rest[: len(known)], rest[len(known) : len(known) + n_out]
        x_ref, w_ref, x_sems, w_sems = rest[-4:]
        z = at_ref[0]
        is_mid = (z == 1) | (z == 2)
        lanes = pl.ds(pl.multiple_of(at_ref[head] * head_dim, 128), head_dim)
        loads = [
            pltpu.make_async_copy(ref, w_ref.at[pl.ds(s, 1)], w_sems.at[s])
            for s, ref in enumerate(weight_refs)
        ]
        piece_refs = x_sources[len(sources) - len(arrays) :]
        own_moves, far_moves = load_columns(
            at_ref, x_sources[0] if 0 in columns else None, list(zip(piece_refs, parts)), x_ref, x_sems, step
        )
        waves = [[move] for move in own_moves] + [far_moves] * bool(far_moves)
        start([*loads, *waves[0]])
        for copy in loads:
            copy.wait()
        for column in columns:
            if column:
                start_next(waves, len(own_moves))
            out_ref = out_refs[0 if column == 0 else -2]
            for r in range(tokens // step):
                if not column:
                    start_next(waves, r)
                here = slice(r * step, (r + 1) * step)
                total = None
                for s in range(4):
                    first = pl.multiple_of((z ^ s) * rows, 128)
                    product = jnp.dot(
                        x_ref[columns.index(column), here, pl.ds(first, rows)], w_ref[s],
                        preferred_element_type=jnp.float32,
                    )
                    total = product if total is None else total + product
                key = normed(total[:, :head_dim] + b_ref[1:2, lanes], g_ref[1:2, :])
                out_ref[here, :head_dim] = key.astype(jnp.bfloat16)
                value = total[:, head_dim:] + b_ref[2:3, lanes]
                out_ref[here, head_dim:] = value.astype(jnp.bfloat16)
                if column:
                    own_ref = own_in[0] if known else out_refs[0]
                    out_refs[-1][here, :] = jnp.where(is_mid, own_ref[here, :], out_ref[here, :])

    hbm = pl.BlockSpec(memory_space=pltpu.HBM)
    out = jax.ShapeDtypeStruct((tokens, cols), jnp.bfloat16)
    return pl.pallas_call(
        kernel,
        in_specs=[pl.BlockSpec(memory_space=pltpu.SMEM)]
        + [hbm] * (len(sources) + 4)
        + [pl.BlockSpec()] * (2 + len(known)),
        out_specs=[pl.BlockSpec()] * n_out,
        out_shape=[out] * n_out,
        scratch_shapes=[
            pltpu.VMEM((len(columns), tokens, width), jnp.bfloat16),
            pltpu.VMEM((4, rows, cols), jnp.bfloat16),
            pltpu.SemaphoreType.DMA((moves,)),
            pltpu.SemaphoreType.DMA((4,)),
        ],
        compiler_params=pltpu.CompilerParams(vmem_limit_bytes=WHOLE),
        cost_estimate=SPACE,
        name="keys_values",
    )(at, *sources, *weights, bias, gain, *known)


def take_rows(at, frames, sizes):
    width = frames.shape[1]
    quarter = sum(sizes)

    def kernel(at_ref, x_ref, *out_refs):
        first = 0
        for ref in out_refs:
            ref[...] = x_ref[first : first + ref.shape[0], :]
            first += ref.shape[0]

    return pl.pallas_call(
        kernel,
        grid_spec=pltpu.PrefetchScalarGridSpec(
            num_scalar_prefetch=1,
            grid=(1,),
            in_specs=[pl.BlockSpec((quarter, width), lambda i, at: (at[1], 0))],
            out_specs=[pl.BlockSpec((size, width), lambda i, at: (0, 0)) for size in sizes],
        ),
        out_shape=[jax.ShapeDtypeStruct((size, width), jnp.bfloat16) for size in sizes],
        cost_estimate=COST,
        name="take_rows",
    )(at, frames)


def attend_pair(at, limits, own, pieces, weights, bias, gain, rows):
    tokens, width = own.shape
    head_dim = gain.shape[1]
    tiles = limits[0].shape[0]
    tile = tokens // tiles
    arrays, parts = zip(*pieces)
    step = 256
    moves = tokens // step + sum(map(len, parts))
    shard = weights[0].shape[1]

    def kernel(at_ref, limit0_ref, limit1_ref, own_ref, *refs):
        piece_refs, weight_refs = refs[: len(arrays)], refs[len(arrays) : len(arrays) + 2]
        row_refs = refs[len(arrays) + 2 : len(arrays) + 6]
        (b_ref, g_ref, edge_ref, done_ref, mixed_ref, total_ref,
         x_ref, w_ref, q_ref, kv_ref, x_sems, w_sems) = refs[len(arrays) + 6 :]
        z = at_ref[0]
        is_mid = (z == 1) | (z == 2)
        loads = [
            pltpu.make_async_copy(ref, w_ref.at[h], w_sems.at[h])
            for h, ref in enumerate(weight_refs)
        ]
        own_moves, far_moves = load_columns(at_ref, own_ref, list(zip(piece_refs, parts)), x_ref, x_sems, step)
        late = [
            pltpu.make_async_copy(ref, kv_ref.at[n // 2, n % 2], w_sems.at[2 + n])
            for n, ref in enumerate(row_refs)
        ]
        waves = [[move] for move in own_moves] + [far_moves, late]
        start([*loads, *waves[0]])
        for copy in loads:
            copy.wait()
        for column in range(2):
            if column:
                start_next(waves, len(own_moves))
            for r in range(tokens // step):
                if not column:
                    start_next(waves, r)
                here = slice(r * step, (r + 1) * step)
                total = None
                for s in range(4):
                    product = jnp.dot(
                        x_ref[column, here, s * shard : (s + 1) * shard],
                        jnp.concatenate([w_ref[0, s], w_ref[1, s]], axis=1),
                        preferred_element_type=jnp.float32,
                    )
                    total = product if total is None else total + product
                for h in range(2):
                    lanes = pl.ds(pl.multiple_of(at_ref[2 + h] * head_dim, 128), head_dim)
                    value = total[:, h * head_dim : (h + 1) * head_dim] + b_ref[0:1, lanes]
                    q_ref[h, column, here, :] = normed(value, g_ref[0:1, :]).astype(jnp.bfloat16)
        for copy in late:
            copy.wait()

        @pl.loop(0, 2)
        def _(h):
            for column in range(2):
                is_edge = is_mid if column == 0 else jnp.logical_not(is_mid)
                for i in range(tiles):
                    here = slice(i * tile, (i + 1) * tile)
                    query = q_ref[h, column, here, :]
                    total = jnp.zeros((tile, 128), jnp.float32)
                    mixed = jnp.zeros((tile, head_dim), jnp.float32)
                    for other in range(2):
                        for t in range(tiles):
                            limit = (limit0_ref, limit1_ref)[column][i, (other ^ column) * tiles + t]
                            total, mixed = tile_step(
                                query, kv_ref.at[h, other], t * tile, tile, head_dim, limit, total, mixed
                            )

                    @pl.when(is_edge)
                    def _():
                        edge_ref[h, here, :] = query
                        mixed_ref[h, here, :] = mixed
                        total_ref[h, here, :] = total

                    @pl.when(jnp.logical_not(is_edge))
                    def _():
                        rows = mixed / jnp.sum(total, axis=-1, keepdims=True)
                        done_ref[h, here, :] = rows.astype(jnp.bfloat16)

    smem = pl.BlockSpec(memory_space=pltpu.SMEM)
    hbm = pl.BlockSpec(memory_space=pltpu.HBM)
    shape = (2, tokens, head_dim)
    return pl.pallas_call(
        kernel,
        in_specs=[smem] * 3 + [hbm] * (1 + len(arrays) + 6) + [pl.BlockSpec()] * 2,
        out_specs=[pl.BlockSpec()] * 4,
        out_shape=[
            jax.ShapeDtypeStruct(shape, jnp.bfloat16),
            jax.ShapeDtypeStruct(shape, jnp.bfloat16),
            jax.ShapeDtypeStruct(shape, jnp.float32),
            jax.ShapeDtypeStruct((2, tokens, 128), jnp.float32),
        ],
        scratch_shapes=[
            pltpu.VMEM((2, tokens, width), jnp.bfloat16),
            pltpu.VMEM((2, 4, shard, head_dim), jnp.bfloat16),
            pltpu.VMEM((2, 2, tokens, head_dim), jnp.bfloat16),
            pltpu.VMEM((2, 2, tokens, 2 * head_dim), jnp.bfloat16),
            pltpu.SemaphoreType.DMA((moves,)),
            pltpu.SemaphoreType.DMA((6,)),
        ],
        compiler_params=pltpu.CompilerParams(vmem_limit_bytes=WHOLE),
        cost_estimate=COST,
        name="attend_pair",
    )(at, *limits, own, *arrays, *weights, *rows, bias, gain)


def attend_halo(at, h, limits, query, halo, done, mixed, total):
    _, tokens, head_dim = query.shape
    tiles = limits[0].shape[0]
    tile = tokens // tiles

    def kernel(at_ref, limit0_ref, limit1_ref, q_ref, halo_ref, done_ref, mixed_ref, total_ref, keep_ref, send_ref):
        is_mid = (at_ref[0] == 1) | (at_ref[0] == 2)
        for i in range(tiles):
            here = slice(i * tile, (i + 1) * tile)
            sums, rows = total_ref[0, here, :], mixed_ref[0, here, :]
            for t in range(tiles):
                limit = jnp.where(is_mid, limit0_ref[i, 2 * tiles + t], limit1_ref[i, 2 * tiles + t])
                sums, rows = tile_step(
                    q_ref[0, here, :], halo_ref, t * tile, tile, head_dim, limit, sums, rows
                )
            edge = (rows / jnp.sum(sums, axis=-1, keepdims=True)).astype(jnp.bfloat16)
            outer = done_ref[0, here, :]
            keep_ref[here, :] = jnp.where(is_mid, edge, outer)
            send_ref[here, :] = jnp.where(is_mid, outer, edge)

    smem = pl.BlockSpec(memory_space=pltpu.SMEM)
    one = pl.BlockSpec((1, tokens, head_dim), lambda i: (h, 0, 0))
    fixed = lambda shape: pl.BlockSpec(shape, lambda i: (0,) * len(shape))
    out = jax.ShapeDtypeStruct((tokens, head_dim), jnp.bfloat16)
    return pl.pallas_call(
        kernel,
        grid=(1,),
        in_specs=[smem] * 3 + [one, fixed(halo.shape), one, one, one],
        out_specs=[fixed(out.shape)] * 2,
        out_shape=[out] * 2,
        compiler_params=pltpu.CompilerParams(vmem_limit_bytes=WHOLE),
        cost_estimate=SPACE,
        name="attend_halo",
    )(at, *limits, query, halo, done, mixed, total)


def assemble(at, parts):
    indices, arrays = zip(*parts)
    tokens, head_dim = arrays[0].shape
    rows = tokens // 3

    def kernel(at_ref, *refs):
        for index, ref in zip(indices, refs):
            lanes = pl.ds(pl.multiple_of(at_ref[index] * head_dim, 128), head_dim)
            refs[-1][:, lanes] = ref[...]

    return pl.pallas_call(
        kernel,
        grid=(tokens // rows,),
        in_specs=[pl.BlockSpec(memory_space=pltpu.SMEM)]
        + [pl.BlockSpec((rows, head_dim), lambda i: (i, 0))] * len(arrays),
        out_specs=pl.BlockSpec((rows, head_dim * len(arrays)), lambda i: (i, 0)),
        out_shape=jax.ShapeDtypeStruct((tokens, head_dim * len(arrays)), jnp.bfloat16),
        compiler_params=pltpu.CompilerParams(vmem_limit_bytes=WHOLE),
        cost_estimate=COST,
        name="assemble",
    )(at, *arrays)


def tile_step(query, rows_ref, at, tile, head_dim, limit, total, mixed):
    scale = math.log2(math.e) / math.sqrt(head_dim)
    keys = rows_ref[at : at + tile, :head_dim]
    values = rows_ref[at : at + tile, head_dim:]
    scores = lax.dot_general(
        query, keys, (((1,), (1,)), ((), ())), preferred_element_type=jnp.float32
    )
    weights = jnp.exp2(scores * scale + limit)
    for c in range(tile // 128):
        total = total + weights[:, c * 128 : (c + 1) * 128]
    mixed = mixed + jnp.dot(
        weights.astype(jnp.bfloat16), values, preferred_element_type=jnp.float32
    )
    return total, mixed


def per_device(frames, modulation, w_qkv, b_qkv, qk_gain, block_lists):
    sizes = tuple(lax.axis_size(a) for a in ("groups", "seq", "fsdp", "head"))
    head_dim = qk_gain.shape[1]
    width_cols = w_qkv.shape[2]
    tokens = frames.shape[0]
    if sizes != (2, 4, 2, 2) or width_cols != 4 * head_dim:
        return general(frames, modulation, w_qkv, b_qkv, qk_gain, block_lists)

    y, z, x, core = (lax.axis_index(a).astype(jnp.int32) for a in ("groups", "seq", "fsdp", "head"))
    rows = w_qkv.shape[0]
    quarter = tokens // 4
    tile_dev = block_lists.shape[0]

    def to(axis, value, bit):
        return lax.ppermute(value, axis, [(i, i ^ bit) for i in range(lax.axis_size(axis))])

    side = z % 2
    mine, twin = 2 * side + y, 2 * side + 1 - y
    across = 2 * (1 - side)
    at = jnp.stack([z, 2 * x + core, mine, twin, across + y, across + 1 - y, y, 2 + y])
    MINE, TWIN, CROSS, CROSS_TWIN = 2, 3, 4, 5
    is_mid = (z == 1) | (z == 2)
    w = jnp.transpose(w_qkv, (1, 0, 2))
    line = Line()

    def arrive(value):
        box = line.reached(value)[0]
        (box[0],) = line.after(box[0])
        return box

    cutting = (0, quarter * FIRST // 12, quarter)
    raws = take_rows(at, frames, [hi - lo for lo, hi in zip(cutting, cutting[1:])])
    raws_other = [to("seq", raw, 1) for raw in raws]
    (w, *_) = lax.optimization_barrier((w, *raws))
    same, cross, q_sent = line.reached(
        *cut_heads(at, w, [((MINE,), (1, 2)), ((CROSS,), (1, 2)), ((6, 7, 6, 7), (0,))])
    )
    got = [to("seq", same[0], 2), to("seq", cross[0], 3), to("seq", cross[0], 1)]
    own_limit = line.reached(see(at, block_lists, tile_dev))
    frames, modulation = line.after(frames, modulation)
    own_x = line.reached(normalize(frames, modulation, 128))
    line.drop(cross)

    def take(i):
        (raw,) = line.after(raws_other[i])
        near = line.reached(normalize(raw, modulation, raw.shape[0]))[0]
        return near, to("fsdp", near[0], 1)

    def spread(near, far):
        far = arrive(far)
        both = jnp.concatenate([near[0], far[0]], axis=0)
        return far, to("head", both, 1)

    def swap(which):
        kept = arrive(got[which])
        return kept, to("groups", kept[0], 1)

    near0, far0 = take(0)
    two_mine, two_twin = swap(0)
    near1, far1 = take(1)
    (q_sent[0],) = line.after(q_sent[0])
    q_got = lax.all_to_all(q_sent[0], "seq", split_axis=0, concat_axis=0, tiled=True)
    line.drop(q_sent)
    three_mine, three_twin = swap(1)
    one_mine, one_twin = swap(2)
    (w,) = line.after(w)
    own_kv = [same, line.reached(*cut_heads(at, w, [((TWIN,), (1, 2))], SPACE))[0]]
    far0, core0 = spread(near0, far0)
    two_twin = arrive(two_twin)
    three_twin = arrive(three_twin)
    far1, core1 = spread(near1, far1)
    w_mine = [own_kv[0], one_mine, two_mine, three_mine]

    def kv(head, boxes, own, pieces, own_rows=None):
        (boxes[0][0],) = line.after(boxes[0][0])
        weights = [box[0] for box in boxes]
        return keys_values(at, head, own, pieces, weights, b_qkv, qk_gain, own_rows)

    own_mine = line.reached(*kv(MINE, w_mine, own_x[0][0], None))[0]
    (own_limit[0][0],) = line.after(own_limit[0][0])
    far_limit = to("seq", own_limit[0][0], 1)
    core0 = arrive(core0)
    core1 = arrive(core1)
    n0, n1 = cutting[1], quarter - cutting[1]
    pieces = [
        (near0, [(0, 0, 0, n0)]),
        (far0, [(2, 0, 0, n0)]),
        (core0, [(1, 0, 0, n0), (3, 0, n0, n0)]),
        (near1, [(0, n0, 0, n1)]),
        (far1, [(2, n0, 0, n1)]),
        (core1, [(1, n0, 0, n1), (3, n0, n1, n1)]),
    ]

    def column_arrays():
        return own_x[0][0], [(box[0], parts) for box, parts in pieces]

    far, edge = kv(MINE, w_mine, None, column_arrays()[1], own_mine[0])
    rows_mine, halo_mine = [own_mine, *line.reached(far)], to("seq", edge, 2)
    q_mine = arrive(q_got)
    q_twin = to("groups", q_mine[0], 1)
    one_twin = arrive(one_twin)
    w_twin = [own_kv[1], one_twin, two_twin, three_twin]
    own, far, edge = kv(TWIN, w_twin, *column_arrays())
    rows_twin, halo_twin = line.reached(own, far), to("seq", edge, 2)
    line.drop(*w_mine, *w_twin)
    limits = own_limit + [arrive(far_limit)]
    q_twin = arrive(q_twin)
    parts = line.reached(
        *attend_pair(
            at, [b[0] for b in limits], *column_arrays(), [q_mine[0], q_twin[0]], b_qkv, qk_gain,
            [b[0] for b in (*rows_mine, *rows_twin)],
        )
    )
    line.drop(q_mine, q_twin, *own_x, *(box for box, _ in pieces), *rows_mine, *rows_twin)

    def finish(h, halo):
        (halo,) = line.after(halo)
        query, *rest = [b[0] for b in parts]
        keep, send = attend_halo(at, h, [b[0] for b in limits], query, halo, *rest)
        return line.reached(keep)[0], to("seq", send, 1)

    keep_mine, back_mine = finish(0, halo_mine)
    keep_twin, back_twin = finish(1, halo_twin)
    parts = [(MINE, keep_mine[0]), (TWIN, keep_twin[0]), (CROSS, back_mine), (CROSS_TWIN, back_twin)]
    return assemble(at, parts)


def solution(mesh):
    placed = (
        P(("groups", "seq"), None),
        P("groups", None),
        P("seq", None, ("fsdp", "head")),
        P(None, ("fsdp", "head")),
        P(),
        P(("groups", "seq"), None),
    )
    return jax.shard_map(
        per_device,
        mesh=mesh,
        in_specs=placed,
        out_specs=P(("groups", "seq"), ("fsdp", "head")),
        check_vma=False,
    )
```

```python
import math

import jax
import jax.numpy as jnp
from jax import lax
from jax.experimental import pallas as pl
from jax.experimental.pallas import tpu as pltpu
from jax.sharding import PartitionSpec as P

EPS = 1e-06
VMEM = 28 << 20
WHOLE = 60 << 20
FIRST = 8
HIDDEN = -1e30
SPACE = pl.CostEstimate(flops=1 << 36, bytes_accessed=1 << 10, transcendentals=0)
COST = pl.CostEstimate(flops=1 << 20, bytes_accessed=1 << 10, transcendentals=0)


def with_halo(shard, sides, width):
    for axis, dim in sides:
        devices, length = (lax.axis_size(axis), shard.shape[dim])
        up = [(i, (i + 1) % devices) for i in range(devices - 1)]
        down = [(j, i) for i, j in up]
        last = lax.slice_in_dim(shard, length - width, length, axis=dim)
        first = lax.slice_in_dim(shard, 0, width, axis=dim)
        before = lax.ppermute(last, axis, up)
        after = lax.ppermute(first, axis, down)
        shard = jnp.concatenate([before, shard, after], axis=dim)
    return shard


def normed_heads(tensor, gain_row, head_dim):
    shaped = tensor.reshape(tensor.shape[0], tensor.shape[1] // head_dim, head_dim)
    scaled = (
        shaped * lax.rsqrt(jnp.mean(shaped * shaped, axis=-1, keepdims=True) + EPS) * gain_row
    )
    return scaled.astype(jnp.bfloat16)


def visible_tiles(block_lists):
    position = lax.axis_index("seq")
    tile_dev = block_lists.shape[0]
    candidates = (position - 1) * tile_dev + jnp.arange(3 * tile_dev, dtype=jnp.int32)
    matches = (block_lists[:, :, None] == candidates[None, None, :]) & (
        block_lists[:, :, None] >= 0
    )
    return jnp.any(matches, axis=1)


def general(frames, modulation, w_qkv, b_qkv, qk_gain, block_lists):
    inputs = frames.astype(jnp.float32)
    average = jnp.mean(inputs, axis=-1, keepdims=True)
    centred = inputs - average
    variance = jnp.mean(centred * centred, axis=-1, keepdims=True)
    normed = centred * lax.rsqrt(variance + EPS) * (1.0 + modulation[0]) + modulation[1]
    normed = normed.astype(jnp.bfloat16)
    tokens = normed.shape[0]
    width_cols = w_qkv.shape[2]
    head_dim = qk_gain.shape[1]
    heads = width_cols // head_dim
    projected = jnp.einsum(
        "td,djc->tjc",
        normed,
        lax.all_gather(w_qkv, "seq", axis=0, tiled=True),
        preferred_element_type=jnp.float32,
    )
    projected = projected + b_qkv
    queries = normed_heads(projected[:, 0], qk_gain[0], head_dim)
    key_rows = normed_heads(projected[:, 1], qk_gain[1], head_dim)
    values = projected[:, 2].astype(jnp.bfloat16).reshape(tokens, heads, head_dim)
    stacked = jnp.stack([key_rows, values], axis=0)
    neighbourhood = with_halo(stacked, (("seq", 1),), tokens)
    tile_len = tokens // block_lists.shape[0]
    allowed_keys = jnp.repeat(
        jnp.repeat(visible_tiles(block_lists), tile_len, axis=0), tile_len, axis=1
    )
    factor = 1.0 / math.sqrt(head_dim)
    scores = (
        jnp.einsum("qhd,khd->hqk", queries, neighbourhood[0], preferred_element_type=jnp.float32)
        * factor
    )
    weights = jnp.where(allowed_keys[None, :, :], jnp.exp(scores), 0.0)
    totals = jnp.sum(weights, axis=-1)
    mixture = jnp.einsum(
        "hqk,khd->qhd",
        weights.astype(jnp.bfloat16),
        neighbourhood[1],
        preferred_element_type=jnp.float32,
    )
    result = (mixture / jnp.transpose(totals)[:, :, None]).astype(jnp.bfloat16)
    return result.reshape(tokens, width_cols)


class Line:
    def __init__(self):
        self.held = []

    def reached(self, *values):
        boxes = [[v] for v in values]
        self.held += boxes
        return boxes

    def after(self, *values):
        out = lax.optimization_barrier((*values, *(box[0] for box in self.held)))
        for box, value in zip(self.held, out[len(values) :]):
            box[0] = value
        return out[: len(values)]

    def drop(self, *boxes):
        self.held = [box for box in self.held if all(box is not b for b in boxes)]
        return [box[0] for box in boxes]


def norm_kernel(x_ref, mod_ref, o_ref):
    x = x_ref[...].astype(jnp.float32)
    centred = x - jnp.mean(x, axis=-1, keepdims=True)
    variance = jnp.mean(centred * centred, axis=-1, keepdims=True)
    scaled = centred * lax.rsqrt(variance + EPS) * (1.0 + mod_ref[0:1, :]) + mod_ref[1:2, :]
    o_ref[...] = scaled.astype(jnp.bfloat16)


def normalize(frames, modulation, rows):
    tokens, width = frames.shape
    return pl.pallas_call(
        norm_kernel,
        grid=(tokens // rows,),
        in_specs=[
            pl.BlockSpec((rows, width), lambda i: (i, 0)),
            pl.BlockSpec((2, width), lambda i: (0, 0)),
        ],
        out_specs=pl.BlockSpec((rows, width), lambda i: (i, 0)),
        out_shape=jax.ShapeDtypeStruct((tokens, width), jnp.bfloat16),
        cost_estimate=COST,
        name="normalize",
    )(frames, modulation)


def cut_heads(at, w, groups, cost=None):
    rows = w.shape[1]
    head_dim = 128
    shapes = [(len(indices), rows, head_dim * len(js)) for indices, js in groups]

    def kernel(at_ref, w_ref, *out_refs):
        for (indices, js), ref in zip(groups, out_refs):
            for n, index in enumerate(indices):
                cols = pl.ds(pl.multiple_of(at_ref[index] * head_dim, 128), head_dim)
                for i, j in enumerate(js):
                    ref[n, :, i * head_dim : (i + 1) * head_dim] = w_ref[j, :, cols]

    return pl.pallas_call(
        kernel,
        in_specs=[pl.BlockSpec(memory_space=pltpu.SMEM), pl.BlockSpec()],
        out_specs=[pl.BlockSpec()] * len(groups),
        out_shape=[jax.ShapeDtypeStruct(shape, jnp.bfloat16) for shape in shapes],
        compiler_params=pltpu.CompilerParams(vmem_limit_bytes=VMEM),
        cost_estimate=cost or COST,
        name="cut_heads",
    )(at, w)


def see(at, lists, tile_dev):
    def kernel(at_ref, lists_ref, o_ref):
        lists = lists_ref[...]
        z = at_ref[0]
        lane = lax.broadcasted_iota(jnp.int32, o_ref.shape, 1)
        out = jnp.full(o_ref.shape, HIDDEN, jnp.float32)
        for c, column in enumerate((z, z ^ 1, jnp.where(z < 2, 2, 1))):
            for t in range(tile_dev):
                hit = (lists == column * tile_dev + t).astype(jnp.float32)
                listed = jnp.max(hit, axis=1, keepdims=True) > 0.0
                out = jnp.where((lane == c * tile_dev + t) & listed, 0.0, out)
        o_ref[...] = out

    return pl.pallas_call(
        kernel,
        in_specs=[pl.BlockSpec(memory_space=pltpu.SMEM), pl.BlockSpec()],
        out_specs=pl.BlockSpec(),
        out_shape=jax.ShapeDtypeStruct((lists.shape[0], 128), jnp.float32),
        cost_estimate=COST,
        name="see",
    )(at, lists)


def load_columns(at, own, pieces, x_ref, sems, step):
    count, tokens, _ = x_ref.shape
    copies = ([], [])
    for r in range(0, tokens if own is not None else 0, step):
        copies[0].append((own.at[pl.ds(r, step)], x_ref.at[0, pl.ds(r, step)]))
    for ref, parts in pieces:
        for i, start, first, size in parts:
            row = pl.multiple_of((at[1] ^ i) * (tokens // 4) + start, 16)
            copies[1].append((ref.at[pl.ds(first, size)], x_ref.at[count - 1, pl.ds(row, size)]))
    made, n = ([], []), 0
    for group, out in zip(copies, made):
        for source, target in group:
            out.append(pltpu.make_async_copy(source, target, sems.at[n]))
            n += 1
    return made


def start(copies):
    for copy in copies:
        copy.start()


def start_next(waves, n):
    if n + 1 < len(waves):
        start(waves[n + 1])
    for copy in waves[n]:
        copy.wait()


def normed(value, gain):
    mean = jnp.mean(value * value, axis=-1, keepdims=True)
    return value * lax.rsqrt(mean + EPS) * gain


def keys_values(at, head, own, pieces, weights, bias, gain, own_rows=None):
    _, rows, cols = weights[0].shape
    head_dim = gain.shape[1]
    arrays, parts = zip(*pieces) if pieces else ((), ())
    width = (arrays or (own,))[0].shape[1]
    tokens = own.shape[0] if own is not None else own_rows.shape[0]
    columns = [0] * (own is not None) + [1] * bool(pieces)
    step = 256
    moves = tokens // step + sum(map(len, parts))
    sources = [own] * (own is not None) + list(arrays)
    known = [] if own_rows is None else [own_rows]
    n_out = (own is not None) + 2 * bool(pieces)

    def kernel(at_ref, *refs):
        x_sources, weight_refs = refs[: len(sources)], refs[len(sources) : len(sources) + 4]
        b_ref, g_ref, *rest = refs[len(sources) + 4 :]
        own_in, out_refs = rest[: len(known)], rest[len(known) : len(known) + n_out]
        x_ref, w_ref, x_sems, w_sems = rest[-4:]
        z = at_ref[0]
        is_mid = (z == 1) | (z == 2)
        lanes = pl.ds(pl.multiple_of(at_ref[head] * head_dim, 128), head_dim)
        loads = [
            pltpu.make_async_copy(ref, w_ref.at[pl.ds(s, 1)], w_sems.at[s])
            for s, ref in enumerate(weight_refs)
        ]
        piece_refs = x_sources[len(sources) - len(arrays) :]
        own_moves, far_moves = load_columns(
            at_ref, x_sources[0] if 0 in columns else None, list(zip(piece_refs, parts)), x_ref, x_sems, step
        )
        waves = [[move] for move in own_moves] + [far_moves] * bool(far_moves)
        start([*loads, *waves[0]])
        for copy in loads:
            copy.wait()
        for column in columns:
            if column:
                start_next(waves, len(own_moves))
            out_ref = out_refs[0 if column == 0 else -2]
            for r in range(tokens // step):
                if not column:
                    start_next(waves, r)
                here = slice(r * step, (r + 1) * step)
                total = None
                for s in range(4):
                    first = pl.multiple_of((z ^ s) * rows, 128)
                    product = jnp.dot(
                        x_ref[columns.index(column), here, pl.ds(first, rows)], w_ref[s],
                        preferred_element_type=jnp.float32,
                    )
                    total = product if total is None else total + product
                key = normed(total[:, :head_dim] + b_ref[1:2, lanes], g_ref[1:2, :])
                out_ref[here, :head_dim] = key.astype(jnp.bfloat16)
                value = total[:, head_dim:] + b_ref[2:3, lanes]
                out_ref[here, head_dim:] = value.astype(jnp.bfloat16)
                if column:
                    own_ref = own_in[0] if known else out_refs[0]
                    out_refs[-1][here, :] = jnp.where(is_mid, own_ref[here, :], out_ref[here, :])

    hbm = pl.BlockSpec(memory_space=pltpu.HBM)
    out = jax.ShapeDtypeStruct((tokens, cols), jnp.bfloat16)
    return pl.pallas_call(
        kernel,
        in_specs=[pl.BlockSpec(memory_space=pltpu.SMEM)]
        + [hbm] * (len(sources) + 4)
        + [pl.BlockSpec()] * (2 + len(known)),
        out_specs=[pl.BlockSpec()] * n_out,
        out_shape=[out] * n_out,
        scratch_shapes=[
            pltpu.VMEM((len(columns), tokens, width), jnp.bfloat16),
            pltpu.VMEM((4, rows, cols), jnp.bfloat16),
            pltpu.SemaphoreType.DMA((moves,)),
            pltpu.SemaphoreType.DMA((4,)),
        ],
        compiler_params=pltpu.CompilerParams(vmem_limit_bytes=WHOLE),
        cost_estimate=SPACE,
        name="keys_values",
    )(at, *sources, *weights, bias, gain, *known)


def take_rows(at, frames, sizes):
    width = frames.shape[1]
    quarter = sum(sizes)

    def kernel(at_ref, x_ref, *out_refs):
        first = 0
        for ref in out_refs:
            ref[...] = x_ref[first : first + ref.shape[0], :]
            first += ref.shape[0]

    return pl.pallas_call(
        kernel,
        grid_spec=pltpu.PrefetchScalarGridSpec(
            num_scalar_prefetch=1,
            grid=(1,),
            in_specs=[pl.BlockSpec((quarter, width), lambda i, at: (at[1], 0))],
            out_specs=[pl.BlockSpec((size, width), lambda i, at: (0, 0)) for size in sizes],
        ),
        out_shape=[jax.ShapeDtypeStruct((size, width), jnp.bfloat16) for size in sizes],
        cost_estimate=COST,
        name="take_rows",
    )(at, frames)


def attend_pair(at, limits, own, pieces, weights, bias, gain, rows):
    tokens, width = own.shape
    head_dim = gain.shape[1]
    tiles = limits[0].shape[0]
    tile = tokens // tiles
    arrays, parts = zip(*pieces)
    step = 256
    moves = tokens // step + sum(map(len, parts))
    shard = weights[0].shape[1]

    def kernel(at_ref, limit0_ref, limit1_ref, own_ref, *refs):
        piece_refs, weight_refs = refs[: len(arrays)], refs[len(arrays) : len(arrays) + 2]
        row_refs = refs[len(arrays) + 2 : len(arrays) + 6]
        (b_ref, g_ref, edge_ref, done_ref, mixed_ref, total_ref,
         x_ref, w_ref, q_ref, kv_ref, x_sems, w_sems) = refs[len(arrays) + 6 :]
        z = at_ref[0]
        is_mid = (z == 1) | (z == 2)
        loads = [
            pltpu.make_async_copy(ref, w_ref.at[h], w_sems.at[h])
            for h, ref in enumerate(weight_refs)
        ]
        own_moves, far_moves = load_columns(at_ref, own_ref, list(zip(piece_refs, parts)), x_ref, x_sems, step)
        late = [
            pltpu.make_async_copy(ref, kv_ref.at[n // 2, n % 2], w_sems.at[2 + n])
            for n, ref in enumerate(row_refs)
        ]
        waves = [[move] for move in own_moves] + [far_moves, late]
        start([*loads, *waves[0]])
        for copy in loads:
            copy.wait()
        for column in range(2):
            if column:
                start_next(waves, len(own_moves))
            for r in range(tokens // step):
                if not column:
                    start_next(waves, r)
                here = slice(r * step, (r + 1) * step)
                total = None
                for s in range(4):
                    product = jnp.dot(
                        x_ref[column, here, s * shard : (s + 1) * shard],
                        jnp.concatenate([w_ref[0, s], w_ref[1, s]], axis=1),
                        preferred_element_type=jnp.float32,
                    )
                    total = product if total is None else total + product
                for h in range(2):
                    lanes = pl.ds(pl.multiple_of(at_ref[2 + h] * head_dim, 128), head_dim)
                    value = total[:, h * head_dim : (h + 1) * head_dim] + b_ref[0:1, lanes]
                    q_ref[h, column, here, :] = normed(value, g_ref[0:1, :]).astype(jnp.bfloat16)
        for copy in late:
            copy.wait()

        @pl.loop(0, 2)
        def _(h):
            for column in range(2):
                is_edge = is_mid if column == 0 else jnp.logical_not(is_mid)
                for i in range(tiles):
                    here = slice(i * tile, (i + 1) * tile)
                    query = q_ref[h, column, here, :]
                    total = jnp.zeros((tile, 128), jnp.float32)
                    mixed = jnp.zeros((tile, head_dim), jnp.float32)
                    for other in range(2):
                        limits_ref = (limit0_ref, limit1_ref)[column]
                        seen = [limits_ref[i, (other ^ column) * tiles + t] for t in range(tiles)]
                        total, mixed = column_step(
                            query, kv_ref.at[h, other], tile, head_dim, seen, total, mixed
                        )

                    @pl.when(is_edge)
                    def _():
                        edge_ref[h, here, :] = query
                        mixed_ref[h, here, :] = mixed
                        total_ref[h, here, :] = total

                    @pl.when(jnp.logical_not(is_edge))
                    def _():
                        rows = mixed / jnp.sum(total, axis=-1, keepdims=True)
                        done_ref[h, here, :] = rows.astype(jnp.bfloat16)

    smem = pl.BlockSpec(memory_space=pltpu.SMEM)
    hbm = pl.BlockSpec(memory_space=pltpu.HBM)
    shape = (2, tokens, head_dim)
    return pl.pallas_call(
        kernel,
        in_specs=[smem] * 3 + [hbm] * (1 + len(arrays) + 6) + [pl.BlockSpec()] * 2,
        out_specs=[pl.BlockSpec()] * 4,
        out_shape=[
            jax.ShapeDtypeStruct(shape, jnp.bfloat16),
            jax.ShapeDtypeStruct(shape, jnp.bfloat16),
            jax.ShapeDtypeStruct(shape, jnp.float32),
            jax.ShapeDtypeStruct((2, tokens, 128), jnp.float32),
        ],
        scratch_shapes=[
            pltpu.VMEM((2, tokens, width), jnp.bfloat16),
            pltpu.VMEM((2, 4, shard, head_dim), jnp.bfloat16),
            pltpu.VMEM((2, 2, tokens, head_dim), jnp.bfloat16),
            pltpu.VMEM((2, 2, tokens, 2 * head_dim), jnp.bfloat16),
            pltpu.SemaphoreType.DMA((moves,)),
            pltpu.SemaphoreType.DMA((6,)),
        ],
        compiler_params=pltpu.CompilerParams(vmem_limit_bytes=WHOLE),
        cost_estimate=COST,
        name="attend_pair",
    )(at, *limits, own, *arrays, *weights, *rows, bias, gain)


def attend_halo(at, h, limits, query, halo, done, mixed, total):
    _, tokens, head_dim = query.shape
    tiles = limits[0].shape[0]
    tile = tokens // tiles

    def kernel(at_ref, limit0_ref, limit1_ref, q_ref, halo_ref, done_ref, mixed_ref, total_ref, keep_ref, send_ref):
        is_mid = (at_ref[0] == 1) | (at_ref[0] == 2)
        for i in range(tiles):
            here = slice(i * tile, (i + 1) * tile)
            sums, rows = total_ref[0, here, :], mixed_ref[0, here, :]
            seen = [
                jnp.where(is_mid, limit0_ref[i, 2 * tiles + t], limit1_ref[i, 2 * tiles + t])
                for t in range(tiles)
            ]
            sums, rows = column_step(q_ref[0, here, :], halo_ref, tile, head_dim, seen, sums, rows)
            edge = (rows / jnp.sum(sums, axis=-1, keepdims=True)).astype(jnp.bfloat16)
            outer = done_ref[0, here, :]
            keep_ref[here, :] = jnp.where(is_mid, edge, outer)
            send_ref[here, :] = jnp.where(is_mid, outer, edge)

    smem = pl.BlockSpec(memory_space=pltpu.SMEM)
    one = pl.BlockSpec((1, tokens, head_dim), lambda i: (h, 0, 0))
    fixed = lambda shape: pl.BlockSpec(shape, lambda i: (0,) * len(shape))
    out = jax.ShapeDtypeStruct((tokens, head_dim), jnp.bfloat16)
    return pl.pallas_call(
        kernel,
        grid=(1,),
        in_specs=[smem] * 3 + [one, fixed(halo.shape), one, one, one],
        out_specs=[fixed(out.shape)] * 2,
        out_shape=[out] * 2,
        compiler_params=pltpu.CompilerParams(vmem_limit_bytes=WHOLE),
        cost_estimate=SPACE,
        name="attend_halo",
    )(at, *limits, query, halo, done, mixed, total)


def assemble(at, parts):
    indices, arrays = zip(*parts)
    tokens, head_dim = arrays[0].shape
    rows = tokens // 3

    def kernel(at_ref, *refs):
        for index, ref in zip(indices, refs):
            lanes = pl.ds(pl.multiple_of(at_ref[index] * head_dim, 128), head_dim)
            refs[-1][:, lanes] = ref[...]

    return pl.pallas_call(
        kernel,
        grid=(tokens // rows,),
        in_specs=[pl.BlockSpec(memory_space=pltpu.SMEM)]
        + [pl.BlockSpec((rows, head_dim), lambda i: (i, 0))] * len(arrays),
        out_specs=pl.BlockSpec((rows, head_dim * len(arrays)), lambda i: (i, 0)),
        out_shape=jax.ShapeDtypeStruct((tokens, head_dim * len(arrays)), jnp.bfloat16),
        compiler_params=pltpu.CompilerParams(vmem_limit_bytes=WHOLE),
        cost_estimate=COST,
        name="assemble",
    )(at, *arrays)


def column_step(query, rows_ref, tile, head_dim, limits, total, mixed):
    scale = math.log2(math.e) / math.sqrt(head_dim)
    scores = lax.dot_general(
        query, rows_ref[:, :head_dim], (((1,), (1,)), ((), ())), preferred_element_type=jnp.float32
    )
    rounded = []
    for t, limit in enumerate(limits):
        weights = jnp.exp2(scores[:, t * tile : (t + 1) * tile] * scale + limit)
        for c in range(tile // 128):
            total = total + weights[:, c * 128 : (c + 1) * 128]
        rounded.append(weights.astype(jnp.bfloat16))
    mixed = mixed + jnp.dot(
        jnp.concatenate(rounded, axis=1), rows_ref[:, head_dim:], preferred_element_type=jnp.float32
    )
    return total, mixed


def per_device(frames, modulation, w_qkv, b_qkv, qk_gain, block_lists):
    sizes = tuple(lax.axis_size(a) for a in ("groups", "seq", "fsdp", "head"))
    head_dim = qk_gain.shape[1]
    width_cols = w_qkv.shape[2]
    tokens = frames.shape[0]
    if sizes != (2, 4, 2, 2) or width_cols != 4 * head_dim:
        return general(frames, modulation, w_qkv, b_qkv, qk_gain, block_lists)

    y, z, x, core = (lax.axis_index(a).astype(jnp.int32) for a in ("groups", "seq", "fsdp", "head"))
    rows = w_qkv.shape[0]
    quarter = tokens // 4
    tile_dev = block_lists.shape[0]

    def to(axis, value, bit):
        return lax.ppermute(value, axis, [(i, i ^ bit) for i in range(lax.axis_size(axis))])

    side = z % 2
    mine, twin = 2 * side + y, 2 * side + 1 - y
    across = 2 * (1 - side)
    at = jnp.stack([z, 2 * x + core, mine, twin, across + y, across + 1 - y, y, 2 + y])
    MINE, TWIN, CROSS, CROSS_TWIN = 2, 3, 4, 5
    is_mid = (z == 1) | (z == 2)
    w = jnp.transpose(w_qkv, (1, 0, 2))
    line = Line()

    def arrive(value):
        box = line.reached(value)[0]
        (box[0],) = line.after(box[0])
        return box

    cutting = (0, quarter * FIRST // 12, quarter)
    raws = take_rows(at, frames, [hi - lo for lo, hi in zip(cutting, cutting[1:])])
    raws_other = [to("seq", raw, 1) for raw in raws]
    (w, *_) = lax.optimization_barrier((w, *raws))
    same, cross, q_sent = line.reached(
        *cut_heads(at, w, [((MINE,), (1, 2)), ((CROSS,), (1, 2)), ((6, 7, 6, 7), (0,))])
    )
    got = [to("seq", same[0], 2), to("seq", cross[0], 3), to("seq", cross[0], 1)]
    own_limit = line.reached(see(at, block_lists, tile_dev))
    frames, modulation = line.after(frames, modulation)
    own_x = line.reached(normalize(frames, modulation, 128))
    line.drop(cross)

    def take(i):
        (raw,) = line.after(raws_other[i])
        near = line.reached(normalize(raw, modulation, raw.shape[0]))[0]
        return near, to("fsdp", near[0], 1)

    def spread(near, far):
        far = arrive(far)
        both = jnp.concatenate([near[0], far[0]], axis=0)
        return far, to("head", both, 1)

    def swap(which):
        kept = arrive(got[which])
        return kept, to("groups", kept[0], 1)

    (q_sent[0],) = line.after(q_sent[0])
    q_got = lax.all_to_all(q_sent[0], "seq", split_axis=0, concat_axis=0, tiled=True)
    line.drop(q_sent)
    near0, far0 = take(0)
    two_mine, two_twin = swap(0)
    near1, far1 = take(1)
    three_mine, three_twin = swap(1)
    one_mine, one_twin = swap(2)
    (w,) = line.after(w)
    own_kv = [same, line.reached(*cut_heads(at, w, [((TWIN,), (1, 2))], SPACE))[0]]
    far0, core0 = spread(near0, far0)
    two_twin = arrive(two_twin)
    three_twin = arrive(three_twin)
    far1, core1 = spread(near1, far1)
    q_mine = arrive(q_got)
    q_twin = to("groups", q_mine[0], 1)
    w_mine = [own_kv[0], one_mine, two_mine, three_mine]

    def kv(head, boxes, own, pieces, own_rows=None):
        (boxes[0][0],) = line.after(boxes[0][0])
        weights = [box[0] for box in boxes]
        return keys_values(at, head, own, pieces, weights, b_qkv, qk_gain, own_rows)

    own_mine = line.reached(*kv(MINE, w_mine, own_x[0][0], None))[0]
    (own_limit[0][0],) = line.after(own_limit[0][0])
    far_limit = to("seq", own_limit[0][0], 1)
    core0 = arrive(core0)
    core1 = arrive(core1)
    n0, n1 = cutting[1], quarter - cutting[1]
    pieces = [
        (near0, [(0, 0, 0, n0)]),
        (far0, [(2, 0, 0, n0)]),
        (core0, [(1, 0, 0, n0), (3, 0, n0, n0)]),
        (near1, [(0, n0, 0, n1)]),
        (far1, [(2, n0, 0, n1)]),
        (core1, [(1, n0, 0, n1), (3, n0, n1, n1)]),
    ]

    def column_arrays():
        return own_x[0][0], [(box[0], parts) for box, parts in pieces]

    far, edge = kv(MINE, w_mine, None, column_arrays()[1], own_mine[0])
    rows_mine, halo_mine = [own_mine, *line.reached(far)], to("seq", edge, 2)
    one_twin = arrive(one_twin)
    w_twin = [own_kv[1], one_twin, two_twin, three_twin]
    own, far, edge = kv(TWIN, w_twin, *column_arrays())
    rows_twin, halo_twin = line.reached(own, far), to("seq", edge, 2)
    line.drop(*w_mine, *w_twin)
    limits = own_limit + [arrive(far_limit)]
    q_twin = arrive(q_twin)
    parts = line.reached(
        *attend_pair(
            at, [b[0] for b in limits], *column_arrays(), [q_mine[0], q_twin[0]], b_qkv, qk_gain,
            [b[0] for b in (*rows_mine, *rows_twin)],
        )
    )
    line.drop(q_mine, q_twin, *own_x, *(box for box, _ in pieces), *rows_mine, *rows_twin)

    def finish(h, halo):
        (halo,) = line.after(halo)
        query, *rest = [b[0] for b in parts]
        keep, send = attend_halo(at, h, [b[0] for b in limits], query, halo, *rest)
        return line.reached(keep)[0], to("seq", send, 1)

    keep_mine, back_mine = finish(0, halo_mine)
    keep_twin, back_twin = finish(1, halo_twin)
    parts = [(MINE, keep_mine[0]), (TWIN, keep_twin[0]), (CROSS, back_mine), (CROSS_TWIN, back_twin)]
    return assemble(at, parts)


def solution(mesh):
    placed = (
        P(("groups", "seq"), None),
        P("groups", None),
        P("seq", None, ("fsdp", "head")),
        P(None, ("fsdp", "head")),
        P(),
        P(("groups", "seq"), None),
    )
    return jax.shard_map(
        per_device,
        mesh=mesh,
        in_specs=placed,
        out_specs=P(("groups", "seq"), ("fsdp", "head")),
        check_vma=False,
    )
```

```python
import math

import jax
import jax.numpy as jnp
from jax import lax
from jax.experimental import pallas as pl
from jax.experimental.pallas import tpu as pltpu
from jax.sharding import PartitionSpec as P

EPS = 1e-06
VMEM = 28 << 20
WHOLE = 60 << 20
FIRST = 8
HIDDEN = -1e30
SPACE = pl.CostEstimate(flops=1 << 36, bytes_accessed=1 << 10, transcendentals=0)
COST = pl.CostEstimate(flops=1 << 20, bytes_accessed=1 << 10, transcendentals=0)


def with_halo(shard, sides, width):
    for axis, dim in sides:
        devices, length = (lax.axis_size(axis), shard.shape[dim])
        up = [(i, (i + 1) % devices) for i in range(devices - 1)]
        down = [(j, i) for i, j in up]
        last = lax.slice_in_dim(shard, length - width, length, axis=dim)
        first = lax.slice_in_dim(shard, 0, width, axis=dim)
        before = lax.ppermute(last, axis, up)
        after = lax.ppermute(first, axis, down)
        shard = jnp.concatenate([before, shard, after], axis=dim)
    return shard


def normed_heads(tensor, gain_row, head_dim):
    shaped = tensor.reshape(tensor.shape[0], tensor.shape[1] // head_dim, head_dim)
    scaled = (
        shaped * lax.rsqrt(jnp.mean(shaped * shaped, axis=-1, keepdims=True) + EPS) * gain_row
    )
    return scaled.astype(jnp.bfloat16)


def visible_tiles(block_lists):
    position = lax.axis_index("seq")
    tile_dev = block_lists.shape[0]
    candidates = (position - 1) * tile_dev + jnp.arange(3 * tile_dev, dtype=jnp.int32)
    matches = (block_lists[:, :, None] == candidates[None, None, :]) & (
        block_lists[:, :, None] >= 0
    )
    return jnp.any(matches, axis=1)


def general(frames, modulation, w_qkv, b_qkv, qk_gain, block_lists):
    inputs = frames.astype(jnp.float32)
    average = jnp.mean(inputs, axis=-1, keepdims=True)
    centred = inputs - average
    variance = jnp.mean(centred * centred, axis=-1, keepdims=True)
    normed = centred * lax.rsqrt(variance + EPS) * (1.0 + modulation[0]) + modulation[1]
    normed = normed.astype(jnp.bfloat16)
    tokens = normed.shape[0]
    width_cols = w_qkv.shape[2]
    head_dim = qk_gain.shape[1]
    heads = width_cols // head_dim
    projected = jnp.einsum(
        "td,djc->tjc",
        normed,
        lax.all_gather(w_qkv, "seq", axis=0, tiled=True),
        preferred_element_type=jnp.float32,
    )
    projected = projected + b_qkv
    queries = normed_heads(projected[:, 0], qk_gain[0], head_dim)
    key_rows = normed_heads(projected[:, 1], qk_gain[1], head_dim)
    values = projected[:, 2].astype(jnp.bfloat16).reshape(tokens, heads, head_dim)
    stacked = jnp.stack([key_rows, values], axis=0)
    neighbourhood = with_halo(stacked, (("seq", 1),), tokens)
    tile_len = tokens // block_lists.shape[0]
    allowed_keys = jnp.repeat(
        jnp.repeat(visible_tiles(block_lists), tile_len, axis=0), tile_len, axis=1
    )
    factor = 1.0 / math.sqrt(head_dim)
    scores = (
        jnp.einsum("qhd,khd->hqk", queries, neighbourhood[0], preferred_element_type=jnp.float32)
        * factor
    )
    weights = jnp.where(allowed_keys[None, :, :], jnp.exp(scores), 0.0)
    totals = jnp.sum(weights, axis=-1)
    mixture = jnp.einsum(
        "hqk,khd->qhd",
        weights.astype(jnp.bfloat16),
        neighbourhood[1],
        preferred_element_type=jnp.float32,
    )
    result = (mixture / jnp.transpose(totals)[:, :, None]).astype(jnp.bfloat16)
    return result.reshape(tokens, width_cols)


class Line:
    def __init__(self):
        self.held = []

    def reached(self, *values):
        boxes = [[v] for v in values]
        self.held += boxes
        return boxes

    def after(self, *values):
        out = lax.optimization_barrier((*values, *(box[0] for box in self.held)))
        for box, value in zip(self.held, out[len(values) :]):
            box[0] = value
        return out[: len(values)]

    def drop(self, *boxes):
        self.held = [box for box in self.held if all(box is not b for b in boxes)]
        return [box[0] for box in boxes]


def norm_kernel(x_ref, mod_ref, o_ref):
    x = x_ref[...].astype(jnp.float32)
    centred = x - jnp.mean(x, axis=-1, keepdims=True)
    variance = jnp.mean(centred * centred, axis=-1, keepdims=True)
    scaled = centred * lax.rsqrt(variance + EPS) * (1.0 + mod_ref[0:1, :]) + mod_ref[1:2, :]
    o_ref[...] = scaled.astype(jnp.bfloat16)


def normalize(frames, modulation, rows):
    tokens, width = frames.shape
    return pl.pallas_call(
        norm_kernel,
        grid=(tokens // rows,),
        in_specs=[
            pl.BlockSpec((rows, width), lambda i: (i, 0)),
            pl.BlockSpec((2, width), lambda i: (0, 0)),
        ],
        out_specs=pl.BlockSpec((rows, width), lambda i: (i, 0)),
        out_shape=jax.ShapeDtypeStruct((tokens, width), jnp.bfloat16),
        cost_estimate=COST,
        name="normalize",
    )(frames, modulation)


def cut_heads(at, w, groups, cost=None):
    rows = w.shape[1]
    head_dim = 128
    shapes = [(len(indices), rows, head_dim * len(js)) for indices, js in groups]

    def kernel(at_ref, w_ref, *out_refs):
        for (indices, js), ref in zip(groups, out_refs):
            for n, index in enumerate(indices):
                cols = pl.ds(pl.multiple_of(at_ref[index] * head_dim, 128), head_dim)
                for i, j in enumerate(js):
                    ref[n, :, i * head_dim : (i + 1) * head_dim] = w_ref[j, :, cols]

    return pl.pallas_call(
        kernel,
        in_specs=[pl.BlockSpec(memory_space=pltpu.SMEM), pl.BlockSpec()],
        out_specs=[pl.BlockSpec()] * len(groups),
        out_shape=[jax.ShapeDtypeStruct(shape, jnp.bfloat16) for shape in shapes],
        compiler_params=pltpu.CompilerParams(vmem_limit_bytes=VMEM),
        cost_estimate=cost or COST,
        name="cut_heads",
    )(at, w)


def see(at, lists, tile_dev):
    def kernel(at_ref, lists_ref, o_ref):
        lists = lists_ref[...]
        z = at_ref[0]
        lane = lax.broadcasted_iota(jnp.int32, o_ref.shape, 1)
        out = jnp.full(o_ref.shape, HIDDEN, jnp.float32)
        for c, column in enumerate((z, z ^ 1, jnp.where(z < 2, 2, 1))):
            for t in range(tile_dev):
                hit = (lists == column * tile_dev + t).astype(jnp.float32)
                listed = jnp.max(hit, axis=1, keepdims=True) > 0.0
                out = jnp.where((lane == c * tile_dev + t) & listed, 0.0, out)
        o_ref[...] = out

    return pl.pallas_call(
        kernel,
        in_specs=[pl.BlockSpec(memory_space=pltpu.SMEM), pl.BlockSpec()],
        out_specs=pl.BlockSpec(),
        out_shape=jax.ShapeDtypeStruct((lists.shape[0], 128), jnp.float32),
        cost_estimate=COST,
        name="see",
    )(at, lists)


def load_columns(at, own, pieces, x_ref, sems, step):
    count, tokens, _ = x_ref.shape
    copies = ([], [])
    for r in range(0, tokens if own is not None else 0, step):
        copies[0].append((own.at[pl.ds(r, step)], x_ref.at[0, pl.ds(r, step)]))
    for ref, parts in pieces:
        for i, start, first, size in parts:
            row = pl.multiple_of((at[1] ^ i) * (tokens // 4) + start, 16)
            copies[1].append((ref.at[pl.ds(first, size)], x_ref.at[count - 1, pl.ds(row, size)]))
    made, n = ([], []), 0
    for group, out in zip(copies, made):
        for source, target in group:
            out.append(pltpu.make_async_copy(source, target, sems.at[n]))
            n += 1
    return made


def start(copies):
    for copy in copies:
        copy.start()


def start_next(waves, n):
    if n + 1 < len(waves):
        start(waves[n + 1])
    for copy in waves[n]:
        copy.wait()


def normed(value, gain):
    mean = jnp.mean(value * value, axis=-1, keepdims=True)
    return value * lax.rsqrt(mean + EPS) * gain


def keys_values(at, head, own, pieces, weights, bias, gain, own_rows=None, query_weights=()):
    _, rows, cols = weights[0].shape
    head_dim = gain.shape[1]
    arrays, parts = zip(*pieces) if pieces else ((), ())
    width = (arrays or (own,))[0].shape[1]
    tokens = own.shape[0] if own is not None else own_rows.shape[0]
    columns = [0] * (own is not None) + [1] * bool(pieces)
    step = 256
    moves = tokens // step + sum(map(len, parts))
    sources = [own] * (own is not None) + list(arrays)
    known = [] if own_rows is None else [own_rows]
    n_out = (own is not None) + 2 * bool(pieces)
    queries = list(query_weights)

    def kernel(at_ref, *refs):
        x_sources, weight_refs = refs[: len(sources)], refs[len(sources) : len(sources) + 4]
        query_refs = refs[len(sources) + 4 : len(sources) + 4 + len(queries)]
        b_ref, g_ref, *rest = refs[len(sources) + 4 + len(queries) :]
        q_ref = rest[len(known) + n_out] if queries else None
        own_in, out_refs = rest[: len(known)], rest[len(known) : len(known) + n_out]
        x_ref, w_ref, wq_ref, x_sems, w_sems = rest[-5:]
        z = at_ref[0]
        is_mid = (z == 1) | (z == 2)
        lanes = pl.ds(pl.multiple_of(at_ref[head] * head_dim, 128), head_dim)
        loads = [
            pltpu.make_async_copy(ref, w_ref.at[pl.ds(s, 1)], w_sems.at[s])
            for s, ref in enumerate(weight_refs)
        ]
        loads += [
            pltpu.make_async_copy(ref, wq_ref.at[h], w_sems.at[4 + h])
            for h, ref in enumerate(query_refs)
        ]
        piece_refs = x_sources[len(sources) - len(arrays) :]
        own_moves, far_moves = load_columns(
            at_ref, x_sources[0] if 0 in columns else None, list(zip(piece_refs, parts)), x_ref, x_sems, step
        )
        waves = [[move] for move in own_moves] + [far_moves] * bool(far_moves)
        start([*loads, *waves[0]])
        for copy in loads:
            copy.wait()
        for column in columns:
            if column:
                start_next(waves, len(own_moves))
            out_ref = out_refs[0 if column == 0 else -2]
            for r in range(tokens // step):
                if not column:
                    start_next(waves, r)
                here = slice(r * step, (r + 1) * step)
                total = None
                for s in range(4):
                    first = pl.multiple_of((z ^ s) * rows, 128)
                    product = jnp.dot(
                        x_ref[columns.index(column), here, pl.ds(first, rows)], w_ref[s],
                        preferred_element_type=jnp.float32,
                    )
                    total = product if total is None else total + product
                key = normed(total[:, :head_dim] + b_ref[1:2, lanes], g_ref[1:2, :])
                out_ref[here, :head_dim] = key.astype(jnp.bfloat16)
                value = total[:, head_dim:] + b_ref[2:3, lanes]
                out_ref[here, head_dim:] = value.astype(jnp.bfloat16)
                if queries:
                    total = None
                    for s in range(4):
                        product = jnp.dot(
                            x_ref[columns.index(column), here, s * rows : (s + 1) * rows],
                            jnp.concatenate([wq_ref[0, s], wq_ref[1, s]], axis=1),
                            preferred_element_type=jnp.float32,
                        )
                        total = product if total is None else total + product
                    for h in range(2):
                        head_lanes = pl.ds(pl.multiple_of(at_ref[2 + h] * head_dim, 128), head_dim)
                        query = total[:, h * head_dim : (h + 1) * head_dim] + b_ref[0:1, head_lanes]
                        query = normed(query, g_ref[0:1, :])
                        q_ref[h, column, here, :] = query.astype(jnp.bfloat16)
                if column:
                    own_ref = own_in[0] if known else out_refs[0]
                    out_refs[-1][here, :] = jnp.where(is_mid, own_ref[here, :], out_ref[here, :])

    hbm = pl.BlockSpec(memory_space=pltpu.HBM)
    out = jax.ShapeDtypeStruct((tokens, cols), jnp.bfloat16)
    return pl.pallas_call(
        kernel,
        in_specs=[pl.BlockSpec(memory_space=pltpu.SMEM)]
        + [hbm] * (len(sources) + 4 + len(queries))
        + [pl.BlockSpec()] * (2 + len(known)),
        out_specs=[pl.BlockSpec()] * (n_out + bool(queries)),
        out_shape=[out] * n_out
        + [jax.ShapeDtypeStruct((2, 2, tokens, head_dim), jnp.bfloat16)] * bool(queries),
        scratch_shapes=[
            pltpu.VMEM((len(columns), tokens, width), jnp.bfloat16),
            pltpu.VMEM((4, rows, cols), jnp.bfloat16),
            pltpu.VMEM((2, 4, rows, head_dim) if queries else (8, 128), jnp.bfloat16),
            pltpu.SemaphoreType.DMA((moves,)),
            pltpu.SemaphoreType.DMA((4 + len(queries),)),
        ],
        compiler_params=pltpu.CompilerParams(vmem_limit_bytes=WHOLE),
        cost_estimate=SPACE,
        name="keys_values",
    )(at, *sources, *weights, *queries, bias, gain, *known)


def take_rows(at, frames, sizes):
    width = frames.shape[1]
    quarter = sum(sizes)

    def kernel(at_ref, x_ref, *out_refs):
        first = 0
        for ref in out_refs:
            ref[...] = x_ref[first : first + ref.shape[0], :]
            first += ref.shape[0]

    return pl.pallas_call(
        kernel,
        grid_spec=pltpu.PrefetchScalarGridSpec(
            num_scalar_prefetch=1,
            grid=(1,),
            in_specs=[pl.BlockSpec((quarter, width), lambda i, at: (at[1], 0))],
            out_specs=[pl.BlockSpec((size, width), lambda i, at: (0, 0)) for size in sizes],
        ),
        out_shape=[jax.ShapeDtypeStruct((size, width), jnp.bfloat16) for size in sizes],
        cost_estimate=COST,
        name="take_rows",
    )(at, frames)


def attend_pair(at, limits, queries, rows):
    _, _, tokens, head_dim = queries.shape
    tiles = limits[0].shape[0]
    tile = tokens // tiles

    def kernel(at_ref, limit0_ref, limit1_ref, query_ref, *refs):
        row_refs = refs[:4]
        edge_ref, done_ref, mixed_ref, total_ref, q_ref, kv_ref, sems = refs[4:]
        z = at_ref[0]
        is_mid = (z == 1) | (z == 2)
        copies = [pltpu.make_async_copy(query_ref, q_ref, sems.at[4])]
        for n, ref in enumerate(row_refs):
            copies.append(pltpu.make_async_copy(ref, kv_ref.at[n // 2, n % 2], sems.at[n]))
        start(copies)
        for copy in copies:
            copy.wait()

        @pl.loop(0, 2)
        def _(h):
            for column in range(2):
                is_edge = is_mid if column == 0 else jnp.logical_not(is_mid)
                for i in range(tiles):
                    here = slice(i * tile, (i + 1) * tile)
                    query = q_ref[h, column, here, :]
                    total = jnp.zeros((tile, 128), jnp.float32)
                    mixed = jnp.zeros((tile, head_dim), jnp.float32)
                    for other in range(2):
                        for t in range(tiles):
                            limit = (limit0_ref, limit1_ref)[column][i, (other ^ column) * tiles + t]
                            total, mixed = column_step(
                                query, kv_ref.at[h, other, t * tile : (t + 1) * tile], tile,
                                head_dim, [limit], total, mixed,
                            )

                    @pl.when(is_edge)
                    def _():
                        edge_ref[h, here, :] = query
                        mixed_ref[h, here, :] = mixed
                        total_ref[h, here, :] = total

                    @pl.when(jnp.logical_not(is_edge))
                    def _():
                        rows = mixed / jnp.sum(total, axis=-1, keepdims=True)
                        done_ref[h, here, :] = rows.astype(jnp.bfloat16)

    smem = pl.BlockSpec(memory_space=pltpu.SMEM)
    hbm = pl.BlockSpec(memory_space=pltpu.HBM)
    shape = (2, tokens, head_dim)
    return pl.pallas_call(
        kernel,
        in_specs=[smem] * 3 + [hbm] * 5,
        out_specs=[pl.BlockSpec()] * 4,
        out_shape=[
            jax.ShapeDtypeStruct(shape, jnp.bfloat16),
            jax.ShapeDtypeStruct(shape, jnp.bfloat16),
            jax.ShapeDtypeStruct(shape, jnp.float32),
            jax.ShapeDtypeStruct((2, tokens, 128), jnp.float32),
        ],
        scratch_shapes=[
            pltpu.VMEM((2, 2, tokens, head_dim), jnp.bfloat16),
            pltpu.VMEM((2, 2, tokens, 2 * head_dim), jnp.bfloat16),
            pltpu.SemaphoreType.DMA((5,)),
        ],
        compiler_params=pltpu.CompilerParams(vmem_limit_bytes=WHOLE),
        cost_estimate=COST,
        name="attend_pair",
    )(at, *limits, queries, *rows)


def attend_halo(at, h, limits, query, halo, done, mixed, total):
    _, tokens, head_dim = query.shape
    tiles = limits[0].shape[0]
    tile = tokens // tiles

    def kernel(at_ref, limit0_ref, limit1_ref, q_ref, halo_ref, done_ref, mixed_ref, total_ref, keep_ref, send_ref):
        is_mid = (at_ref[0] == 1) | (at_ref[0] == 2)
        for i in range(tiles):
            here = slice(i * tile, (i + 1) * tile)
            sums, rows = total_ref[0, here, :], mixed_ref[0, here, :]
            seen = [
                jnp.where(is_mid, limit0_ref[i, 2 * tiles + t], limit1_ref[i, 2 * tiles + t])
                for t in range(tiles)
            ]
            sums, rows = column_step(q_ref[0, here, :], halo_ref, tile, head_dim, seen, sums, rows)
            edge = (rows / jnp.sum(sums, axis=-1, keepdims=True)).astype(jnp.bfloat16)
            outer = done_ref[0, here, :]
            keep_ref[here, :] = jnp.where(is_mid, edge, outer)
            send_ref[here, :] = jnp.where(is_mid, outer, edge)

    smem = pl.BlockSpec(memory_space=pltpu.SMEM)
    one = pl.BlockSpec((1, tokens, head_dim), lambda i: (h, 0, 0))
    fixed = lambda shape: pl.BlockSpec(shape, lambda i: (0,) * len(shape))
    out = jax.ShapeDtypeStruct((tokens, head_dim), jnp.bfloat16)
    return pl.pallas_call(
        kernel,
        grid=(1,),
        in_specs=[smem] * 3 + [one, fixed(halo.shape), one, one, one],
        out_specs=[fixed(out.shape)] * 2,
        out_shape=[out] * 2,
        compiler_params=pltpu.CompilerParams(vmem_limit_bytes=WHOLE),
        cost_estimate=SPACE,
        name="attend_halo",
    )(at, *limits, query, halo, done, mixed, total)


def assemble(at, parts):
    indices, arrays = zip(*parts)
    tokens, head_dim = arrays[0].shape
    rows = tokens // 3

    def kernel(at_ref, *refs):
        for index, ref in zip(indices, refs):
            lanes = pl.ds(pl.multiple_of(at_ref[index] * head_dim, 128), head_dim)
            refs[-1][:, lanes] = ref[...]

    return pl.pallas_call(
        kernel,
        grid=(tokens // rows,),
        in_specs=[pl.BlockSpec(memory_space=pltpu.SMEM)]
        + [pl.BlockSpec((rows, head_dim), lambda i: (i, 0))] * len(arrays),
        out_specs=pl.BlockSpec((rows, head_dim * len(arrays)), lambda i: (i, 0)),
        out_shape=jax.ShapeDtypeStruct((tokens, head_dim * len(arrays)), jnp.bfloat16),
        compiler_params=pltpu.CompilerParams(vmem_limit_bytes=WHOLE),
        cost_estimate=COST,
        name="assemble",
    )(at, *arrays)


def column_step(query, rows_ref, tile, head_dim, limits, total, mixed):
    scale = math.log2(math.e) / math.sqrt(head_dim)
    scores = lax.dot_general(
        query, rows_ref[:, :head_dim], (((1,), (1,)), ((), ())), preferred_element_type=jnp.float32
    )
    rounded = []
    for t, limit in enumerate(limits):
        weights = jnp.exp2(scores[:, t * tile : (t + 1) * tile] * scale + limit)
        for c in range(tile // 128):
            total = total + weights[:, c * 128 : (c + 1) * 128]
        rounded.append(weights.astype(jnp.bfloat16))
    mixed = mixed + jnp.dot(
        jnp.concatenate(rounded, axis=1), rows_ref[:, head_dim:], preferred_element_type=jnp.float32
    )
    return total, mixed


def per_device(frames, modulation, w_qkv, b_qkv, qk_gain, block_lists):
    sizes = tuple(lax.axis_size(a) for a in ("groups", "seq", "fsdp", "head"))
    head_dim = qk_gain.shape[1]
    width_cols = w_qkv.shape[2]
    tokens = frames.shape[0]
    if sizes != (2, 4, 2, 2) or width_cols != 4 * head_dim:
        return general(frames, modulation, w_qkv, b_qkv, qk_gain, block_lists)

    y, z, x, core = (lax.axis_index(a).astype(jnp.int32) for a in ("groups", "seq", "fsdp", "head"))
    rows = w_qkv.shape[0]
    quarter = tokens // 4
    tile_dev = block_lists.shape[0]

    def to(axis, value, bit):
        return lax.ppermute(value, axis, [(i, i ^ bit) for i in range(lax.axis_size(axis))])

    side = z % 2
    mine, twin = 2 * side + y, 2 * side + 1 - y
    across = 2 * (1 - side)
    at = jnp.stack([z, 2 * x + core, mine, twin, across + y, across + 1 - y, y, 2 + y])
    MINE, TWIN, CROSS, CROSS_TWIN = 2, 3, 4, 5
    is_mid = (z == 1) | (z == 2)
    w = jnp.transpose(w_qkv, (1, 0, 2))
    line = Line()

    def arrive(value):
        box = line.reached(value)[0]
        (box[0],) = line.after(box[0])
        return box

    cutting = (0, quarter * FIRST // 12, quarter)
    raws = take_rows(at, frames, [hi - lo for lo, hi in zip(cutting, cutting[1:])])
    raws_other = [to("seq", raw, 1) for raw in raws]
    (w, *_) = lax.optimization_barrier((w, *raws))
    same, cross, q_sent = line.reached(
        *cut_heads(at, w, [((MINE,), (1, 2)), ((CROSS,), (1, 2)), ((6, 7, 6, 7), (0,))])
    )
    got = [to("seq", same[0], 2), to("seq", cross[0], 3), to("seq", cross[0], 1)]
    own_limit = line.reached(see(at, block_lists, tile_dev))
    frames, modulation = line.after(frames, modulation)
    own_x = line.reached(normalize(frames, modulation, 128))
    line.drop(cross)

    def take(i):
        (raw,) = line.after(raws_other[i])
        near = line.reached(normalize(raw, modulation, raw.shape[0]))[0]
        return near, to("fsdp", near[0], 1)

    def spread(near, far):
        far = arrive(far)
        both = jnp.concatenate([near[0], far[0]], axis=0)
        return far, to("head", both, 1)

    def swap(which):
        kept = arrive(got[which])
        return kept, to("groups", kept[0], 1)

    near0, far0 = take(0)
    two_mine, two_twin = swap(0)
    near1, far1 = take(1)
    (q_sent[0],) = line.after(q_sent[0])
    q_got = lax.all_to_all(q_sent[0], "seq", split_axis=0, concat_axis=0, tiled=True)
    line.drop(q_sent)
    far0, core0 = spread(near0, far0)
    three_mine, three_twin = swap(1)
    one_mine, one_twin = swap(2)
    (w,) = line.after(w)
    own_kv = [same, line.reached(*cut_heads(at, w, [((TWIN,), (1, 2))], SPACE))[0]]
    two_twin = arrive(two_twin)
    three_twin = arrive(three_twin)
    far1, core1 = spread(near1, far1)
    q_mine = arrive(q_got)
    q_twin = to("groups", q_mine[0], 1)
    w_mine = [own_kv[0], one_mine, two_mine, three_mine]

    def kv(head, boxes, own, pieces, own_rows=None, query_weights=()):
        (boxes[0][0],) = line.after(boxes[0][0])
        weights = [box[0] for box in boxes]
        return keys_values(at, head, own, pieces, weights, b_qkv, qk_gain, own_rows, query_weights)

    own_mine = line.reached(*kv(MINE, w_mine, own_x[0][0], None))[0]
    (own_limit[0][0],) = line.after(own_limit[0][0])
    far_limit = to("seq", own_limit[0][0], 1)
    core0 = arrive(core0)
    core1 = arrive(core1)
    n0, n1 = cutting[1], quarter - cutting[1]
    pieces = [
        (near0, [(0, 0, 0, n0)]),
        (far0, [(2, 0, 0, n0)]),
        (core0, [(1, 0, 0, n0), (3, 0, n0, n0)]),
        (near1, [(0, n0, 0, n1)]),
        (far1, [(2, n0, 0, n1)]),
        (core1, [(1, n0, 0, n1), (3, n0, n1, n1)]),
    ]

    def column_arrays():
        return own_x[0][0], [(box[0], parts) for box, parts in pieces]

    far, edge = kv(MINE, w_mine, None, column_arrays()[1], own_mine[0])
    rows_mine, halo_mine = [own_mine, *line.reached(far)], to("seq", edge, 2)
    one_twin = arrive(one_twin)
    q_twin = arrive(q_twin)
    w_twin = [own_kv[1], one_twin, two_twin, three_twin]
    own, far, edge, queries = kv(TWIN, w_twin, *column_arrays(), None, (q_mine[0], q_twin[0]))
    rows_twin, halo_twin = line.reached(own, far), to("seq", edge, 2)
    line.drop(*w_mine, *w_twin, q_mine, q_twin, *own_x, *(box for box, _ in pieces))
    limits = own_limit + [arrive(far_limit)]
    rows = [b[0] for b in (*rows_mine, *rows_twin)]
    parts = line.reached(*attend_pair(at, [b[0] for b in limits], queries, rows))
    line.drop(*rows_mine, *rows_twin)

    def finish(h, halo):
        (halo,) = line.after(halo)
        query, *rest = [b[0] for b in parts]
        keep, send = attend_halo(at, h, [b[0] for b in limits], query, halo, *rest)
        return line.reached(keep)[0], to("seq", send, 1)

    keep_mine, back_mine = finish(0, halo_mine)
    keep_twin, back_twin = finish(1, halo_twin)
    parts = [(MINE, keep_mine[0]), (TWIN, keep_twin[0]), (CROSS, back_mine), (CROSS_TWIN, back_twin)]
    return assemble(at, parts)


def solution(mesh):
    placed = (
        P(("groups", "seq"), None),
        P("groups", None),
        P("seq", None, ("fsdp", "head")),
        P(None, ("fsdp", "head")),
        P(),
        P(("groups", "seq"), None),
    )
    return jax.shard_map(
        per_device,
        mesh=mesh,
        in_specs=placed,
        out_specs=P(("groups", "seq"), ("fsdp", "head")),
        check_vma=False,
    )
```

```python
import math

import jax
import jax.numpy as jnp
from jax import lax
from jax.experimental import pallas as pl
from jax.experimental.pallas import tpu as pltpu
from jax.sharding import PartitionSpec as P

EPS = 1e-06
VMEM = 28 << 20
WHOLE = 60 << 20
FIRST = 8
HIDDEN = -1e30
SPACE = pl.CostEstimate(flops=1 << 36, bytes_accessed=1 << 10, transcendentals=0)
COST = pl.CostEstimate(flops=1 << 20, bytes_accessed=1 << 10, transcendentals=0)


def with_halo(shard, sides, width):
    for axis, dim in sides:
        devices, length = (lax.axis_size(axis), shard.shape[dim])
        up = [(i, (i + 1) % devices) for i in range(devices - 1)]
        down = [(j, i) for i, j in up]
        last = lax.slice_in_dim(shard, length - width, length, axis=dim)
        first = lax.slice_in_dim(shard, 0, width, axis=dim)
        before = lax.ppermute(last, axis, up)
        after = lax.ppermute(first, axis, down)
        shard = jnp.concatenate([before, shard, after], axis=dim)
    return shard


def normed_heads(tensor, gain_row, head_dim):
    shaped = tensor.reshape(tensor.shape[0], tensor.shape[1] // head_dim, head_dim)
    scaled = (
        shaped * lax.rsqrt(jnp.mean(shaped * shaped, axis=-1, keepdims=True) + EPS) * gain_row
    )
    return scaled.astype(jnp.bfloat16)


def visible_tiles(block_lists):
    position = lax.axis_index("seq")
    tile_dev = block_lists.shape[0]
    candidates = (position - 1) * tile_dev + jnp.arange(3 * tile_dev, dtype=jnp.int32)
    matches = (block_lists[:, :, None] == candidates[None, None, :]) & (
        block_lists[:, :, None] >= 0
    )
    return jnp.any(matches, axis=1)


def general(frames, modulation, w_qkv, b_qkv, qk_gain, block_lists):
    inputs = frames.astype(jnp.float32)
    average = jnp.mean(inputs, axis=-1, keepdims=True)
    centred = inputs - average
    variance = jnp.mean(centred * centred, axis=-1, keepdims=True)
    normed = centred * lax.rsqrt(variance + EPS) * (1.0 + modulation[0]) + modulation[1]
    normed = normed.astype(jnp.bfloat16)
    tokens = normed.shape[0]
    width_cols = w_qkv.shape[2]
    head_dim = qk_gain.shape[1]
    heads = width_cols // head_dim
    projected = jnp.einsum(
        "td,djc->tjc",
        normed,
        lax.all_gather(w_qkv, "seq", axis=0, tiled=True),
        preferred_element_type=jnp.float32,
    )
    projected = projected + b_qkv
    queries = normed_heads(projected[:, 0], qk_gain[0], head_dim)
    key_rows = normed_heads(projected[:, 1], qk_gain[1], head_dim)
    values = projected[:, 2].astype(jnp.bfloat16).reshape(tokens, heads, head_dim)
    stacked = jnp.stack([key_rows, values], axis=0)
    neighbourhood = with_halo(stacked, (("seq", 1),), tokens)
    tile_len = tokens // block_lists.shape[0]
    allowed_keys = jnp.repeat(
        jnp.repeat(visible_tiles(block_lists), tile_len, axis=0), tile_len, axis=1
    )
    factor = 1.0 / math.sqrt(head_dim)
    scores = (
        jnp.einsum("qhd,khd->hqk", queries, neighbourhood[0], preferred_element_type=jnp.float32)
        * factor
    )
    weights = jnp.where(allowed_keys[None, :, :], jnp.exp(scores), 0.0)
    totals = jnp.sum(weights, axis=-1)
    mixture = jnp.einsum(
        "hqk,khd->qhd",
        weights.astype(jnp.bfloat16),
        neighbourhood[1],
        preferred_element_type=jnp.float32,
    )
    result = (mixture / jnp.transpose(totals)[:, :, None]).astype(jnp.bfloat16)
    return result.reshape(tokens, width_cols)


class Line:
    def __init__(self):
        self.held = []

    def reached(self, *values):
        boxes = [[v] for v in values]
        self.held += boxes
        return boxes

    def after(self, *values):
        out = lax.optimization_barrier((*values, *(box[0] for box in self.held)))
        for box, value in zip(self.held, out[len(values) :]):
            box[0] = value
        return out[: len(values)]

    def drop(self, *boxes):
        self.held = [box for box in self.held if all(box is not b for b in boxes)]
        return [box[0] for box in boxes]


def norm_kernel(x_ref, mod_ref, o_ref):
    x = x_ref[...].astype(jnp.float32)
    centred = x - jnp.mean(x, axis=-1, keepdims=True)
    variance = jnp.mean(centred * centred, axis=-1, keepdims=True)
    scaled = centred * lax.rsqrt(variance + EPS) * (1.0 + mod_ref[0:1, :]) + mod_ref[1:2, :]
    o_ref[...] = scaled.astype(jnp.bfloat16)


def normalize(frames, modulation, rows):
    tokens, width = frames.shape
    return pl.pallas_call(
        norm_kernel,
        grid=(tokens // rows,),
        in_specs=[
            pl.BlockSpec((rows, width), lambda i: (i, 0)),
            pl.BlockSpec((2, width), lambda i: (0, 0)),
        ],
        out_specs=pl.BlockSpec((rows, width), lambda i: (i, 0)),
        out_shape=jax.ShapeDtypeStruct((tokens, width), jnp.bfloat16),
        cost_estimate=COST,
        name="normalize",
    )(frames, modulation)


def cut_heads(at, w, groups, cost=None):
    rows = w.shape[1]
    head_dim = 128
    shapes = [(len(indices), rows, head_dim * len(js)) for indices, js in groups]

    def kernel(at_ref, w_ref, *out_refs):
        for (indices, js), ref in zip(groups, out_refs):
            for n, index in enumerate(indices):
                cols = pl.ds(pl.multiple_of(at_ref[index] * head_dim, 128), head_dim)
                for i, j in enumerate(js):
                    ref[n, :, i * head_dim : (i + 1) * head_dim] = w_ref[j, :, cols]

    return pl.pallas_call(
        kernel,
        in_specs=[pl.BlockSpec(memory_space=pltpu.SMEM), pl.BlockSpec()],
        out_specs=[pl.BlockSpec()] * len(groups),
        out_shape=[jax.ShapeDtypeStruct(shape, jnp.bfloat16) for shape in shapes],
        compiler_params=pltpu.CompilerParams(vmem_limit_bytes=VMEM),
        cost_estimate=cost or COST,
        name="cut_heads",
    )(at, w)


def see(at, lists, tile_dev):
    def kernel(at_ref, lists_ref, o_ref):
        lists = lists_ref[...]
        z = at_ref[0]
        lane = lax.broadcasted_iota(jnp.int32, o_ref.shape, 1)
        out = jnp.full(o_ref.shape, HIDDEN, jnp.float32)
        for c, column in enumerate((z, z ^ 1, jnp.where(z < 2, 2, 1))):
            for t in range(tile_dev):
                hit = (lists == column * tile_dev + t).astype(jnp.float32)
                listed = jnp.max(hit, axis=1, keepdims=True) > 0.0
                out = jnp.where((lane == c * tile_dev + t) & listed, 0.0, out)
        o_ref[...] = out

    return pl.pallas_call(
        kernel,
        in_specs=[pl.BlockSpec(memory_space=pltpu.SMEM), pl.BlockSpec()],
        out_specs=pl.BlockSpec(),
        out_shape=jax.ShapeDtypeStruct((lists.shape[0], 128), jnp.float32),
        cost_estimate=COST,
        name="see",
    )(at, lists)


def load_columns(at, own, pieces, x_ref, sems, step):
    count, tokens, _ = x_ref.shape
    copies = ([], [])
    for r in range(0, tokens if own is not None else 0, step):
        copies[0].append((own.at[pl.ds(r, step)], x_ref.at[0, pl.ds(r, step)]))
    for ref, parts in pieces:
        for i, start, first, size in parts:
            row = pl.multiple_of((at[1] ^ i) * (tokens // 4) + start, 16)
            copies[1].append((ref.at[pl.ds(first, size)], x_ref.at[count - 1, pl.ds(row, size)]))
    made, n = ([], []), 0
    for group, out in zip(copies, made):
        for source, target in group:
            out.append(pltpu.make_async_copy(source, target, sems.at[n]))
            n += 1
    return made


def start(copies):
    for copy in copies:
        copy.start()


def start_next(waves, n):
    if n + 1 < len(waves):
        start(waves[n + 1])
    for copy in waves[n]:
        copy.wait()


def normed(value, gain):
    mean = jnp.mean(value * value, axis=-1, keepdims=True)
    return value * lax.rsqrt(mean + EPS) * gain


def keys_values(at, head, own, pieces, weights, bias, gain, own_rows=None, query_weights=()):
    _, rows, cols = weights[0].shape
    head_dim = gain.shape[1]
    arrays, parts = zip(*pieces) if pieces else ((), ())
    width = (arrays or (own,))[0].shape[1]
    tokens = own.shape[0] if own is not None else own_rows.shape[0]
    columns = [0] * (own is not None) + [1] * bool(pieces)
    step = 256
    moves = tokens // step + sum(map(len, parts))
    sources = [own] * (own is not None) + list(arrays)
    known = [] if own_rows is None else [own_rows]
    n_out = (own is not None) + 2 * bool(pieces)
    queries = list(query_weights)

    def kernel(at_ref, *refs):
        x_sources, weight_refs = refs[: len(sources)], refs[len(sources) : len(sources) + 4]
        query_refs = refs[len(sources) + 4 : len(sources) + 4 + len(queries)]
        b_ref, g_ref, *rest = refs[len(sources) + 4 + len(queries) :]
        q_ref = rest[len(known) + n_out] if queries else None
        own_in, out_refs = rest[: len(known)], rest[len(known) : len(known) + n_out]
        x_ref, w_ref, wq_ref, x_sems, w_sems = rest[-5:]
        z = at_ref[0]
        is_mid = (z == 1) | (z == 2)
        lanes = pl.ds(pl.multiple_of(at_ref[head] * head_dim, 128), head_dim)
        loads = [
            pltpu.make_async_copy(ref, w_ref.at[pl.ds(s, 1)], w_sems.at[s])
            for s, ref in enumerate(weight_refs)
        ]
        loads += [
            pltpu.make_async_copy(ref, wq_ref.at[h], w_sems.at[4 + h])
            for h, ref in enumerate(query_refs)
        ]
        piece_refs = x_sources[len(sources) - len(arrays) :]
        own_moves, far_moves = load_columns(
            at_ref, x_sources[0] if 0 in columns else None, list(zip(piece_refs, parts)), x_ref, x_sems, step
        )
        waves = [[move] for move in own_moves] + [far_moves] * bool(far_moves)
        start([*loads, *waves[0]])
        for copy in loads:
            copy.wait()
        for column in columns:
            if column:
                start_next(waves, len(own_moves))
            out_ref = out_refs[0 if column == 0 else -2]
            for r in range(tokens // step):
                if not column:
                    start_next(waves, r)
                here = slice(r * step, (r + 1) * step)
                total = None
                for s in range(4):
                    first = pl.multiple_of((z ^ s) * rows, 128)
                    product = jnp.dot(
                        x_ref[columns.index(column), here, pl.ds(first, rows)], w_ref[s],
                        preferred_element_type=jnp.float32,
                    )
                    total = product if total is None else total + product
                key = normed(total[:, :head_dim] + b_ref[1:2, lanes], g_ref[1:2, :])
                out_ref[here, :head_dim] = key.astype(jnp.bfloat16)
                value = total[:, head_dim:] + b_ref[2:3, lanes]
                out_ref[here, head_dim:] = value.astype(jnp.bfloat16)
                if queries:
                    total = None
                    for s in range(4):
                        product = jnp.dot(
                            x_ref[columns.index(column), here, s * rows : (s + 1) * rows],
                            jnp.concatenate([wq_ref[0, s], wq_ref[1, s]], axis=1),
                            preferred_element_type=jnp.float32,
                        )
                        total = product if total is None else total + product
                    for h in range(2):
                        head_lanes = pl.ds(pl.multiple_of(at_ref[2 + h] * head_dim, 128), head_dim)
                        query = total[:, h * head_dim : (h + 1) * head_dim] + b_ref[0:1, head_lanes]
                        query = normed(query, g_ref[0:1, :])
                        q_ref[h, column, here, :] = query.astype(jnp.bfloat16)
                if column:
                    own_ref = own_in[0] if known else out_refs[0]
                    out_refs[-1][here, :] = jnp.where(is_mid, own_ref[here, :], out_ref[here, :])

    hbm = pl.BlockSpec(memory_space=pltpu.HBM)
    out = jax.ShapeDtypeStruct((tokens, cols), jnp.bfloat16)
    return pl.pallas_call(
        kernel,
        in_specs=[pl.BlockSpec(memory_space=pltpu.SMEM)]
        + [hbm] * (len(sources) + 4 + len(queries))
        + [pl.BlockSpec()] * (2 + len(known)),
        out_specs=[pl.BlockSpec()] * (n_out + bool(queries)),
        out_shape=[out] * n_out
        + [jax.ShapeDtypeStruct((2, 2, tokens, head_dim), jnp.bfloat16)] * bool(queries),
        scratch_shapes=[
            pltpu.VMEM((len(columns), tokens, width), jnp.bfloat16),
            pltpu.VMEM((4, rows, cols), jnp.bfloat16),
            pltpu.VMEM((2, 4, rows, head_dim) if queries else (8, 128), jnp.bfloat16),
            pltpu.SemaphoreType.DMA((moves,)),
            pltpu.SemaphoreType.DMA((4 + len(queries),)),
        ],
        compiler_params=pltpu.CompilerParams(vmem_limit_bytes=WHOLE),
        cost_estimate=SPACE,
        name="keys_values",
    )(at, *sources, *weights, *queries, bias, gain, *known)


def take_rows(at, frames, sizes):
    width = frames.shape[1]
    quarter = sum(sizes)

    def kernel(at_ref, x_ref, *out_refs):
        first = 0
        for ref in out_refs:
            ref[...] = x_ref[first : first + ref.shape[0], :]
            first += ref.shape[0]

    return pl.pallas_call(
        kernel,
        grid_spec=pltpu.PrefetchScalarGridSpec(
            num_scalar_prefetch=1,
            grid=(1,),
            in_specs=[pl.BlockSpec((quarter, width), lambda i, at: (at[1], 0))],
            out_specs=[pl.BlockSpec((size, width), lambda i, at: (0, 0)) for size in sizes],
        ),
        out_shape=[jax.ShapeDtypeStruct((size, width), jnp.bfloat16) for size in sizes],
        cost_estimate=COST,
        name="take_rows",
    )(at, frames)


def attend_pair(at, limits, queries, rows):
    _, _, tokens, head_dim = queries.shape
    tiles = limits[0].shape[0]
    tile = tokens // tiles

    def kernel(at_ref, limit0_ref, limit1_ref, query_ref, *refs):
        row_refs = refs[:4]
        edge_ref, done_ref, mixed_ref, total_ref, q_ref, kv_ref, sems = refs[4:]
        z = at_ref[0]
        is_mid = (z == 1) | (z == 2)
        copies = [pltpu.make_async_copy(query_ref, q_ref, sems.at[4])]
        for n, ref in enumerate(row_refs):
            copies.append(pltpu.make_async_copy(ref, kv_ref.at[n // 2, n % 2], sems.at[n]))
        start(copies)
        for copy in copies:
            copy.wait()

        @pl.loop(0, 2)
        def _(h):
            for column in range(2):
                is_edge = is_mid if column == 0 else jnp.logical_not(is_mid)
                for i in range(tiles):
                    here = slice(i * tile, (i + 1) * tile)
                    query = q_ref[h, column, here, :]
                    total = jnp.zeros((tile, 128), jnp.float32)
                    mixed = jnp.zeros((tile, head_dim), jnp.float32)
                    for other in range(2):
                        for t in range(tiles):
                            limit = (limit0_ref, limit1_ref)[column][i, (other ^ column) * tiles + t]
                            total, mixed = column_step(
                                query, kv_ref.at[h, other, t * tile : (t + 1) * tile], tile,
                                head_dim, [limit], total, mixed,
                            )

                    @pl.when(is_edge)
                    def _():
                        edge_ref[h, here, :] = query
                        mixed_ref[h, here, :] = mixed
                        total_ref[h, here, :] = total

                    @pl.when(jnp.logical_not(is_edge))
                    def _():
                        rows = mixed / jnp.sum(total, axis=-1, keepdims=True)
                        done_ref[h, here, :] = rows.astype(jnp.bfloat16)

    smem = pl.BlockSpec(memory_space=pltpu.SMEM)
    hbm = pl.BlockSpec(memory_space=pltpu.HBM)
    shape = (2, tokens, head_dim)
    return pl.pallas_call(
        kernel,
        in_specs=[smem] * 3 + [hbm] * 5,
        out_specs=[pl.BlockSpec()] * 4,
        out_shape=[
            jax.ShapeDtypeStruct(shape, jnp.bfloat16),
            jax.ShapeDtypeStruct(shape, jnp.bfloat16),
            jax.ShapeDtypeStruct(shape, jnp.float32),
            jax.ShapeDtypeStruct((2, tokens, 128), jnp.float32),
        ],
        scratch_shapes=[
            pltpu.VMEM((2, 2, tokens, head_dim), jnp.bfloat16),
            pltpu.VMEM((2, 2, tokens, 2 * head_dim), jnp.bfloat16),
            pltpu.SemaphoreType.DMA((5,)),
        ],
        compiler_params=pltpu.CompilerParams(vmem_limit_bytes=WHOLE),
        cost_estimate=COST,
        name="attend_pair",
    )(at, *limits, queries, *rows)


def attend_halo(at, h, limits, query, halo, done, mixed, total):
    _, tokens, head_dim = query.shape
    tiles = limits[0].shape[0]
    tile = tokens // tiles

    def kernel(at_ref, limit0_ref, limit1_ref, q_ref, halo_ref, done_ref, mixed_ref, total_ref, keep_ref, send_ref):
        is_mid = (at_ref[0] == 1) | (at_ref[0] == 2)
        for i in range(tiles):
            here = slice(i * tile, (i + 1) * tile)
            sums, rows = total_ref[0, here, :], mixed_ref[0, here, :]
            seen = [
                jnp.where(is_mid, limit0_ref[i, 2 * tiles + t], limit1_ref[i, 2 * tiles + t])
                for t in range(tiles)
            ]
            sums, rows = column_step(q_ref[0, here, :], halo_ref, tile, head_dim, seen, sums, rows)
            edge = (rows / jnp.sum(sums, axis=-1, keepdims=True)).astype(jnp.bfloat16)
            outer = done_ref[0, here, :]
            keep_ref[here, :] = jnp.where(is_mid, edge, outer)
            send_ref[here, :] = jnp.where(is_mid, outer, edge)

    smem = pl.BlockSpec(memory_space=pltpu.SMEM)
    one = pl.BlockSpec((1, tokens, head_dim), lambda i: (h, 0, 0))
    fixed = lambda shape: pl.BlockSpec(shape, lambda i: (0,) * len(shape))
    out = jax.ShapeDtypeStruct((tokens, head_dim), jnp.bfloat16)
    return pl.pallas_call(
        kernel,
        grid=(1,),
        in_specs=[smem] * 3 + [one, fixed(halo.shape), one, one, one],
        out_specs=[fixed(out.shape)] * 2,
        out_shape=[out] * 2,
        compiler_params=pltpu.CompilerParams(vmem_limit_bytes=WHOLE),
        cost_estimate=SPACE,
        name="attend_halo",
    )(at, *limits, query, halo, done, mixed, total)


def assemble(at, parts):
    indices, arrays = zip(*parts)
    tokens, head_dim = arrays[0].shape
    rows = tokens // 3

    def kernel(at_ref, *refs):
        for index, ref in zip(indices, refs):
            lanes = pl.ds(pl.multiple_of(at_ref[index] * head_dim, 128), head_dim)
            refs[-1][:, lanes] = ref[...]

    return pl.pallas_call(
        kernel,
        grid=(tokens // rows,),
        in_specs=[pl.BlockSpec(memory_space=pltpu.SMEM)]
        + [pl.BlockSpec((rows, head_dim), lambda i: (i, 0))] * len(arrays),
        out_specs=pl.BlockSpec((rows, head_dim * len(arrays)), lambda i: (i, 0)),
        out_shape=jax.ShapeDtypeStruct((tokens, head_dim * len(arrays)), jnp.bfloat16),
        compiler_params=pltpu.CompilerParams(vmem_limit_bytes=WHOLE),
        cost_estimate=COST,
        name="assemble",
    )(at, *arrays)


def column_step(query, rows_ref, tile, head_dim, limits, total, mixed):
    scale = math.log2(math.e) / math.sqrt(head_dim)
    scores = lax.dot_general(
        query, rows_ref[:, :head_dim], (((1,), (1,)), ((), ())), preferred_element_type=jnp.float32
    )
    rounded = []
    for t, limit in enumerate(limits):
        weights = jnp.exp2(scores[:, t * tile : (t + 1) * tile] * scale + limit)
        for c in range(tile // 128):
            total = total + weights[:, c * 128 : (c + 1) * 128]
        rounded.append(weights.astype(jnp.bfloat16))
    mixed = mixed + jnp.dot(
        jnp.concatenate(rounded, axis=1), rows_ref[:, head_dim:], preferred_element_type=jnp.float32
    )
    return total, mixed


def per_device(frames, modulation, w_qkv, b_qkv, qk_gain, block_lists):
    sizes = tuple(lax.axis_size(a) for a in ("groups", "seq", "fsdp", "head"))
    head_dim = qk_gain.shape[1]
    width_cols = w_qkv.shape[2]
    tokens = frames.shape[0]
    if sizes != (2, 4, 2, 2) or width_cols != 4 * head_dim:
        return general(frames, modulation, w_qkv, b_qkv, qk_gain, block_lists)

    y, z, x, core = (lax.axis_index(a).astype(jnp.int32) for a in ("groups", "seq", "fsdp", "head"))
    rows = w_qkv.shape[0]
    quarter = tokens // 4
    tile_dev = block_lists.shape[0]

    def to(axis, value, bit):
        return lax.ppermute(value, axis, [(i, i ^ bit) for i in range(lax.axis_size(axis))])

    side = z % 2
    mine, twin = 2 * side + y, 2 * side + 1 - y
    across = 2 * (1 - side)
    at = jnp.stack([z, 2 * x + core, mine, twin, across + y, across + 1 - y, y, 2 + y])
    MINE, TWIN, CROSS, CROSS_TWIN = 2, 3, 4, 5
    is_mid = (z == 1) | (z == 2)
    w = jnp.transpose(w_qkv, (1, 0, 2))
    line = Line()

    def arrive(value):
        box = line.reached(value)[0]
        (box[0],) = line.after(box[0])
        return box

    cutting = (0, quarter * FIRST // 12, quarter)
    raws = take_rows(at, frames, [hi - lo for lo, hi in zip(cutting, cutting[1:])])
    raws_other = [to("seq", raw, 1) for raw in raws]
    (w, *_) = lax.optimization_barrier((w, *raws))
    same, cross, q_sent = line.reached(
        *cut_heads(at, w, [((MINE,), (1, 2)), ((CROSS,), (1, 2)), ((6, 7, 6, 7), (0,))])
    )
    got = [to("seq", same[0], 2), to("seq", cross[0], 3), to("seq", cross[0], 1)]
    own_limit = line.reached(see(at, block_lists, tile_dev))
    frames, modulation = line.after(frames, modulation)
    own_x = line.reached(normalize(frames, modulation, 128))
    line.drop(cross)

    def take(i):
        (raw,) = line.after(raws_other[i])
        near = line.reached(normalize(raw, modulation, raw.shape[0]))[0]
        return near, to("fsdp", near[0], 1)

    def spread(near, far):
        far = arrive(far)
        both = jnp.concatenate([near[0], far[0]], axis=0)
        return far, to("head", both, 1)

    def swap(which):
        kept = arrive(got[which])
        return kept, to("groups", kept[0], 1)

    (q_sent[0],) = line.after(q_sent[0])
    q_got = lax.all_to_all(q_sent[0], "seq", split_axis=0, concat_axis=0, tiled=True)
    line.drop(q_sent)
    near0, far0 = take(0)
    two_mine, two_twin = swap(0)
    near1, far1 = take(1)
    three_mine, three_twin = swap(1)
    one_mine, one_twin = swap(2)
    (w,) = line.after(w)
    own_kv = [same, line.reached(*cut_heads(at, w, [((TWIN,), (1, 2))], SPACE))[0]]
    far0, core0 = spread(near0, far0)
    two_twin = arrive(two_twin)
    three_twin = arrive(three_twin)
    far1, core1 = spread(near1, far1)
    q_mine = arrive(q_got)
    q_twin = to("groups", q_mine[0], 1)
    w_mine = [own_kv[0], one_mine, two_mine, three_mine]

    def kv(head, boxes, own, pieces, own_rows=None, query_weights=()):
        (boxes[0][0],) = line.after(boxes[0][0])
        weights = [box[0] for box in boxes]
        return keys_values(at, head, own, pieces, weights, b_qkv, qk_gain, own_rows, query_weights)

    own_mine = line.reached(*kv(MINE, w_mine, own_x[0][0], None))[0]
    (own_limit[0][0],) = line.after(own_limit[0][0])
    far_limit = to("seq", own_limit[0][0], 1)
    core0 = arrive(core0)
    core1 = arrive(core1)
    n0, n1 = cutting[1], quarter - cutting[1]
    pieces = [
        (near0, [(0, 0, 0, n0)]),
        (far0, [(2, 0, 0, n0)]),
        (core0, [(1, 0, 0, n0), (3, 0, n0, n0)]),
        (near1, [(0, n0, 0, n1)]),
        (far1, [(2, n0, 0, n1)]),
        (core1, [(1, n0, 0, n1), (3, n0, n1, n1)]),
    ]

    def column_arrays():
        return own_x[0][0], [(box[0], parts) for box, parts in pieces]

    far, edge = kv(MINE, w_mine, None, column_arrays()[1], own_mine[0])
    rows_mine, halo_mine = [own_mine, *line.reached(far)], to("seq", edge, 2)
    one_twin = arrive(one_twin)
    q_twin = arrive(q_twin)
    w_twin = [own_kv[1], one_twin, two_twin, three_twin]
    own, far, edge, queries = kv(TWIN, w_twin, *column_arrays(), None, (q_mine[0], q_twin[0]))
    rows_twin, halo_twin = line.reached(own, far), to("seq", edge, 2)
    line.drop(*w_mine, *w_twin, q_mine, q_twin, *own_x, *(box for box, _ in pieces))
    limits = own_limit + [arrive(far_limit)]
    rows = [b[0] for b in (*rows_mine, *rows_twin)]
    parts = line.reached(*attend_pair(at, [b[0] for b in limits], queries, rows))
    line.drop(*rows_mine, *rows_twin)

    def finish(h, halo):
        (halo,) = line.after(halo)
        query, *rest = [b[0] for b in parts]
        keep, send = attend_halo(at, h, [b[0] for b in limits], query, halo, *rest)
        return line.reached(keep)[0], to("seq", send, 1)

    keep_mine, back_mine = finish(0, halo_mine)
    keep_twin, back_twin = finish(1, halo_twin)
    parts = [(MINE, keep_mine[0]), (TWIN, keep_twin[0]), (CROSS, back_mine), (CROSS_TWIN, back_twin)]
    return assemble(at, parts)


def solution(mesh):
    placed = (
        P(("groups", "seq"), None),
        P("groups", None),
        P("seq", None, ("fsdp", "head")),
        P(None, ("fsdp", "head")),
        P(),
        P(("groups", "seq"), None),
    )
    return jax.shard_map(
        per_device,
        mesh=mesh,
        in_specs=placed,
        out_specs=P(("groups", "seq"), ("fsdp", "head")),
        check_vma=False,
    )
```

```python
import math

import jax
import jax.numpy as jnp
from jax import lax
from jax.experimental import pallas as pl
from jax.experimental.pallas import tpu as pltpu
from jax.sharding import PartitionSpec as P

EPS = 1e-06
VMEM = 28 << 20
WHOLE = 60 << 20
FIRST = 8
HIDDEN = -1e30
SPACE = pl.CostEstimate(flops=1 << 36, bytes_accessed=1 << 10, transcendentals=0)
COST = pl.CostEstimate(flops=1 << 20, bytes_accessed=1 << 10, transcendentals=0)


def with_halo(shard, sides, width):
    for axis, dim in sides:
        devices, length = (lax.axis_size(axis), shard.shape[dim])
        up = [(i, (i + 1) % devices) for i in range(devices - 1)]
        down = [(j, i) for i, j in up]
        last = lax.slice_in_dim(shard, length - width, length, axis=dim)
        first = lax.slice_in_dim(shard, 0, width, axis=dim)
        before = lax.ppermute(last, axis, up)
        after = lax.ppermute(first, axis, down)
        shard = jnp.concatenate([before, shard, after], axis=dim)
    return shard


def normed_heads(tensor, gain_row, head_dim):
    shaped = tensor.reshape(tensor.shape[0], tensor.shape[1] // head_dim, head_dim)
    scaled = (
        shaped * lax.rsqrt(jnp.mean(shaped * shaped, axis=-1, keepdims=True) + EPS) * gain_row
    )
    return scaled.astype(jnp.bfloat16)


def visible_tiles(block_lists):
    position = lax.axis_index("seq")
    tile_dev = block_lists.shape[0]
    candidates = (position - 1) * tile_dev + jnp.arange(3 * tile_dev, dtype=jnp.int32)
    matches = (block_lists[:, :, None] == candidates[None, None, :]) & (
        block_lists[:, :, None] >= 0
    )
    return jnp.any(matches, axis=1)


def general(frames, modulation, w_qkv, b_qkv, qk_gain, block_lists):
    inputs = frames.astype(jnp.float32)
    average = jnp.mean(inputs, axis=-1, keepdims=True)
    centred = inputs - average
    variance = jnp.mean(centred * centred, axis=-1, keepdims=True)
    normed = centred * lax.rsqrt(variance + EPS) * (1.0 + modulation[0]) + modulation[1]
    normed = normed.astype(jnp.bfloat16)
    tokens = normed.shape[0]
    width_cols = w_qkv.shape[2]
    head_dim = qk_gain.shape[1]
    heads = width_cols // head_dim
    projected = jnp.einsum(
        "td,djc->tjc",
        normed,
        lax.all_gather(w_qkv, "seq", axis=0, tiled=True),
        preferred_element_type=jnp.float32,
    )
    projected = projected + b_qkv
    queries = normed_heads(projected[:, 0], qk_gain[0], head_dim)
    key_rows = normed_heads(projected[:, 1], qk_gain[1], head_dim)
    values = projected[:, 2].astype(jnp.bfloat16).reshape(tokens, heads, head_dim)
    stacked = jnp.stack([key_rows, values], axis=0)
    neighbourhood = with_halo(stacked, (("seq", 1),), tokens)
    tile_len = tokens // block_lists.shape[0]
    allowed_keys = jnp.repeat(
        jnp.repeat(visible_tiles(block_lists), tile_len, axis=0), tile_len, axis=1
    )
    factor = 1.0 / math.sqrt(head_dim)
    scores = (
        jnp.einsum("qhd,khd->hqk", queries, neighbourhood[0], preferred_element_type=jnp.float32)
        * factor
    )
    weights = jnp.where(allowed_keys[None, :, :], jnp.exp(scores), 0.0)
    totals = jnp.sum(weights, axis=-1)
    mixture = jnp.einsum(
        "hqk,khd->qhd",
        weights.astype(jnp.bfloat16),
        neighbourhood[1],
        preferred_element_type=jnp.float32,
    )
    result = (mixture / jnp.transpose(totals)[:, :, None]).astype(jnp.bfloat16)
    return result.reshape(tokens, width_cols)


class Line:
    def __init__(self):
        self.held = []

    def reached(self, *values):
        boxes = [[v] for v in values]
        self.held += boxes
        return boxes

    def after(self, *values):
        out = lax.optimization_barrier((*values, *(box[0] for box in self.held)))
        for box, value in zip(self.held, out[len(values) :]):
            box[0] = value
        return out[: len(values)]

    def drop(self, *boxes):
        self.held = [box for box in self.held if all(box is not b for b in boxes)]
        return [box[0] for box in boxes]


def norm_kernel(x_ref, mod_ref, o_ref):
    x = x_ref[...].astype(jnp.float32)
    centred = x - jnp.mean(x, axis=-1, keepdims=True)
    variance = jnp.mean(centred * centred, axis=-1, keepdims=True)
    scaled = centred * lax.rsqrt(variance + EPS) * (1.0 + mod_ref[0:1, :]) + mod_ref[1:2, :]
    o_ref[...] = scaled.astype(jnp.bfloat16)


def normalize(frames, modulation, rows):
    tokens, width = frames.shape
    return pl.pallas_call(
        norm_kernel,
        grid=(tokens // rows,),
        in_specs=[
            pl.BlockSpec((rows, width), lambda i: (i, 0)),
            pl.BlockSpec((2, width), lambda i: (0, 0)),
        ],
        out_specs=pl.BlockSpec((rows, width), lambda i: (i, 0)),
        out_shape=jax.ShapeDtypeStruct((tokens, width), jnp.bfloat16),
        cost_estimate=COST,
        name="normalize",
    )(frames, modulation)


def cut_heads(at, w, groups, cost=None):
    rows = w.shape[1]
    head_dim = 128
    shapes = [(len(indices), rows, head_dim * len(js)) for indices, js in groups]

    def kernel(at_ref, w_ref, *out_refs):
        for (indices, js), ref in zip(groups, out_refs):
            for n, index in enumerate(indices):
                cols = pl.ds(pl.multiple_of(at_ref[index] * head_dim, 128), head_dim)
                for i, j in enumerate(js):
                    ref[n, :, i * head_dim : (i + 1) * head_dim] = w_ref[j, :, cols]

    return pl.pallas_call(
        kernel,
        in_specs=[pl.BlockSpec(memory_space=pltpu.SMEM), pl.BlockSpec()],
        out_specs=[pl.BlockSpec()] * len(groups),
        out_shape=[jax.ShapeDtypeStruct(shape, jnp.bfloat16) for shape in shapes],
        compiler_params=pltpu.CompilerParams(vmem_limit_bytes=VMEM),
        cost_estimate=cost or COST,
        name="cut_heads",
    )(at, w)


def see(at, lists, tile_dev):
    def kernel(at_ref, lists_ref, o_ref):
        lists = lists_ref[...]
        z = at_ref[0]
        lane = lax.broadcasted_iota(jnp.int32, o_ref.shape, 1)
        out = jnp.full(o_ref.shape, HIDDEN, jnp.float32)
        for c, column in enumerate((z, z ^ 1, jnp.where(z < 2, 2, 1))):
            for t in range(tile_dev):
                hit = (lists == column * tile_dev + t).astype(jnp.float32)
                listed = jnp.max(hit, axis=1, keepdims=True) > 0.0
                out = jnp.where((lane == c * tile_dev + t) & listed, 0.0, out)
        o_ref[...] = out

    return pl.pallas_call(
        kernel,
        in_specs=[pl.BlockSpec(memory_space=pltpu.SMEM), pl.BlockSpec()],
        out_specs=pl.BlockSpec(),
        out_shape=jax.ShapeDtypeStruct((lists.shape[0], 128), jnp.float32),
        cost_estimate=COST,
        name="see",
    )(at, lists)


def load_columns(at, own, pieces, x_ref, sems, step):
    count, tokens, _ = x_ref.shape
    copies = ([], [])
    for r in range(0, tokens if own is not None else 0, step):
        copies[0].append((own.at[pl.ds(r, step)], x_ref.at[0, pl.ds(r, step)]))
    for ref, parts in pieces:
        for i, start, first, size in parts:
            row = pl.multiple_of((at[1] ^ i) * (tokens // 4) + start, 16)
            copies[1].append((ref.at[pl.ds(first, size)], x_ref.at[count - 1, pl.ds(row, size)]))
    made, n = ([], []), 0
    for group, out in zip(copies, made):
        for source, target in group:
            out.append(pltpu.make_async_copy(source, target, sems.at[n]))
            n += 1
    return made


def start(copies):
    for copy in copies:
        copy.start()


def start_next(waves, n):
    if n + 1 < len(waves):
        start(waves[n + 1])
    for copy in waves[n]:
        copy.wait()


def normed(value, gain):
    mean = jnp.mean(value * value, axis=-1, keepdims=True)
    return value * lax.rsqrt(mean + EPS) * gain


def keys_values(at, head, own, pieces, weights, bias, gain, own_rows=None):
    _, rows, cols = weights[0].shape
    head_dim = gain.shape[1]
    arrays, parts = zip(*pieces) if pieces else ((), ())
    width = (arrays or (own,))[0].shape[1]
    tokens = own.shape[0] if own is not None else own_rows.shape[0]
    columns = [0] * (own is not None) + [1] * bool(pieces)
    step = 256
    moves = tokens // step + sum(map(len, parts))
    sources = [own] * (own is not None) + list(arrays)
    known = [] if own_rows is None else [own_rows]
    n_out = (own is not None) + 2 * bool(pieces)

    def kernel(at_ref, *refs):
        x_sources, weight_refs = refs[: len(sources)], refs[len(sources) : len(sources) + 4]
        b_ref, g_ref, *rest = refs[len(sources) + 4 :]
        own_in, out_refs = rest[: len(known)], rest[len(known) : len(known) + n_out]
        x_ref, w_ref, x_sems, w_sems = rest[-4:]
        z = at_ref[0]
        is_mid = (z == 1) | (z == 2)
        lanes = pl.ds(pl.multiple_of(at_ref[head] * head_dim, 128), head_dim)
        loads = [
            pltpu.make_async_copy(ref, w_ref.at[pl.ds(s, 1)], w_sems.at[s])
            for s, ref in enumerate(weight_refs)
        ]
        piece_refs = x_sources[len(sources) - len(arrays) :]
        own_moves, far_moves = load_columns(
            at_ref, x_sources[0] if 0 in columns else None, list(zip(piece_refs, parts)), x_ref, x_sems, step
        )
        waves = [[move] for move in own_moves] + [far_moves] * bool(far_moves)
        start([*loads, *waves[0]])
        for copy in loads:
            copy.wait()
        for column in columns:
            if column:
                start_next(waves, len(own_moves))
            out_ref = out_refs[0 if column == 0 else -2]
            for r in range(tokens // step):
                if not column:
                    start_next(waves, r)
                here = slice(r * step, (r + 1) * step)
                total = None
                for s in range(4):
                    first = pl.multiple_of((z ^ s) * rows, 128)
                    product = jnp.dot(
                        x_ref[columns.index(column), here, pl.ds(first, rows)], w_ref[s],
                        preferred_element_type=jnp.float32,
                    )
                    total = product if total is None else total + product
                key = normed(total[:, :head_dim] + b_ref[1:2, lanes], g_ref[1:2, :])
                out_ref[here, :head_dim] = key.astype(jnp.bfloat16)
                value = total[:, head_dim:] + b_ref[2:3, lanes]
                out_ref[here, head_dim:] = value.astype(jnp.bfloat16)
                if column:
                    own_ref = own_in[0] if known else out_refs[0]
                    out_refs[-1][here, :] = jnp.where(is_mid, own_ref[here, :], out_ref[here, :])

    hbm = pl.BlockSpec(memory_space=pltpu.HBM)
    out = jax.ShapeDtypeStruct((tokens, cols), jnp.bfloat16)
    return pl.pallas_call(
        kernel,
        in_specs=[pl.BlockSpec(memory_space=pltpu.SMEM)]
        + [hbm] * (len(sources) + 4)
        + [pl.BlockSpec()] * (2 + len(known)),
        out_specs=[pl.BlockSpec()] * n_out,
        out_shape=[out] * n_out,
        scratch_shapes=[
            pltpu.VMEM((len(columns), tokens, width), jnp.bfloat16),
            pltpu.VMEM((4, rows, cols), jnp.bfloat16),
            pltpu.SemaphoreType.DMA((moves,)),
            pltpu.SemaphoreType.DMA((4,)),
        ],
        compiler_params=pltpu.CompilerParams(vmem_limit_bytes=WHOLE),
        cost_estimate=SPACE,
        name="keys_values",
    )(at, *sources, *weights, bias, gain, *known)


def take_rows(at, frames, sizes):
    width = frames.shape[1]
    quarter = sum(sizes)

    def kernel(at_ref, x_ref, *out_refs):
        first = 0
        for ref in out_refs:
            ref[...] = x_ref[first : first + ref.shape[0], :]
            first += ref.shape[0]

    return pl.pallas_call(
        kernel,
        grid_spec=pltpu.PrefetchScalarGridSpec(
            num_scalar_prefetch=1,
            grid=(1,),
            in_specs=[pl.BlockSpec((quarter, width), lambda i, at: (at[1], 0))],
            out_specs=[pl.BlockSpec((size, width), lambda i, at: (0, 0)) for size in sizes],
        ),
        out_shape=[jax.ShapeDtypeStruct((size, width), jnp.bfloat16) for size in sizes],
        cost_estimate=COST,
        name="take_rows",
    )(at, frames)


def attend_pair(at, limits, own, pieces, weights, bias, gain, rows):
    tokens, width = own.shape
    head_dim = gain.shape[1]
    tiles = limits[0].shape[0]
    tile = tokens // tiles
    arrays, parts = zip(*pieces)
    step = 256
    moves = tokens // step + sum(map(len, parts))
    shard = weights[0].shape[1]

    def kernel(at_ref, limit0_ref, limit1_ref, own_ref, *refs):
        piece_refs, weight_refs = refs[: len(arrays)], refs[len(arrays) : len(arrays) + 2]
        row_refs = refs[len(arrays) + 2 : len(arrays) + 6]
        (b_ref, g_ref, edge_ref, done_ref, mixed_ref, total_ref,
         x_ref, w_ref, q_ref, kv_ref, x_sems, w_sems) = refs[len(arrays) + 6 :]
        z = at_ref[0]
        is_mid = (z == 1) | (z == 2)
        loads = [
            pltpu.make_async_copy(ref, w_ref.at[h], w_sems.at[h])
            for h, ref in enumerate(weight_refs)
        ]
        own_moves, far_moves = load_columns(at_ref, own_ref, list(zip(piece_refs, parts)), x_ref, x_sems, step)
        late = [
            pltpu.make_async_copy(ref, kv_ref.at[n // 2, n % 2], w_sems.at[2 + n])
            for n, ref in enumerate(row_refs)
        ]
        waves = [[move] for move in own_moves] + [far_moves, late]
        start([*loads, *waves[0]])
        for copy in loads:
            copy.wait()
        for column in range(2):
            if column:
                start_next(waves, len(own_moves))
            for r in range(tokens // step):
                if not column:
                    start_next(waves, r)
                here = slice(r * step, (r + 1) * step)
                total = None
                for s in range(4):
                    product = jnp.dot(
                        x_ref[column, here, s * shard : (s + 1) * shard],
                        jnp.concatenate([w_ref[0, s], w_ref[1, s]], axis=1),
                        preferred_element_type=jnp.float32,
                    )
                    total = product if total is None else total + product
                for h in range(2):
                    lanes = pl.ds(pl.multiple_of(at_ref[2 + h] * head_dim, 128), head_dim)
                    value = total[:, h * head_dim : (h + 1) * head_dim] + b_ref[0:1, lanes]
                    q_ref[h, column, here, :] = normed(value, g_ref[0:1, :]).astype(jnp.bfloat16)
        for copy in late:
            copy.wait()

        @pl.loop(0, 2)
        def _(h):
            for column in range(2):
                is_edge = is_mid if column == 0 else jnp.logical_not(is_mid)
                for i in range(tiles):
                    here = slice(i * tile, (i + 1) * tile)
                    query = q_ref[h, column, here, :]
                    total = jnp.zeros((tile, 128), jnp.float32)
                    mixed = jnp.zeros((tile, head_dim), jnp.float32)
                    for other in range(2):
                        for t in range(tiles):
                            limit = (limit0_ref, limit1_ref)[column][i, (other ^ column) * tiles + t]
                            total, mixed = column_step(
                                query, kv_ref.at[h, other, t * tile : (t + 1) * tile], tile,
                                head_dim, [limit], total, mixed,
                            )

                    @pl.when(is_edge)
                    def _():
                        edge_ref[h, here, :] = query
                        mixed_ref[h, here, :] = mixed
                        total_ref[h, here, :] = total

                    @pl.when(jnp.logical_not(is_edge))
                    def _():
                        rows = mixed / jnp.sum(total, axis=-1, keepdims=True)
                        done_ref[h, here, :] = rows.astype(jnp.bfloat16)

    smem = pl.BlockSpec(memory_space=pltpu.SMEM)
    hbm = pl.BlockSpec(memory_space=pltpu.HBM)
    shape = (2, tokens, head_dim)
    return pl.pallas_call(
        kernel,
        in_specs=[smem] * 3 + [hbm] * (1 + len(arrays) + 6) + [pl.BlockSpec()] * 2,
        out_specs=[pl.BlockSpec()] * 4,
        out_shape=[
            jax.ShapeDtypeStruct(shape, jnp.bfloat16),
            jax.ShapeDtypeStruct(shape, jnp.bfloat16),
            jax.ShapeDtypeStruct(shape, jnp.float32),
            jax.ShapeDtypeStruct((2, tokens, 128), jnp.float32),
        ],
        scratch_shapes=[
            pltpu.VMEM((2, tokens, width), jnp.bfloat16),
            pltpu.VMEM((2, 4, shard, head_dim), jnp.bfloat16),
            pltpu.VMEM((2, 2, tokens, head_dim), jnp.bfloat16),
            pltpu.VMEM((2, 2, tokens, 2 * head_dim), jnp.bfloat16),
            pltpu.SemaphoreType.DMA((moves,)),
            pltpu.SemaphoreType.DMA((6,)),
        ],
        compiler_params=pltpu.CompilerParams(vmem_limit_bytes=WHOLE),
        cost_estimate=COST,
        name="attend_pair",
    )(at, *limits, own, *arrays, *weights, *rows, bias, gain)


def attend_halo(at, h, limits, query, halo, done, mixed, total):
    _, tokens, head_dim = query.shape
    tiles = limits[0].shape[0]
    tile = tokens // tiles

    def kernel(at_ref, limit0_ref, limit1_ref, q_ref, halo_ref, done_ref, mixed_ref, total_ref, keep_ref, send_ref):
        is_mid = (at_ref[0] == 1) | (at_ref[0] == 2)
        for i in range(tiles):
            here = slice(i * tile, (i + 1) * tile)
            sums, rows = total_ref[0, here, :], mixed_ref[0, here, :]
            seen = [
                jnp.where(is_mid, limit0_ref[i, 2 * tiles + t], limit1_ref[i, 2 * tiles + t])
                for t in range(tiles)
            ]
            sums, rows = column_step(q_ref[0, here, :], halo_ref, tile, head_dim, seen, sums, rows)
            edge = (rows / jnp.sum(sums, axis=-1, keepdims=True)).astype(jnp.bfloat16)
            outer = done_ref[0, here, :]
            keep_ref[here, :] = jnp.where(is_mid, edge, outer)
            send_ref[here, :] = jnp.where(is_mid, outer, edge)

    smem = pl.BlockSpec(memory_space=pltpu.SMEM)
    one = pl.BlockSpec((1, tokens, head_dim), lambda i: (h, 0, 0))
    fixed = lambda shape: pl.BlockSpec(shape, lambda i: (0,) * len(shape))
    out = jax.ShapeDtypeStruct((tokens, head_dim), jnp.bfloat16)
    return pl.pallas_call(
        kernel,
        grid=(1,),
        in_specs=[smem] * 3 + [one, fixed(halo.shape), one, one, one],
        out_specs=[fixed(out.shape)] * 2,
        out_shape=[out] * 2,
        compiler_params=pltpu.CompilerParams(vmem_limit_bytes=WHOLE),
        cost_estimate=SPACE,
        name="attend_halo",
    )(at, *limits, query, halo, done, mixed, total)


def assemble(at, parts):
    indices, arrays = zip(*parts)
    tokens, head_dim = arrays[0].shape
    rows = tokens // 3

    def kernel(at_ref, *refs):
        for index, ref in zip(indices, refs):
            lanes = pl.ds(pl.multiple_of(at_ref[index] * head_dim, 128), head_dim)
            refs[-1][:, lanes] = ref[...]

    return pl.pallas_call(
        kernel,
        grid=(tokens // rows,),
        in_specs=[pl.BlockSpec(memory_space=pltpu.SMEM)]
        + [pl.BlockSpec((rows, head_dim), lambda i: (i, 0))] * len(arrays),
        out_specs=pl.BlockSpec((rows, head_dim * len(arrays)), lambda i: (i, 0)),
        out_shape=jax.ShapeDtypeStruct((tokens, head_dim * len(arrays)), jnp.bfloat16),
        compiler_params=pltpu.CompilerParams(vmem_limit_bytes=WHOLE),
        cost_estimate=COST,
        name="assemble",
    )(at, *arrays)


def column_step(query, rows_ref, tile, head_dim, limits, total, mixed):
    scale = math.log2(math.e) / math.sqrt(head_dim)
    scores = lax.dot_general(
        query, rows_ref[:, :head_dim], (((1,), (1,)), ((), ())), preferred_element_type=jnp.float32
    )
    rounded = []
    for t, limit in enumerate(limits):
        weights = jnp.exp2(scores[:, t * tile : (t + 1) * tile] * scale + limit)
        for c in range(tile // 128):
            total = total + weights[:, c * 128 : (c + 1) * 128]
        rounded.append(weights.astype(jnp.bfloat16))
    mixed = mixed + jnp.dot(
        jnp.concatenate(rounded, axis=1), rows_ref[:, head_dim:], preferred_element_type=jnp.float32
    )
    return total, mixed


def per_device(frames, modulation, w_qkv, b_qkv, qk_gain, block_lists):
    sizes = tuple(lax.axis_size(a) for a in ("groups", "seq", "fsdp", "head"))
    head_dim = qk_gain.shape[1]
    width_cols = w_qkv.shape[2]
    tokens = frames.shape[0]
    if sizes != (2, 4, 2, 2) or width_cols != 4 * head_dim:
        return general(frames, modulation, w_qkv, b_qkv, qk_gain, block_lists)

    y, z, x, core = (lax.axis_index(a).astype(jnp.int32) for a in ("groups", "seq", "fsdp", "head"))
    rows = w_qkv.shape[0]
    quarter = tokens // 4
    tile_dev = block_lists.shape[0]

    def to(axis, value, bit):
        return lax.ppermute(value, axis, [(i, i ^ bit) for i in range(lax.axis_size(axis))])

    side = z % 2
    mine, twin = 2 * side + y, 2 * side + 1 - y
    across = 2 * (1 - side)
    at = jnp.stack([z, 2 * x + core, mine, twin, across + y, across + 1 - y, y, 2 + y])
    MINE, TWIN, CROSS, CROSS_TWIN = 2, 3, 4, 5
    is_mid = (z == 1) | (z == 2)
    w = jnp.transpose(w_qkv, (1, 0, 2))
    line = Line()

    def arrive(value):
        box = line.reached(value)[0]
        (box[0],) = line.after(box[0])
        return box

    cutting = (0, quarter * FIRST // 12, quarter)
    raws = take_rows(at, frames, [hi - lo for lo, hi in zip(cutting, cutting[1:])])
    raws_other = [to("seq", raw, 1) for raw in raws]
    (w, *_) = lax.optimization_barrier((w, *raws))
    same, cross, q_sent = line.reached(
        *cut_heads(at, w, [((MINE,), (1, 2)), ((CROSS,), (1, 2)), ((6, 7, 6, 7), (0,))])
    )
    got = [to("seq", same[0], 2), to("seq", cross[0], 3), to("seq", cross[0], 1)]
    own_limit = line.reached(see(at, block_lists, tile_dev))
    frames, modulation = line.after(frames, modulation)
    own_x = line.reached(normalize(frames, modulation, 128))
    line.drop(cross)

    def take(i):
        (raw,) = line.after(raws_other[i])
        near = line.reached(normalize(raw, modulation, raw.shape[0]))[0]
        return near, to("fsdp", near[0], 1)

    def spread(near, far):
        far = arrive(far)
        (near[0],) = line.after(near[0])
        return far, to("head", near[0], 1), to("head", far[0], 1)

    def swap(which):
        kept = arrive(got[which])
        return kept, to("groups", kept[0], 1)

    near0, far0 = take(0)
    two_mine, two_twin = swap(0)
    near1, far1 = take(1)
    (q_sent[0],) = line.after(q_sent[0])
    q_got = lax.all_to_all(q_sent[0], "seq", split_axis=0, concat_axis=0, tiled=True)
    line.drop(q_sent)
    three_mine, three_twin = swap(1)
    one_mine, one_twin = swap(2)
    (w,) = line.after(w)
    own_kv = [same, line.reached(*cut_heads(at, w, [((TWIN,), (1, 2))], SPACE))[0]]
    far0, core0, core2 = spread(near0, far0)
    two_twin = arrive(two_twin)
    three_twin = arrive(three_twin)
    far1, core1, core3 = spread(near1, far1)
    w_mine = [own_kv[0], one_mine, two_mine, three_mine]

    def kv(head, boxes, own, pieces, own_rows=None):
        (boxes[0][0],) = line.after(boxes[0][0])
        weights = [box[0] for box in boxes]
        return keys_values(at, head, own, pieces, weights, b_qkv, qk_gain, own_rows)

    own_mine = line.reached(*kv(MINE, w_mine, own_x[0][0], None))[0]
    (own_limit[0][0],) = line.after(own_limit[0][0])
    far_limit = to("seq", own_limit[0][0], 1)
    core0, core1, core2, core3 = (arrive(core) for core in (core0, core1, core2, core3))
    n0, n1 = cutting[1], quarter - cutting[1]
    pieces = [
        (near0, [(0, 0, 0, n0)]),
        (far0, [(2, 0, 0, n0)]),
        (core0, [(1, 0, 0, n0)]),
        (core2, [(3, 0, 0, n0)]),
        (near1, [(0, n0, 0, n1)]),
        (far1, [(2, n0, 0, n1)]),
        (core1, [(1, n0, 0, n1)]),
        (core3, [(3, n0, 0, n1)]),
    ]

    def column_arrays():
        return own_x[0][0], [(box[0], parts) for box, parts in pieces]

    far, edge = kv(MINE, w_mine, None, column_arrays()[1], own_mine[0])
    rows_mine, halo_mine = [own_mine, *line.reached(far)], to("seq", edge, 2)
    q_mine = arrive(q_got)
    q_twin = to("groups", q_mine[0], 1)
    one_twin = arrive(one_twin)
    w_twin = [own_kv[1], one_twin, two_twin, three_twin]
    own, far, edge = kv(TWIN, w_twin, *column_arrays())
    rows_twin, halo_twin = line.reached(own, far), to("seq", edge, 2)
    line.drop(*w_mine, *w_twin)
    limits = own_limit + [arrive(far_limit)]
    q_twin = arrive(q_twin)
    parts = line.reached(
        *attend_pair(
            at, [b[0] for b in limits], *column_arrays(), [q_mine[0], q_twin[0]], b_qkv, qk_gain,
            [b[0] for b in (*rows_mine, *rows_twin)],
        )
    )
    line.drop(q_mine, q_twin, *own_x, *(box for box, _ in pieces), *rows_mine, *rows_twin)

    def finish(h, halo):
        (halo,) = line.after(halo)
        query, *rest = [b[0] for b in parts]
        keep, send = attend_halo(at, h, [b[0] for b in limits], query, halo, *rest)
        return line.reached(keep)[0], to("seq", send, 1)

    keep_mine, back_mine = finish(0, halo_mine)
    keep_twin, back_twin = finish(1, halo_twin)
    parts = [(MINE, keep_mine[0]), (TWIN, keep_twin[0]), (CROSS, back_mine), (CROSS_TWIN, back_twin)]
    return assemble(at, parts)


def solution(mesh):
    placed = (
        P(("groups", "seq"), None),
        P("groups", None),
        P("seq", None, ("fsdp", "head")),
        P(None, ("fsdp", "head")),
        P(),
        P(("groups", "seq"), None),
    )
    return jax.shard_map(
        per_device,
        mesh=mesh,
        in_specs=placed,
        out_specs=P(("groups", "seq"), ("fsdp", "head")),
        check_vma=False,
    )
```

```python
import math

import jax
import jax.numpy as jnp
from jax import lax
from jax.experimental import pallas as pl
from jax.experimental.pallas import tpu as pltpu
from jax.sharding import PartitionSpec as P

EPS = 1e-06
VMEM = 28 << 20
WHOLE = 60 << 20
FIRST = 8
HIDDEN = -1e30
SPACE = pl.CostEstimate(flops=1 << 36, bytes_accessed=1 << 10, transcendentals=0)
COST = pl.CostEstimate(flops=1 << 20, bytes_accessed=1 << 10, transcendentals=0)


def with_halo(shard, sides, width):
    for axis, dim in sides:
        devices, length = (lax.axis_size(axis), shard.shape[dim])
        up = [(i, (i + 1) % devices) for i in range(devices - 1)]
        down = [(j, i) for i, j in up]
        last = lax.slice_in_dim(shard, length - width, length, axis=dim)
        first = lax.slice_in_dim(shard, 0, width, axis=dim)
        before = lax.ppermute(last, axis, up)
        after = lax.ppermute(first, axis, down)
        shard = jnp.concatenate([before, shard, after], axis=dim)
    return shard


def normed_heads(tensor, gain_row, head_dim):
    shaped = tensor.reshape(tensor.shape[0], tensor.shape[1] // head_dim, head_dim)
    scaled = (
        shaped * lax.rsqrt(jnp.mean(shaped * shaped, axis=-1, keepdims=True) + EPS) * gain_row
    )
    return scaled.astype(jnp.bfloat16)


def visible_tiles(block_lists):
    position = lax.axis_index("seq")
    tile_dev = block_lists.shape[0]
    candidates = (position - 1) * tile_dev + jnp.arange(3 * tile_dev, dtype=jnp.int32)
    matches = (block_lists[:, :, None] == candidates[None, None, :]) & (
        block_lists[:, :, None] >= 0
    )
    return jnp.any(matches, axis=1)


def general(frames, modulation, w_qkv, b_qkv, qk_gain, block_lists):
    inputs = frames.astype(jnp.float32)
    average = jnp.mean(inputs, axis=-1, keepdims=True)
    centred = inputs - average
    variance = jnp.mean(centred * centred, axis=-1, keepdims=True)
    normed = centred * lax.rsqrt(variance + EPS) * (1.0 + modulation[0]) + modulation[1]
    normed = normed.astype(jnp.bfloat16)
    tokens = normed.shape[0]
    width_cols = w_qkv.shape[2]
    head_dim = qk_gain.shape[1]
    heads = width_cols // head_dim
    projected = jnp.einsum(
        "td,djc->tjc",
        normed,
        lax.all_gather(w_qkv, "seq", axis=0, tiled=True),
        preferred_element_type=jnp.float32,
    )
    projected = projected + b_qkv
    queries = normed_heads(projected[:, 0], qk_gain[0], head_dim)
    key_rows = normed_heads(projected[:, 1], qk_gain[1], head_dim)
    values = projected[:, 2].astype(jnp.bfloat16).reshape(tokens, heads, head_dim)
    stacked = jnp.stack([key_rows, values], axis=0)
    neighbourhood = with_halo(stacked, (("seq", 1),), tokens)
    tile_len = tokens // block_lists.shape[0]
    allowed_keys = jnp.repeat(
        jnp.repeat(visible_tiles(block_lists), tile_len, axis=0), tile_len, axis=1
    )
    factor = 1.0 / math.sqrt(head_dim)
    scores = (
        jnp.einsum("qhd,khd->hqk", queries, neighbourhood[0], preferred_element_type=jnp.float32)
        * factor
    )
    weights = jnp.where(allowed_keys[None, :, :], jnp.exp(scores), 0.0)
    totals = jnp.sum(weights, axis=-1)
    mixture = jnp.einsum(
        "hqk,khd->qhd",
        weights.astype(jnp.bfloat16),
        neighbourhood[1],
        preferred_element_type=jnp.float32,
    )
    result = (mixture / jnp.transpose(totals)[:, :, None]).astype(jnp.bfloat16)
    return result.reshape(tokens, width_cols)


class Line:
    def __init__(self):
        self.held = []

    def reached(self, *values):
        boxes = [[v] for v in values]
        self.held += boxes
        return boxes

    def after(self, *values):
        out = lax.optimization_barrier((*values, *(box[0] for box in self.held)))
        for box, value in zip(self.held, out[len(values) :]):
            box[0] = value
        return out[: len(values)]

    def drop(self, *boxes):
        self.held = [box for box in self.held if all(box is not b for b in boxes)]
        return [box[0] for box in boxes]


def norm_kernel(x_ref, mod_ref, o_ref):
    x = x_ref[...].astype(jnp.float32)
    centred = x - jnp.mean(x, axis=-1, keepdims=True)
    variance = jnp.mean(centred * centred, axis=-1, keepdims=True)
    scaled = centred * lax.rsqrt(variance + EPS) * (1.0 + mod_ref[0:1, :]) + mod_ref[1:2, :]
    o_ref[...] = scaled.astype(jnp.bfloat16)


def normalize(frames, modulation, rows):
    tokens, width = frames.shape
    return pl.pallas_call(
        norm_kernel,
        grid=(tokens // rows,),
        in_specs=[
            pl.BlockSpec((rows, width), lambda i: (i, 0)),
            pl.BlockSpec((2, width), lambda i: (0, 0)),
        ],
        out_specs=pl.BlockSpec((rows, width), lambda i: (i, 0)),
        out_shape=jax.ShapeDtypeStruct((tokens, width), jnp.bfloat16),
        cost_estimate=COST,
        name="normalize",
    )(frames, modulation)


def cut_heads(at, w, groups, cost=None):
    rows = w.shape[1]
    head_dim = 128
    shapes = [(len(indices), rows, head_dim * len(js)) for indices, js in groups]

    def kernel(at_ref, w_ref, *out_refs):
        for (indices, js), ref in zip(groups, out_refs):
            for n, index in enumerate(indices):
                cols = pl.ds(pl.multiple_of(at_ref[index] * head_dim, 128), head_dim)
                for i, j in enumerate(js):
                    ref[n, :, i * head_dim : (i + 1) * head_dim] = w_ref[j, :, cols]

    return pl.pallas_call(
        kernel,
        in_specs=[pl.BlockSpec(memory_space=pltpu.SMEM), pl.BlockSpec()],
        out_specs=[pl.BlockSpec()] * len(groups),
        out_shape=[jax.ShapeDtypeStruct(shape, jnp.bfloat16) for shape in shapes],
        compiler_params=pltpu.CompilerParams(vmem_limit_bytes=VMEM),
        cost_estimate=cost or COST,
        name="cut_heads",
    )(at, w)


def see(at, lists, tile_dev):
    def kernel(at_ref, lists_ref, o_ref):
        lists = lists_ref[...]
        z = at_ref[0]
        lane = lax.broadcasted_iota(jnp.int32, o_ref.shape, 1)
        out = jnp.full(o_ref.shape, HIDDEN, jnp.float32)
        for c, column in enumerate((z, z ^ 1, jnp.where(z < 2, 2, 1))):
            for t in range(tile_dev):
                hit = (lists == column * tile_dev + t).astype(jnp.float32)
                listed = jnp.max(hit, axis=1, keepdims=True) > 0.0
                out = jnp.where((lane == c * tile_dev + t) & listed, 0.0, out)
        o_ref[...] = out

    return pl.pallas_call(
        kernel,
        in_specs=[pl.BlockSpec(memory_space=pltpu.SMEM), pl.BlockSpec()],
        out_specs=pl.BlockSpec(),
        out_shape=jax.ShapeDtypeStruct((lists.shape[0], 128), jnp.float32),
        cost_estimate=COST,
        name="see",
    )(at, lists)


def load_columns(at, own, pieces, x_ref, sems, step):
    count, tokens, _ = x_ref.shape
    copies = ([], [])
    for r in range(0, tokens if own is not None else 0, step):
        copies[0].append((own.at[pl.ds(r, step)], x_ref.at[0, pl.ds(r, step)]))
    for ref, parts in pieces:
        for i, start, first, size in parts:
            row = pl.multiple_of((at[1] ^ i) * (tokens // 4) + start, 16)
            copies[1].append((ref.at[pl.ds(first, size)], x_ref.at[count - 1, pl.ds(row, size)]))
    made, n = ([], []), 0
    for group, out in zip(copies, made):
        for source, target in group:
            out.append(pltpu.make_async_copy(source, target, sems.at[n]))
            n += 1
    return made


def start(copies):
    for copy in copies:
        copy.start()


def start_next(waves, n):
    if n + 1 < len(waves):
        start(waves[n + 1])
    for copy in waves[n]:
        copy.wait()


def normed(value, gain):
    mean = jnp.mean(value * value, axis=-1, keepdims=True)
    return value * lax.rsqrt(mean + EPS) * gain


def keys_values(at, head, own, pieces, weights, bias, gain, own_rows=None):
    _, rows, cols = weights[0].shape
    head_dim = gain.shape[1]
    arrays, parts = zip(*pieces) if pieces else ((), ())
    width = (arrays or (own,))[0].shape[1]
    tokens = own.shape[0] if own is not None else own_rows.shape[0]
    columns = [0] * (own is not None) + [1] * bool(pieces)
    step = 256
    moves = tokens // step + sum(map(len, parts))
    sources = [own] * (own is not None) + list(arrays)
    known = [] if own_rows is None else [own_rows]
    n_out = (own is not None) + 2 * bool(pieces)

    def kernel(at_ref, *refs):
        x_sources, weight_refs = refs[: len(sources)], refs[len(sources) : len(sources) + 4]
        b_ref, g_ref, *rest = refs[len(sources) + 4 :]
        own_in, out_refs = rest[: len(known)], rest[len(known) : len(known) + n_out]
        x_ref, w_ref, x_sems, w_sems = rest[-4:]
        z = at_ref[0]
        is_mid = (z == 1) | (z == 2)
        lanes = pl.ds(pl.multiple_of(at_ref[head] * head_dim, 128), head_dim)
        loads = [
            pltpu.make_async_copy(ref, w_ref.at[pl.ds(s, 1)], w_sems.at[s])
            for s, ref in enumerate(weight_refs)
        ]
        piece_refs = x_sources[len(sources) - len(arrays) :]
        own_moves, far_moves = load_columns(
            at_ref, x_sources[0] if 0 in columns else None, list(zip(piece_refs, parts)), x_ref, x_sems, step
        )
        waves = [[move] for move in own_moves] + [far_moves] * bool(far_moves)
        start([*loads, *waves[0]])
        for copy in loads:
            copy.wait()
        for column in columns:
            if column:
                start_next(waves, len(own_moves))
            out_ref = out_refs[0 if column == 0 else -2]
            for r in range(tokens // step):
                if not column:
                    start_next(waves, r)
                here = slice(r * step, (r + 1) * step)
                total = None
                for s in range(4):
                    first = pl.multiple_of((z ^ s) * rows, 128)
                    product = jnp.dot(
                        x_ref[columns.index(column), here, pl.ds(first, rows)], w_ref[s],
                        preferred_element_type=jnp.float32,
                    )
                    total = product if total is None else total + product
                key = normed(total[:, :head_dim] + b_ref[1:2, lanes], g_ref[1:2, :])
                out_ref[here, :head_dim] = key.astype(jnp.bfloat16)
                value = total[:, head_dim:] + b_ref[2:3, lanes]
                out_ref[here, head_dim:] = value.astype(jnp.bfloat16)
                if column:
                    own_ref = own_in[0] if known else out_refs[0]
                    out_refs[-1][here, :] = jnp.where(is_mid, own_ref[here, :], out_ref[here, :])

    hbm = pl.BlockSpec(memory_space=pltpu.HBM)
    out = jax.ShapeDtypeStruct((tokens, cols), jnp.bfloat16)
    return pl.pallas_call(
        kernel,
        in_specs=[pl.BlockSpec(memory_space=pltpu.SMEM)]
        + [hbm] * (len(sources) + 4)
        + [pl.BlockSpec()] * (2 + len(known)),
        out_specs=[pl.BlockSpec()] * n_out,
        out_shape=[out] * n_out,
        scratch_shapes=[
            pltpu.VMEM((len(columns), tokens, width), jnp.bfloat16),
            pltpu.VMEM((4, rows, cols), jnp.bfloat16),
            pltpu.SemaphoreType.DMA((moves,)),
            pltpu.SemaphoreType.DMA((4,)),
        ],
        compiler_params=pltpu.CompilerParams(vmem_limit_bytes=WHOLE),
        cost_estimate=SPACE,
        name="keys_values",
    )(at, *sources, *weights, bias, gain, *known)


def take_rows(at, frames, sizes):
    width = frames.shape[1]
    quarter = sum(sizes)

    def kernel(at_ref, x_ref, *out_refs):
        first = 0
        for ref in out_refs:
            ref[...] = x_ref[first : first + ref.shape[0], :]
            first += ref.shape[0]

    return pl.pallas_call(
        kernel,
        grid_spec=pltpu.PrefetchScalarGridSpec(
            num_scalar_prefetch=1,
            grid=(1,),
            in_specs=[pl.BlockSpec((quarter, width), lambda i, at: (at[1], 0))],
            out_specs=[pl.BlockSpec((size, width), lambda i, at: (0, 0)) for size in sizes],
        ),
        out_shape=[jax.ShapeDtypeStruct((size, width), jnp.bfloat16) for size in sizes],
        cost_estimate=COST,
        name="take_rows",
    )(at, frames)


def attend_pair(at, limits, own, pieces, weights, bias, gain, rows):
    tokens, width = own.shape
    head_dim = gain.shape[1]
    tiles = limits[0].shape[0]
    tile = tokens // tiles
    arrays, parts = zip(*pieces)
    step = 256
    moves = tokens // step + sum(map(len, parts))
    shard = weights[0].shape[1]

    def kernel(at_ref, limit0_ref, limit1_ref, own_ref, *refs):
        piece_refs, weight_refs = refs[: len(arrays)], refs[len(arrays) : len(arrays) + 2]
        row_refs = refs[len(arrays) + 2 : len(arrays) + 6]
        (b_ref, g_ref, edge_ref, done_ref, mixed_ref, total_ref,
         x_ref, w_ref, q_ref, kv_ref, x_sems, w_sems) = refs[len(arrays) + 6 :]
        z = at_ref[0]
        is_mid = (z == 1) | (z == 2)
        loads = [
            pltpu.make_async_copy(ref, w_ref.at[h], w_sems.at[h])
            for h, ref in enumerate(weight_refs)
        ]
        own_moves, far_moves = load_columns(at_ref, own_ref, list(zip(piece_refs, parts)), x_ref, x_sems, step)
        late = [
            pltpu.make_async_copy(ref, kv_ref.at[n // 2, n % 2], w_sems.at[2 + n])
            for n, ref in enumerate(row_refs)
        ]
        waves = [[move] for move in own_moves] + [far_moves, late]
        start([*loads, *waves[0]])
        for copy in loads:
            copy.wait()
        for column in range(2):
            if column:
                start_next(waves, len(own_moves))
            for r in range(tokens // step):
                if not column:
                    start_next(waves, r)
                here = slice(r * step, (r + 1) * step)
                total = None
                for s in range(4):
                    product = jnp.dot(
                        x_ref[column, here, s * shard : (s + 1) * shard],
                        jnp.concatenate([w_ref[0, s], w_ref[1, s]], axis=1),
                        preferred_element_type=jnp.float32,
                    )
                    total = product if total is None else total + product
                for h in range(2):
                    lanes = pl.ds(pl.multiple_of(at_ref[2 + h] * head_dim, 128), head_dim)
                    value = total[:, h * head_dim : (h + 1) * head_dim] + b_ref[0:1, lanes]
                    q_ref[h, column, here, :] = normed(value, g_ref[0:1, :]).astype(jnp.bfloat16)
        for copy in late:
            copy.wait()

        @pl.loop(0, 2)
        def _(h):
            for column in range(2):
                is_edge = is_mid if column == 0 else jnp.logical_not(is_mid)
                for i in range(tiles):
                    here = slice(i * tile, (i + 1) * tile)
                    query = q_ref[h, column, here, :]
                    total = jnp.zeros((tile, 128), jnp.float32)
                    mixed = jnp.zeros((tile, head_dim), jnp.float32)
                    for other in range(2):
                        for t in range(tiles):
                            limit = (limit0_ref, limit1_ref)[column][i, (other ^ column) * tiles + t]
                            total, mixed = column_step(
                                query, kv_ref.at[h, other, t * tile : (t + 1) * tile], tile,
                                head_dim, [limit], total, mixed,
                            )

                    @pl.when(is_edge)
                    def _():
                        edge_ref[h, here, :] = query
                        mixed_ref[h, here, :] = mixed
                        total_ref[h, here, :] = total

                    @pl.when(jnp.logical_not(is_edge))
                    def _():
                        rows = mixed / jnp.sum(total, axis=-1, keepdims=True)
                        done_ref[h, here, :] = rows.astype(jnp.bfloat16)

    smem = pl.BlockSpec(memory_space=pltpu.SMEM)
    hbm = pl.BlockSpec(memory_space=pltpu.HBM)
    shape = (2, tokens, head_dim)
    return pl.pallas_call(
        kernel,
        in_specs=[smem] * 3 + [hbm] * (1 + len(arrays) + 6) + [pl.BlockSpec()] * 2,
        out_specs=[pl.BlockSpec()] * 4,
        out_shape=[
            jax.ShapeDtypeStruct(shape, jnp.bfloat16),
            jax.ShapeDtypeStruct(shape, jnp.bfloat16),
            jax.ShapeDtypeStruct(shape, jnp.float32),
            jax.ShapeDtypeStruct((2, tokens, 128), jnp.float32),
        ],
        scratch_shapes=[
            pltpu.VMEM((2, tokens, width), jnp.bfloat16),
            pltpu.VMEM((2, 4, shard, head_dim), jnp.bfloat16),
            pltpu.VMEM((2, 2, tokens, head_dim), jnp.bfloat16),
            pltpu.VMEM((2, 2, tokens, 2 * head_dim), jnp.bfloat16),
            pltpu.SemaphoreType.DMA((moves,)),
            pltpu.SemaphoreType.DMA((6,)),
        ],
        compiler_params=pltpu.CompilerParams(vmem_limit_bytes=WHOLE),
        cost_estimate=COST,
        name="attend_pair",
    )(at, *limits, own, *arrays, *weights, *rows, bias, gain)


def attend_halo(at, h, limits, query, halo, done, mixed, total):
    _, tokens, head_dim = query.shape
    tiles = limits[0].shape[0]
    tile = tokens // tiles

    def kernel(at_ref, limit0_ref, limit1_ref, q_ref, halo_ref, done_ref, mixed_ref, total_ref, keep_ref, send_ref):
        is_mid = (at_ref[0] == 1) | (at_ref[0] == 2)
        for i in range(tiles):
            here = slice(i * tile, (i + 1) * tile)
            sums, rows = total_ref[0, here, :], mixed_ref[0, here, :]
            seen = [
                jnp.where(is_mid, limit0_ref[i, 2 * tiles + t], limit1_ref[i, 2 * tiles + t])
                for t in range(tiles)
            ]
            sums, rows = column_step(q_ref[0, here, :], halo_ref, tile, head_dim, seen, sums, rows)
            edge = (rows / jnp.sum(sums, axis=-1, keepdims=True)).astype(jnp.bfloat16)
            outer = done_ref[0, here, :]
            keep_ref[here, :] = jnp.where(is_mid, edge, outer)
            send_ref[here, :] = jnp.where(is_mid, outer, edge)

    smem = pl.BlockSpec(memory_space=pltpu.SMEM)
    one = pl.BlockSpec((1, tokens, head_dim), lambda i: (h, 0, 0))
    fixed = lambda shape: pl.BlockSpec(shape, lambda i: (0,) * len(shape))
    out = jax.ShapeDtypeStruct((tokens, head_dim), jnp.bfloat16)
    return pl.pallas_call(
        kernel,
        grid=(1,),
        in_specs=[smem] * 3 + [one, fixed(halo.shape), one, one, one],
        out_specs=[fixed(out.shape)] * 2,
        out_shape=[out] * 2,
        compiler_params=pltpu.CompilerParams(vmem_limit_bytes=WHOLE),
        cost_estimate=SPACE,
        name="attend_halo",
    )(at, *limits, query, halo, done, mixed, total)


def assemble(at, parts):
    indices, arrays = zip(*parts)
    tokens, head_dim = arrays[0].shape
    rows = tokens // 3

    def kernel(at_ref, *refs):
        for index, ref in zip(indices, refs):
            lanes = pl.ds(pl.multiple_of(at_ref[index] * head_dim, 128), head_dim)
            refs[-1][:, lanes] = ref[...]

    return pl.pallas_call(
        kernel,
        grid=(tokens // rows,),
        in_specs=[pl.BlockSpec(memory_space=pltpu.SMEM)]
        + [pl.BlockSpec((rows, head_dim), lambda i: (i, 0))] * len(arrays),
        out_specs=pl.BlockSpec((rows, head_dim * len(arrays)), lambda i: (i, 0)),
        out_shape=jax.ShapeDtypeStruct((tokens, head_dim * len(arrays)), jnp.bfloat16),
        compiler_params=pltpu.CompilerParams(vmem_limit_bytes=WHOLE),
        cost_estimate=COST,
        name="assemble",
    )(at, *arrays)


def column_step(query, rows_ref, tile, head_dim, limits, total, mixed):
    scale = math.log2(math.e) / math.sqrt(head_dim)
    scores = lax.dot_general(
        query, rows_ref[:, :head_dim], (((1,), (1,)), ((), ())), preferred_element_type=jnp.float32
    )
    rounded = []
    for t, limit in enumerate(limits):
        weights = jnp.exp2(scores[:, t * tile : (t + 1) * tile] * scale + limit)
        for c in range(tile // 128):
            total = total + weights[:, c * 128 : (c + 1) * 128]
        rounded.append(weights.astype(jnp.bfloat16))
    mixed = mixed + jnp.dot(
        jnp.concatenate(rounded, axis=1), rows_ref[:, head_dim:], preferred_element_type=jnp.float32
    )
    return total, mixed


def per_device(frames, modulation, w_qkv, b_qkv, qk_gain, block_lists):
    sizes = tuple(lax.axis_size(a) for a in ("groups", "seq", "fsdp", "head"))
    head_dim = qk_gain.shape[1]
    width_cols = w_qkv.shape[2]
    tokens = frames.shape[0]
    if sizes != (2, 4, 2, 2) or width_cols != 4 * head_dim:
        return general(frames, modulation, w_qkv, b_qkv, qk_gain, block_lists)

    y, z, x, core = (lax.axis_index(a).astype(jnp.int32) for a in ("groups", "seq", "fsdp", "head"))
    rows = w_qkv.shape[0]
    quarter = tokens // 4
    tile_dev = block_lists.shape[0]

    def to(axis, value, bit):
        return lax.ppermute(value, axis, [(i, i ^ bit) for i in range(lax.axis_size(axis))])

    side = z % 2
    mine, twin = 2 * side + y, 2 * side + 1 - y
    across = 2 * (1 - side)
    at = jnp.stack([z, 2 * x + core, mine, twin, across + y, across + 1 - y, y, 2 + y])
    MINE, TWIN, CROSS, CROSS_TWIN = 2, 3, 4, 5
    is_mid = (z == 1) | (z == 2)
    w = jnp.transpose(w_qkv, (1, 0, 2))
    line = Line()

    def arrive(value):
        box = line.reached(value)[0]
        (box[0],) = line.after(box[0])
        return box

    cutting = (0, quarter * FIRST // 12, quarter)
    raws = take_rows(at, frames, [hi - lo for lo, hi in zip(cutting, cutting[1:])])
    raws_other = [to("seq", raw, 1) for raw in raws]
    (w, *_) = lax.optimization_barrier((w, *raws))
    same, cross, q_sent = line.reached(
        *cut_heads(at, w, [((MINE,), (1, 2)), ((CROSS,), (1, 2)), ((6, 7, 6, 7), (0,))])
    )
    got = [to("seq", same[0], 2), to("seq", cross[0], 3), to("seq", cross[0], 1)]
    own_limit = line.reached(see(at, block_lists, tile_dev))
    frames, modulation = line.after(frames, modulation)
    own_x = line.reached(normalize(frames, modulation, 128))
    line.drop(cross)

    def take(i):
        (raw,) = line.after(raws_other[i])
        near = line.reached(normalize(raw, modulation, raw.shape[0]))[0]
        return near, to("fsdp", near[0], 1)

    def spread(near, far):
        far = arrive(far)
        (near[0],) = line.after(near[0])
        return far, to("head", near[0], 1), to("head", far[0], 1)

    def swap(which):
        kept = arrive(got[which])
        return kept, to("groups", kept[0], 1)

    near0, far0 = take(0)
    two_mine, two_twin = swap(0)
    one_mine, one_twin = swap(2)
    near1, far1 = take(1)
    (q_sent[0],) = line.after(q_sent[0])
    q_got = lax.all_to_all(q_sent[0], "seq", split_axis=0, concat_axis=0, tiled=True)
    line.drop(q_sent)
    three_mine, three_twin = swap(1)
    (w,) = line.after(w)
    own_kv = [same, line.reached(*cut_heads(at, w, [((TWIN,), (1, 2))], SPACE))[0]]
    far0, core0, core2 = spread(near0, far0)
    two_twin = arrive(two_twin)
    three_twin = arrive(three_twin)
    far1, core1, core3 = spread(near1, far1)
    w_mine = [own_kv[0], one_mine, two_mine, three_mine]

    def kv(head, boxes, own, pieces, own_rows=None):
        (boxes[0][0],) = line.after(boxes[0][0])
        weights = [box[0] for box in boxes]
        return keys_values(at, head, own, pieces, weights, b_qkv, qk_gain, own_rows)

    own_mine = line.reached(*kv(MINE, w_mine, own_x[0][0], None))[0]
    (own_limit[0][0],) = line.after(own_limit[0][0])
    far_limit = to("seq", own_limit[0][0], 1)
    core0, core1, core2, core3 = (arrive(core) for core in (core0, core1, core2, core3))
    n0, n1 = cutting[1], quarter - cutting[1]
    pieces = [
        (near0, [(0, 0, 0, n0)]),
        (far0, [(2, 0, 0, n0)]),
        (core0, [(1, 0, 0, n0)]),
        (core2, [(3, 0, 0, n0)]),
        (near1, [(0, n0, 0, n1)]),
        (far1, [(2, n0, 0, n1)]),
        (core1, [(1, n0, 0, n1)]),
        (core3, [(3, n0, 0, n1)]),
    ]

    def column_arrays():
        return own_x[0][0], [(box[0], parts) for box, parts in pieces]

    far, edge = kv(MINE, w_mine, None, column_arrays()[1], own_mine[0])
    rows_mine, halo_mine = [own_mine, *line.reached(far)], to("seq", edge, 2)
    q_mine = arrive(q_got)
    q_twin = to("groups", q_mine[0], 1)
    one_twin = arrive(one_twin)
    w_twin = [own_kv[1], one_twin, two_twin, three_twin]
    own, far, edge = kv(TWIN, w_twin, *column_arrays())
    rows_twin, halo_twin = line.reached(own, far), to("seq", edge, 2)
    line.drop(*w_mine, *w_twin)
    limits = own_limit + [arrive(far_limit)]
    q_twin = arrive(q_twin)
    parts = line.reached(
        *attend_pair(
            at, [b[0] for b in limits], *column_arrays(), [q_mine[0], q_twin[0]], b_qkv, qk_gain,
            [b[0] for b in (*rows_mine, *rows_twin)],
        )
    )
    line.drop(q_mine, q_twin, *own_x, *(box for box, _ in pieces), *rows_mine, *rows_twin)

    def finish(h, halo):
        (halo,) = line.after(halo)
        query, *rest = [b[0] for b in parts]
        keep, send = attend_halo(at, h, [b[0] for b in limits], query, halo, *rest)
        return line.reached(keep)[0], to("seq", send, 1)

    keep_mine, back_mine = finish(0, halo_mine)
    keep_twin, back_twin = finish(1, halo_twin)
    parts = [(MINE, keep_mine[0]), (TWIN, keep_twin[0]), (CROSS, back_mine), (CROSS_TWIN, back_twin)]
    return assemble(at, parts)


def solution(mesh):
    placed = (
        P(("groups", "seq"), None),
        P("groups", None),
        P("seq", None, ("fsdp", "head")),
        P(None, ("fsdp", "head")),
        P(),
        P(("groups", "seq"), None),
    )
    return jax.shard_map(
        per_device,
        mesh=mesh,
        in_specs=placed,
        out_specs=P(("groups", "seq"), ("fsdp", "head")),
        check_vma=False,
    )
```
